32 devices in a mesh: stream: 2 (over y), dp: 16 (over z, x, core).
Axes of the slice: x: 2, y: 2, z: 4, core: 2. Of those that a mesh axis runs over, the one named last changes fastest.
Arguments:
- tokens: bfloat16 [2, 16384, 768], P('stream', 'dp'), may hold values from -40 to 40, as said below
- first_gain: float32 [2, 768], P('stream'), may hold values from 0.25 to 1.75
- first_shift: float32 [2, 768], P('stream'), may hold values from -1.5 to 1.5
- query_weight: bfloat16 [2, 768, 768], P('stream'), may hold values from -0.21875 to 0.21875
- query_bias: float32 [2, 768], P('stream'), may hold values from -1.5 to 1.5
- key_weight: bfloat16 [2, 768, 768], P('stream'), may hold values from -0.21875 to 0.21875
- value_weight: bfloat16 [2, 768, 768], P('stream'), may hold values from -0.21875 to 0.21875
- value_bias: float32 [2, 768], P('stream'), may hold values from -0.5 to 0.5
- out_weight: bfloat16 [2, 768, 768], P('stream'), may hold values from -1.75 to 1.75
- out_bias: float32 [2, 768], P('stream'), may hold values from -1.5 to 1.5
- second_gain: float32 [2, 768], P('stream'), may hold values from 0.25 to 1.75
- second_shift: float32 [2, 768], P('stream'), may hold values from -1.5 to 1.5
- up_weight: bfloat16 [2, 768, 3072], P('stream'), may hold values from -0.21875 to 0.21875
- up_bias: float32 [2, 3072], P('stream'), may hold values from -1.5 to 1.5
- down_weight: bfloat16 [2, 3072, 768], P('stream'), may hold values from -0.109375 to 0.109375
- down_bias: float32 [2, 768], P('stream'), may hold values from -1.5 to 1.5
- box_table: float32 [2, 768], P('stream'), may hold values from -4 to 4
- segments: int32 [2, 32, 512], P(None, 'dp'), may hold values from 0 to 63, never falling along the last dimension, each value on 1 to 16 neighbouring positions
- validity: int32 [2, 32, 512], P(None, 'dp'), may hold values from 0 to 1, as said below
- seg_boxes: int32 [32, 64, 4], P('dp'), may hold values from 0 to 1023
- cotangent: bfloat16 [2, 16384, 768], P('stream', 'dp'), may hold values from -6 to 6
Outputs:
- layer_out: bfloat16 [2, 16384, 768], P('stream', 'dp')
- grad_tokens: float32 [2, 16384, 768], P('stream', 'dp')
- grad_first_gain: float32 [2, 768], P('stream', 'dp')
- grad_first_shift: float32 [2, 768], P('stream', 'dp')
- grad_query_weight: float32 [2, 768, 768], P('stream', 'dp')
- grad_query_bias: float32 [2, 768], P('stream', 'dp')
- grad_key_weight: float32 [2, 768, 768], P('stream', 'dp')
- grad_value_weight: float32 [2, 768, 768], P('stream', 'dp')
- grad_value_bias: float32 [2, 768], P('stream', 'dp')
- grad_out_weight: float32 [2, 768, 768], P('stream', 'dp')
- grad_out_bias: float32 [2, 768], P('stream', 'dp')
- grad_second_gain: float32 [2, 768], P('stream', 'dp')
- grad_second_shift: float32 [2, 768], P('stream', 'dp')
- grad_up_weight: float32 [2, 768, 3072], P('stream', 'dp')
- gradient_expand_bias: float32 [2, 3072], P('stream', 'dp')
- grad_down_weight: float32 [2, 3072, 768], P('stream', 'dp')
- grad_down_bias: float32 [2, 768], P('stream', 'dp')
- grad_box_table: float32 [2, 768], P('stream', 'dp')
- root_means: float32 [2, 3], P('stream')
The draws below stay inside these ranges and needn't reach their ends.
Inputs may be any that keep to these rules, and one draw needn't show every extreme that they name: `tokens`: activations of both streams. `validity`: in each page of each stream the valid tokens come first, 256 of them or more. `segments`: within a page of a stream the segment numbers never fall; a segment spans 1 to 16 tokens.
All inputs are finite; a program needn't handle non-finite values.
Results may differ from the reference program's by a relative error of at most 0.012.
The reference program's roundings to bfloat16 on the way count: a program that leaves them out, or rounds other values in their place, can miss the bound.
Values may be sent and summed in bfloat16 or wider, within the bound.
No kernel may reach another device: no remote copies, remote signals or barrier semaphores. Data moves between devices by JAX's collectives and lax.ppermute only.
A program may use at most 192 MiB of HBM per device.

```python
import math
import jax
import jax.numpy as jnp
import numpy as np
from jax import lax

D = 768
HEADS = 12
HEAD_DIM = 64
FF = 3072
PAGE_LEN = 512
SEGS = 64
BUCKETS = 32
PAGES = 32
TOKENS = 16384


def draw_tokens(key, part):
    page = jnp.arange(TOKENS, dtype=jnp.int32) // PAGE_LEN
    ramp = page.astype(jnp.float32) / max(PAGES - 1, 1)
    base = jax.random.normal(key, (2, TOKENS, D), jnp.float32)
    return (base * (1.0 + 5.0 * ramp)[None, :, None]).astype(jnp.bfloat16)


def draw_validity(key, part):
    lengths = jax.random.randint(key, (2, PAGES), PAGE_LEN // 2, PAGE_LEN + 1)
    places = jnp.arange(PAGE_LEN, dtype=jnp.int32)
    return (places[None, None, :] < lengths[:, :, None]).astype(jnp.int32)


def set_ends(entries, stream_key, smallest, largest):
    index_at = [jax.random.randint(jax.random.fold_in(stream_key, axis), (), 0, length) for axis, length in enumerate(entries.shape)]
    widest = entries.shape.index(max(entries.shape))
    neighbour = index_at[:widest] + [(index_at[widest] + 1) % entries.shape[widest]] + index_at[widest + 1:]
    return entries.at[tuple(index_at)].set(smallest).at[tuple(neighbour)].set(largest)


def block_levels(own_key, shape, pieces, least, largest):
    loudness = 1.0
    for dim, parts in pieces:
        steps = jax.random.uniform(jax.random.fold_in(jax.random.fold_in(own_key, 6), dim), (parts,), jnp.float32, least / len(pieces), largest / len(pieces))
        loudness = loudness * jnp.repeat(jnp.exp(steps), shape[dim] // parts).reshape((-1,) + (1,) * (len(shape) - 1 - dim))
    return loudness


def split_up(count, total, reach, skew):
    weights = [(1 << 20) // math.isqrt(rank ** skew) + 1 for rank in range(2, count + 1)]
    rest, given = total - reach - (count - 1), [1] * (count - 1)
    while rest > 0:
        free = [i for i in range(count - 1) if given[i] < reach]
        mass, left = sum([weights[i] for i in free]), rest
        for i in free:
            extra = min(reach - given[i], max(1, left * weights[i] // mass), rest)
            given[i] = given[i] + extra
            rest = rest - extra
    return np.array([reach] + given)


def ragged(own_key, number_of, total, bound, slope):
    if number_of == 2:
        one = jax.random.randint(own_key, (), max(1, total - bound), min(bound, total - 1) + 1)
        return jnp.stack([one, total - one])
    tallies = jnp.asarray(split_up(number_of, total, bound, slope), jnp.int32)
    twos = (number_of - 1) // 2
    donor, sink = tallies[1:1 + 2 * twos:2], tallies[2:2 + 2 * twos:2]
    slack = jnp.minimum(donor - 1, bound - sink)
    shifted = jax.random.randint(jax.random.fold_in(own_key, 1), (twos,), 0, 1 << 20) % (slack + 1)
    tallies = tallies.at[1:1 + 2 * twos:2].set(donor - shifted).at[2:2 + 2 * twos:2].set(sink + shifted)
    return tallies[jax.random.permutation(jax.random.fold_in(own_key, 2), number_of)]


def centred(own_key, extent, scale, reach, pieces=(), kind=jnp.bfloat16):
    values = scale * jax.random.normal(own_key, extent, jnp.float32)
    if pieces:
        values = values * block_levels(own_key, extent, pieces, -0.22, 0.18)
    return jnp.clip(values, -reach, reach).astype(kind)


def setup_inputs(seed: int = 0) -> dict:
    splits = jax.random.split(jax.random.key(seed), 22)
    tokens = draw_tokens(jax.random.fold_in(splits[21], 71), 0)
    first_gain = jnp.clip(1.0 + 0.15 * jax.random.normal(splits[1], (2, D), jnp.float32), 0.25, 1.75)
    first_shift = centred(splits[2], (2, D), 0.3, 1.5, ((0, 2),), jnp.float32)
    query_weight = centred(splits[3], (2, D, D), D ** -0.5, 0.21875, ((0, 2),))
    query_bias = centred(splits[4], (2, D), 0.3, 1.5, ((0, 2),), jnp.float32)
    key_weight = centred(splits[5], (2, D, D), D ** -0.5, 0.21875, ((0, 2),))
    value_weight = centred(splits[6], (2, D, D), D ** -0.5, 0.21875, ((0, 2),))
    value_bias = centred(splits[7], (2, D), 0.1, 0.5, ((0, 2),), jnp.float32)
    out_weight = centred(splits[8], (2, D, D), (D // 64) ** -0.5, 1.75, ((0, 2),))
    out_bias = centred(splits[9], (2, D), 0.3, 1.5, ((0, 2),), jnp.float32)
    second_gain = jnp.clip(1.0 + 0.15 * jax.random.normal(splits[10], (2, D), jnp.float32), 0.25, 1.75)
    second_shift = centred(splits[11], (2, D), 0.3, 1.5, ((0, 2),), jnp.float32)
    up_weight = centred(splits[12], (2, D, FF), D ** -0.5, 0.21875, ((0, 2),))
    up_bias = centred(splits[13], (2, FF), 0.3, 1.5, ((0, 2),), jnp.float32)
    down_weight = centred(splits[14], (2, FF, D), FF ** -0.5, 0.109375, ((0, 2),))
    down_bias = centred(splits[15], (2, D), 0.3, 1.5, ((0, 2),), jnp.float32)
    box_table = centred(splits[16], (2, 2 * HEADS * BUCKETS), 1.0, 4.0, ((0, 2),), jnp.float32)
    segments = jax.vmap(lambda own: jnp.searchsorted(jnp.cumsum(ragged(own, SEGS, PAGE_LEN, 2 * PAGE_LEN // SEGS, 1)), jnp.arange(PAGE_LEN), side="right"))(jax.random.split(splits[17], 2 * PAGES)).reshape((2, PAGES, PAGE_LEN)).astype(jnp.int32)
    validity = draw_validity(jax.random.fold_in(splits[21], 71), 0)
    seg_boxes = set_ends(jax.random.randint(splits[19], (PAGES, SEGS, 4), 0, 1024), jax.random.fold_in(splits[19], 1), 0, 1023).astype(jnp.int32)
    cotangent = centred(splits[20], (2, TOKENS, D), 1.0, 6.0, ((0, 2), (1, 16)))
    return dict(tokens=tokens, first_gain=first_gain, first_shift=first_shift, query_weight=query_weight, query_bias=query_bias, key_weight=key_weight, value_weight=value_weight, value_bias=value_bias, out_weight=out_weight, out_bias=out_bias, second_gain=second_gain, second_shift=second_shift, up_weight=up_weight, up_bias=up_bias, down_weight=down_weight, down_bias=down_bias, box_table=box_table, segments=segments, validity=validity, seg_boxes=seg_boxes, cotangent=cotangent)


score_scale = 0.125
norm_eps = 1e-05
mask_fill = -1000000000.0
box_step = 32
group_pairs = 4
precise_variant = lax.Precision.HIGHEST

@jax.custom_vjp
def low(v):
    return lax.optimization_barrier(v.astype(jnp.bfloat16)).astype(jnp.float32)

@jax.custom_vjp
def low_back(v):
    return v

def low_keep(v):
    return (low(v), None)

def low_pass(kept, grad):
    return (grad,)

def back_keep(v):
    return (v, None)

def back_low(kept, grad):
    return (low(grad),)
low.defvjp(low_keep, low_pass)
low_back.defvjp(back_keep, back_low)

def norm_rows(value_rows, gain, shift):
    centre = value_rows - lax.optimization_barrier(jnp.mean(value_rows, -1, keepdims=True))
    spread = lax.optimization_barrier(jnp.mean(centre * centre, -1, keepdims=True))
    return centre * lax.rsqrt(spread + norm_eps) * gain + shift

def project(value_rows, weight_matrix):
    return jnp.einsum('vzy,vyc->vzc', value_rows, weight_matrix, precision=precise_variant)

def bucket_of(seg_boxes):
    half = BUCKETS // 2
    centre_x = (seg_boxes[..., 0] + seg_boxes[..., 2]) // 2
    centre_y = (seg_boxes[..., 1] + seg_boxes[..., 3]) // 2
    step_x = jnp.clip((centre_x[:, None, :] - centre_x[:, :, None]) // box_step, -half, half - 1) + half
    step_y = jnp.clip((centre_y[:, None, :] - centre_y[:, :, None]) // box_step, -half, half - 1) + half
    return (step_x.astype(jnp.int32), step_y.astype(jnp.int32))

def pick_bias(table, left, right):
    return table[:, left][:, :, right]

def attend(block):
    query, keys, value_rows, seg_bias, own_seg, far_seg, far_keep = block
    bias = jax.vmap(pick_bias)(seg_bias, own_seg, far_seg)
    scores = jnp.einsum('gqhe,gkhe->ghqk', query, keys, precision=precise_variant) * score_scale + bias
    scores = low_back(jnp.where(far_keep[:, None, None, :] > 0, scores, mask_fill))
    peak_score = lax.optimization_barrier(jnp.max(scores, -1, keepdims=True))
    raised = jnp.exp(scores - peak_score)
    probs = low(raised / lax.optimization_barrier(jnp.sum(raised, -1, keepdims=True)))
    return jnp.einsum('ghqk,gkhe->gqhe', probs, value_rows, precision=precise_variant)

def layer(inputs, params, segments, validity, step_x, step_y):
    first_gain, first_shift, query_weight, query_bias, key_weight, value_weight, value_bias, out_weight, out_bias, second_gain, second_shift, up_weight, up_bias, down_weight, down_bias, box_table = params
    streams, count, width = inputs.shape
    blocks = 2 * PAGES // group_pairs
    normed = low(norm_rows(inputs, first_gain[:, None], first_shift[:, None]))
    query = low_back(low(project(normed, query_weight) + query_bias[:, None]))
    keys = low_back(low(project(normed, key_weight)))
    value_rows = low_back(low(project(normed, value_weight) + value_bias[:, None]))
    tables = box_table.reshape(2, 2, HEADS, BUCKETS)
    seg_bias = low(jnp.take(tables[:, 0], step_x, axis=2) + jnp.take(tables[:, 1], step_y, axis=2))
    seg_bias = jnp.transpose(seg_bias, (0, 2, 1, 3, 4)).reshape(blocks, group_pairs, HEADS, SEGS, SEGS)

    def heads_of(array):
        return array.reshape(blocks, group_pairs, PAGE_LEN, HEADS, HEAD_DIM)
    own_seg = segments.reshape(blocks, group_pairs, PAGE_LEN)
    far_seg = segments[::-1].reshape(blocks, group_pairs, PAGE_LEN)
    far_keep = validity[::-1].reshape(blocks, group_pairs, PAGE_LEN)
    mixed = lax.map(jax.checkpoint(attend), (heads_of(query), heads_of(keys[::-1]), heads_of(value_rows[::-1]), seg_bias, own_seg, far_seg, far_keep))
    mixed = low_back(low(mixed.reshape(streams, count, width)))
    branch = low_back(project(mixed, out_weight) + out_bias[:, None])
    middle = inputs + branch
    normed_two = low(norm_rows(middle, second_gain[:, None], second_shift[:, None]))
    hidden = low_back(project(normed_two, up_weight) + up_bias[:, None])
    activated = low(jax.nn.gelu(hidden, approximate=False))
    feed = low_back(project(activated, down_weight) + down_bias[:, None])
    return (middle + feed, (branch, feed))

def reference(tokens, first_gain, first_shift, query_weight, query_bias, key_weight, value_weight, value_bias, out_weight, out_bias, second_gain, second_shift, up_weight, up_bias, down_weight, down_bias, box_table, segments, validity, seg_boxes, cotangent):
    params = tuple((item.astype(jnp.float32) for item in (first_gain, first_shift, query_weight, query_bias, key_weight, value_weight, value_bias, out_weight, out_bias, second_gain, second_shift, up_weight, up_bias, down_weight, down_bias, box_table)))
    step_x, step_y = bucket_of(seg_boxes)

    def forward(inputs, weights):
        return layer(inputs, weights, segments, validity, step_x, step_y)
    output, pull, extras = jax.vjp(forward, tokens.astype(jnp.float32), params, has_aux=True)
    branch, feed = extras
    grad_tokens, grads = pull(cotangent.astype(jnp.float32))
    keep = validity.reshape(2, -1, 1).astype(jnp.float32)
    width = tokens.shape[2]
    counted = lax.optimization_barrier(jnp.sum(keep, (1, 2))) * width
    squares = jnp.stack([lax.optimization_barrier(jnp.sum(output * output * keep, (1, 2))), lax.optimization_barrier(jnp.sum(branch * branch * keep, (1, 2))), lax.optimization_barrier(jnp.sum(feed * feed * keep, (1, 2)))], 1)
    root_means = jnp.sqrt(squares / counted[:, None] + 1e-06)
    return (output.astype(jnp.bfloat16), grad_tokens) + tuple(grads) + (root_means,)
```

```python
import functools

import jax
import jax.numpy as jnp
from jax import lax
from jax.experimental import pallas as pl
from jax.experimental.pallas import tpu as pltpu
from jax.sharding import PartitionSpec as P

HEADS = 12
BUCKETS = 32

score_scale = 0.125
norm_eps = 1e-05
mask_fill = -1000000000.0
box_step = 32
precise_variant = lax.Precision.HIGHEST
f32 = jnp.float32
bf16 = jnp.bfloat16
VMEM_BYTES = 60 * 1024 * 1024


def nn(a, b):
    return lax.dot_general(a, b, (((1,), (0,)), ((), ())), preferred_element_type=f32)


def nt(a, b):
    return lax.dot_general(a, b, (((1,), (1,)), ((), ())), preferred_element_type=f32)


def tn(a, b):
    return lax.dot_general(a, b, (((0,), (0,)), ((), ())), preferred_element_type=f32)


def normal_rows(rows):
    centre = rows - jnp.mean(rows, -1, keepdims=True)
    spread = jnp.mean(centre * centre, -1, keepdims=True)
    scale = lax.rsqrt(spread + norm_eps)
    return centre * scale, scale


def params(**kw):
    return pltpu.CompilerParams(vmem_limit_bytes=VMEM_BYTES, **kw)


def cost(flops, moved, trans=0):
    return pl.CostEstimate(flops=int(flops), bytes_accessed=int(moved), transcendentals=int(trans))


def full(shape):
    zeros = (0,) * len(shape)
    return pl.BlockSpec(shape, lambda *_: zeros)


def query_kernel(x_ref, gain_ref, shift_ref, w_ref, b_ref, n_ref, q_ref):
    norm, _ = normal_rows(x_ref[...].astype(f32))
    low = (norm * gain_ref[...] + shift_ref[...]).astype(bf16)
    n_ref[...] = low
    query = (nn(low, w_ref[...]) + b_ref[...]).astype(bf16)
    q_ref[...] = (query.astype(f32) * score_scale).astype(bf16)


def query_call(x, gain, shift, weight, bias):
    length, width = x.shape
    tile = 256
    rows = pl.BlockSpec((tile, width), lambda i: (i, 0))
    return pl.pallas_call(
        query_kernel,
        grid=(length // tile,),
        in_specs=[rows, full((1, width)), full((1, width)), full(weight.shape), full((1, width))],
        out_specs=[rows, rows],
        out_shape=[jax.ShapeDtypeStruct(x.shape, bf16)] * 2,
        compiler_params=params(),
        cost_estimate=cost(2 * length * width * width, 6 * length * width + 2 * width * width),
        name="query",
    )(x, gain, shift, weight, bias)


def pair_kernel(x_ref, gain_ref, shift_ref, wk_ref, wv_ref, b_ref, n_ref, k_ref, v_ref):
    norm, _ = normal_rows(x_ref[...].astype(f32))
    low = (norm * gain_ref[...] + shift_ref[...]).astype(bf16)
    n_ref[...] = low
    k_ref[...] = nn(low, wk_ref[...]).astype(bf16)
    v_ref[...] = (nn(low, wv_ref[...]) + b_ref[...]).astype(bf16)


def pair_call(x, gain, shift, key_weight, value_weight, bias):
    length, width = x.shape
    tile = 256
    rows = pl.BlockSpec((tile, width), lambda i: (i, 0))
    return pl.pallas_call(
        pair_kernel,
        grid=(length // tile,),
        in_specs=[
            rows,
            full((1, width)),
            full((1, width)),
            full(key_weight.shape),
            full(value_weight.shape),
            full((1, width)),
        ],
        out_specs=[rows, rows, rows],
        out_shape=[jax.ShapeDtypeStruct(x.shape, bf16)] * 3,
        compiler_params=params(),
        cost_estimate=cost(4 * length * width * width, 8 * length * width + 4 * width * width),
        name="pair",
    )(x, gain, shift, key_weight, value_weight, bias)


def head_lanes(value, head, head_dim):
    lane = lax.broadcasted_iota(jnp.int32, value.shape, 1)
    mine = (lane >= head * head_dim) & (lane < (head + 1) * head_dim)
    return jnp.where(mine, value, jnp.zeros_like(value))


def attend_kernel(q_ref, k_ref, v_ref, bias_ref, hq_ref, hk_ref, o_ref, lse_ref):
    q, v = q_ref[...], v_ref[...]
    left = jnp.concatenate([k_ref[...], hk_ref[0]], 1)
    v_turned = v.astype(f32).T.astype(bf16)
    parts = []
    for head in range(2):
        picked = nn(hq_ref[0], bias_ref[0, head]).astype(bf16)
        right = jnp.concatenate([head_lanes(q, head, 64), picked], 1)
        scores = nt(left, right)
        peak = jnp.max(scores, 0, keepdims=True)
        raised = jnp.exp(scores - peak)
        total = jnp.sum(raised, 0, keepdims=True)
        probs = (raised * (1.0 / total)).astype(bf16)
        parts.append(nn(v_turned[head * 64 : (head + 1) * 64], probs))
        lse_ref[0, 0, head : head + 1, :] = peak + jnp.log(total)
    o_ref[...] = jnp.concatenate(parts, 0).T.astype(bf16)


def attend_specs(page_len):
    rows = pl.BlockSpec((page_len, 128), lambda p, h: (p, h))
    bias = pl.BlockSpec((1, 2, 64, 128), lambda p, h: (p, h, 0, 0))
    hot = pl.BlockSpec((1, page_len, 128), lambda p, h: (p, 0, 0))
    lse = pl.BlockSpec((1, 1, 2, page_len), lambda p, h: (p, h, 0, 0))
    return rows, bias, hot, lse


def attend_call(q, k, v, bias, hot_q, hot_k):
    length, width = q.shape
    pages, page_len = hot_q.shape[0], hot_q.shape[1]
    rows, bias_spec, hot, lse = attend_specs(page_len)
    hot64 = pl.BlockSpec((1, page_len, 64), lambda p, h: (p, 0, 0))
    return pl.pallas_call(
        attend_kernel,
        grid=(pages, width // 128),
        in_specs=[rows, rows, rows, bias_spec, hot64, hot],
        out_specs=[rows, lse],
        out_shape=[
            jax.ShapeDtypeStruct((length, width), bf16),
            jax.ShapeDtypeStruct((pages, width // 128, 2, page_len), f32),
        ],
        compiler_params=params(),
        cost_estimate=cost(
            8 * length * page_len * width, 8 * length * width, length * page_len * HEADS
        ),
        name="attend",
    )(q, k, v, bias, hot_q, hot_k)


def attend_back_kernel(
    q_ref,
    k_ref,
    v_ref,
    bias_ref,
    hq_ref,
    hk_ref,
    hkt_ref,
    lse_ref,
    o_ref,
    do_ref,
    dq_ref,
    dk_ref,
    dv_ref,
    gb_ref,
):
    q, k, v, do = q_ref[...], k_ref[...], v_ref[...], do_ref[...]
    hot_q = hq_ref[0]
    left = jnp.concatenate([k, hk_ref[0]], 1)
    k_turned = k.astype(f32).T.astype(bf16)
    overlap = do.astype(f32) * o_ref[...].astype(f32)
    row = lax.broadcasted_iota(jnp.int32, (8, 128), 0)
    lane = lax.broadcasted_iota(jnp.int32, (8, 128), 1)
    chooser = (row == lane // 64).astype(f32)
    delta = lax.dot_general(
        chooser,
        overlap,
        (((1,), (1,)), ((), ())),
        preferred_element_type=f32,
        precision=precise_variant,
    )
    parts, dk, dv = [], 0.0, 0.0
    for head in range(2):
        q_head, do_head = head_lanes(q, head, 64), head_lanes(do, head, 64)
        picked = nn(hot_q, bias_ref[0, head]).astype(bf16)
        right = jnp.concatenate([q_head, picked], 1)
        probs = jnp.exp(nt(left, right) - lse_ref[0, 0, head : head + 1, :])
        slope = nt(v, do_head)
        turn = (probs * (slope - delta[head : head + 1, :])).astype(bf16)
        dv = dv + nn(probs.astype(bf16), do_head)
        dk = dk + nn(turn, q_head)
        both = nn(jnp.concatenate([k_turned[head * 64 : (head + 1) * 64], hkt_ref[0]], 0), turn)
        parts.append(both[:64])
        sums = both[64:]
        high = sums.astype(bf16)
        rest = (sums - high.astype(f32)).astype(bf16)
        gb_ref[0, head] = nn(high, hot_q) + nn(rest, hot_q)
    dq_ref[...] = (jnp.concatenate(parts, 0) * score_scale).T.astype(bf16)
    dk_ref[...] = dk.astype(bf16)
    dv_ref[...] = dv.astype(bf16)


def attend_back_call(q, k, v, bias, hot_q, hot_k, hot_kt, lse_in, o, do):
    length, width = q.shape
    pages, page_len = hot_q.shape[0], hot_q.shape[1]
    rows, bias_spec, hot, lse = attend_specs(page_len)
    hot64 = pl.BlockSpec((1, page_len, 64), lambda p, h: (p, 0, 0))
    turned = pl.BlockSpec((1, 64, page_len), lambda p, h: (p, 0, 0))
    grad_bias = pl.BlockSpec((1, 2, 64, 64), lambda p, h: (p, h, 0, 0))
    wide = jax.ShapeDtypeStruct((length, width), bf16)
    return pl.pallas_call(
        attend_back_kernel,
        grid=(pages, width // 128),
        in_specs=[rows, rows, rows, bias_spec, hot64, hot, turned, lse, rows, rows],
        out_specs=[rows, rows, rows, grad_bias],
        out_shape=[wide, wide, wide, jax.ShapeDtypeStruct((pages, HEADS, 64, 64), f32)],
        compiler_params=params(),
        cost_estimate=cost(
            20 * length * page_len * width, 16 * length * width, length * page_len * HEADS
        ),
        name="attend_back",
    )(q, k, v, bias, hot_q, hot_k, hot_kt, lse_in, o, do)


def put_rows(scratch, keep, send, at, me, relative):
    if not relative:
        keep[pl.ds(at, scratch.shape[0]), :] = scratch[...].astype(bf16)
        return
    step = scratch.shape[0] // 16
    for place in range(16):
        owner = place ^ me
        rows = scratch[pl.ds(pl.multiple_of(owner * step, step), step), :].astype(bf16)
        target = send if place & 1 else keep
        target[(place >> 1) & 1, at + (place >> 2) * step : at + ((place >> 2) + 1) * step, :] = (
            rows
        )


def put_quarter(scratch, keep, send, at, me, relative):
    if not relative:
        keep[pl.ds(at, scratch.shape[0]), :] = scratch[...].astype(bf16)
        return
    step = scratch.shape[0] // 4
    for place in range(4):
        owner = place ^ (me & 3)
        rows = scratch[pl.ds(pl.multiple_of(owner * step, step), step), :].astype(bf16)
        target = send if place & 1 else keep
        target[place >> 1, at : at + step, :] = rows


def feed_kernel(
    me_ref,
    x_ref,
    mixed_ref,
    cot_ref,
    keep_ref,
    wo_ref,
    bo_ref,
    gain_ref,
    shift_ref,
    up_ref,
    upb_ref,
    down_ref,
    downb_ref,
    out_ref,
    gm_ref,
    gx_ref,
    upg_ref,
    small_ref,
    kept_ref,
    sent_ref,
    okept_ref,
    osent_ref,
    middle_ref,
    n2_ref,
    feed_ref,
    gn_ref,
    act_ref,
    gh_ref,
    dw_ref,
    *,
    relative,
    tile,
):
    step = pl.program_id(0)
    me = me_ref[0]
    length = x_ref.shape[0]
    tiles = length // tile

    @pl.when(step == 0)
    def _():
        small_ref[...] = jnp.zeros_like(small_ref)

        @pl.loop(0, tiles)
        def _(i):
            at = pl.ds(pl.multiple_of(i * tile, tile), tile)
            branch = nn(mixed_ref[at, :], wo_ref[...]) + bo_ref[...]
            middle = x_ref[at, :].astype(f32) + branch
            middle_ref[at, :] = middle
            norm, _ = normal_rows(middle)
            n2_ref[at, :] = (norm * gain_ref[...] + shift_ref[...]).astype(bf16)
            feed_ref[at, :] = jnp.zeros_like(middle)
            gn_ref[at, :] = jnp.zeros_like(middle)
            small_ref[5:6, :] += jnp.sum(branch * branch * keep_ref[at, :], 0, keepdims=True)

    up, down, up_bias = up_ref[...], down_ref[...], upb_ref[...]
    upg_ref[...] = jnp.zeros_like(upg_ref)

    @pl.loop(0, tiles)
    def _(i):
        at = pl.ds(pl.multiple_of(i * tile, tile), tile)
        hidden = nn(n2_ref[at, :], up) + up_bias
        gate = 0.5 * (1.0 + lax.erf(hidden * 0.7071067811865476))
        bell = jnp.exp(hidden * hidden * -0.5) * 0.3989422804014327
        act = (hidden * gate).astype(bf16)
        act_ref[at, :] = act
        gh = nt(cot_ref[at, :], down) * (gate + hidden * bell)
        gh_low = gh.astype(bf16)
        gh_ref[at, :] = gh_low
        upg_ref[...] += jnp.sum(gh_low.astype(f32), 0, keepdims=True)
        feed_ref[at, :] += nn(act, down)
        gn_ref[at, :] += nt(gh_low, up)

    dw_ref[...] = tn(n2_ref[...], gh_ref[...])
    put_rows(dw_ref, kept_ref.at[0], sent_ref.at[0], 0, me, relative)
    dw_ref[...] = tn(act_ref[...], cot_ref[...])
    put_quarter(dw_ref, kept_ref.at[0], sent_ref.at[0], 192 if relative else 768, me, relative)

    @pl.when(step == pl.num_programs(0) - 1)
    def _():
        @pl.loop(0, tiles)
        def _(i):
            at = pl.ds(pl.multiple_of(i * tile, tile), tile)
            feed = feed_ref[at, :] + downb_ref[...]
            middle = middle_ref[at, :]
            output = middle + feed
            out_ref[at, :] = output.astype(bf16)
            weight = keep_ref[at, :]
            cot = cot_ref[at, :].astype(f32)
            norm, scale = normal_rows(middle)
            grad = gn_ref[at, :]
            inner = grad * gain_ref[...]
            grad_middle = cot + scale * (
                inner
                - jnp.mean(inner, -1, keepdims=True)
                - norm * jnp.mean(inner * norm, -1, keepdims=True)
            )
            gm_ref[at, :] = grad_middle
            low = grad_middle.astype(bf16)
            gh_ref[at, :] = low
            gx_ref[at, :] = nt(low, wo_ref[...]).astype(bf16)
            small_ref[0:1, :] += jnp.sum(low.astype(f32), 0, keepdims=True)
            small_ref[1:2, :] += jnp.sum(grad * norm, 0, keepdims=True)
            small_ref[2:3, :] += jnp.sum(grad, 0, keepdims=True)
            small_ref[3:4, :] += jnp.sum(cot, 0, keepdims=True)
            small_ref[4:5, :] += jnp.sum(output * output * weight, 0, keepdims=True)
            small_ref[6:7, :] += jnp.sum(feed * feed * weight, 0, keepdims=True)

        dw_ref[...] = tn(mixed_ref[...], gh_ref[...])
        put_rows(dw_ref, okept_ref, osent_ref, 0, me, relative)


def block_shapes(rows, relative, lead=()):
    if relative:
        return lead + (2, rows // 4, 768), lead + (2, rows // 4, 768)
    return lead + (rows, 768), lead + (16, 128)


def feed_call(me, x, mixed, cot, keep, wo, bo, gain, shift, up, upb, down, downb, relative):
    length, width = x.shape
    hidden = up.shape[1]
    blocks = hidden // width
    tile = 256
    rows = full((length, width))
    row = full((1, width))
    kept, sent = block_shapes(2 * width, relative)
    okept, osent = block_shapes(width, relative)
    shape = jax.ShapeDtypeStruct
    grid_spec = pltpu.PrefetchScalarGridSpec(
        num_scalar_prefetch=1,
        grid=(blocks,),
        in_specs=[
            rows,
            rows,
            rows,
            full((length, 1)),
            full((width, width)),
            row,
            row,
            row,
            pl.BlockSpec((width, width), lambda j, *_: (0, j)),
            pl.BlockSpec((1, width), lambda j, *_: (0, j)),
            pl.BlockSpec((width, width), lambda j, *_: (j, 0)),
            row,
        ],
        out_specs=[
            rows,
            rows,
            rows,
            pl.BlockSpec((1, width), lambda j, *_: (0, j)),
            full((8, width)),
            pl.BlockSpec((1,) + kept, lambda j, *_: (j,) + (0,) * len(kept)),
            pl.BlockSpec((1,) + sent, lambda j, *_: (j,) + (0,) * len(sent)),
            full(okept),
            full(osent),
        ],
        scratch_shapes=[
            pltpu.VMEM((length, width), f32),
            pltpu.VMEM((length, width), bf16),
            pltpu.VMEM((length, width), f32),
            pltpu.VMEM((length, width), f32),
            pltpu.VMEM((length, width), bf16),
            pltpu.VMEM((length, width), bf16),
            pltpu.VMEM((width, width), f32),
        ],
    )
    return pl.pallas_call(
        functools.partial(feed_kernel, relative=relative, tile=tile),
        grid_spec=grid_spec,
        out_shape=[
            shape((length, width), bf16),
            shape((length, width), f32),
            shape((length, width), bf16),
            shape((1, hidden), f32),
            shape((8, width), f32),
            shape((blocks,) + kept, bf16),
            shape((blocks,) + sent, bf16),
            shape(okept, bf16),
            shape(osent, bf16),
        ],
        compiler_params=params(),
        cost_estimate=cost(
            12 * length * width * hidden + 6 * length * width * width,
            40 * length * width,
            2 * length * hidden,
        ),
        name="feed",
    )(me, x, mixed, cot, keep, wo, bo, gain, shift, up, upb, down, downb)


def weights_kernel(
    me_ref,
    x_ref,
    xp_ref,
    n_ref,
    np_ref,
    dq_ref,
    dk_ref,
    dv_ref,
    wq_ref,
    wk_ref,
    wv_ref,
    gq_ref,
    gp_ref,
    small_ref,
    kept_ref,
    sent_ref,
    dw_ref,
    *,
    relative,
    tile,
):
    me = me_ref[0]
    length = x_ref.shape[0]
    small_ref[...] = jnp.zeros_like(small_ref)

    @pl.loop(0, length // tile)
    def _(i):
        at = pl.ds(pl.multiple_of(i * tile, tile), tile)
        dq, dk, dv = dq_ref[at, :], dk_ref[at, :], dv_ref[at, :]
        far = nt(dk, wk_ref[...]) + nt(dv, wv_ref[...])
        gp_ref[at, :] = far.astype(bf16)
        own = nt(dq, wq_ref[...])
        gq_ref[at, :] = own
        norm, _ = normal_rows(x_ref[at, :].astype(f32))
        far_norm, _ = normal_rows(xp_ref[at, :].astype(f32))
        small_ref[0:1, :] += jnp.sum(dq.astype(f32), 0, keepdims=True)
        small_ref[1:2, :] += jnp.sum(own * norm, 0, keepdims=True)
        small_ref[2:3, :] += jnp.sum(own, 0, keepdims=True)
        small_ref[3:4, :] += jnp.sum(dv.astype(f32), 0, keepdims=True)
        small_ref[4:5, :] += jnp.sum(far * far_norm, 0, keepdims=True)
        small_ref[5:6, :] += jnp.sum(far, 0, keepdims=True)

    step = 192 if relative else 768
    dw_ref[...] = tn(n_ref[...], dq_ref[...])
    put_rows(dw_ref, kept_ref, sent_ref, 0, me, relative)
    dw_ref[...] = tn(np_ref[...], dk_ref[...])
    put_rows(dw_ref, kept_ref, sent_ref, step, me, relative)
    dw_ref[...] = tn(np_ref[...], dv_ref[...])
    put_rows(dw_ref, kept_ref, sent_ref, 2 * step, me, relative)


def weights_call(me, x, xp, n, n_far, dq, dk, dv, wq, wk, wv, relative):
    length, width = x.shape
    rows, square = full((length, width)), full((width, width))
    kept, sent = block_shapes(3 * width, relative)
    shape = jax.ShapeDtypeStruct
    grid_spec = pltpu.PrefetchScalarGridSpec(
        num_scalar_prefetch=1,
        grid=(1,),
        in_specs=[rows] * 7 + [square] * 3,
        out_specs=[rows, rows, full((8, width)), full(kept), full(sent)],
        scratch_shapes=[pltpu.VMEM((width, width), f32)],
    )
    return pl.pallas_call(
        functools.partial(weights_kernel, relative=relative, tile=256),
        grid_spec=grid_spec,
        out_shape=[
            shape((length, width), f32),
            shape((length, width), bf16),
            shape((8, width), f32),
            shape(kept, bf16),
            shape(sent, bf16),
        ],
        compiler_params=params(),
        cost_estimate=cost(12 * length * width * width, 24 * length * width),
        name="weights",
    )(me, x, xp, n, n_far, dq, dk, dv, wq, wk, wv)


def tokens_kernel(x_ref, gain_ref, gm_ref, gq_ref, gf_ref, out_ref):
    norm, scale = normal_rows(x_ref[...].astype(f32))
    inner = (gq_ref[...] + gf_ref[...].astype(f32)) * gain_ref[...]
    out_ref[...] = gm_ref[...] + scale * (
        inner
        - jnp.mean(inner, -1, keepdims=True)
        - norm * jnp.mean(inner * norm, -1, keepdims=True)
    )


def tokens_call(x, gain, gm, gq, gf):
    length, width = x.shape
    rows = pl.BlockSpec((256, width), lambda i: (i, 0))
    return pl.pallas_call(
        tokens_kernel,
        grid=(length // 256,),
        in_specs=[rows, full((1, width)), rows, rows, rows],
        out_specs=rows,
        out_shape=jax.ShapeDtypeStruct((length, width), f32),
        compiler_params=params(),
        cost_estimate=cost(20 * length * width, 16 * length * width),
        name="tokens",
    )(x, gain, gm, gq, gf)


def swapped(value, axis, mask):
    pairs = [(source, source ^ mask) for source in range(lax.axis_size(axis))]
    return lax.ppermute(value, axis, pairs)


def added(a, b, dtype=bf16):
    return (a.astype(f32) + b.astype(f32)).astype(dtype)


def near_sums(kept, sent):
    half = added(kept, swapped(sent, "dp", 1))
    return added(half[0], swapped(half[1], "dp", 2))


def far_sums(value):
    other = swapped(value[1::2], "dp", 4)
    half = added(value[0::2], other)
    return added(half[0], swapped(half[1], "dp", 8), f32)


def everywhere(value):
    mask = 1
    while mask < lax.axis_size("dp"):
        value = value + swapped(value, "dp", mask)
        mask *= 2
    return value


def pick_stream(pair, stream):
    return jnp.where(stream == 0, pair[0], pair[1])


def partner_weights(stacked, me):
    low = me & 3
    piece = swapped(lax.dynamic_index_in_dim(stacked, low, 0, keepdims=False), "stream", 1)
    half = jnp.stack([piece, swapped(piece, "dp", 2)])
    whole = jnp.stack([half, swapped(half, "dp", 1)], 1).reshape(stacked.shape)
    return whole[jnp.arange(4) ^ low]


def box_onehots(seg_boxes, buckets):
    half = buckets // 2
    levels = jnp.arange(buckets, dtype=jnp.int32)
    centre_x = (seg_boxes[..., 0] + seg_boxes[..., 2]) // 2
    centre_y = (seg_boxes[..., 1] + seg_boxes[..., 3]) // 2
    step_x = (
        jnp.clip((centre_x[:, None, :] - centre_x[:, :, None]) // box_step, -half, half - 1) + half
    )
    step_y = (
        jnp.clip((centre_y[:, None, :] - centre_y[:, :, None]) // box_step, -half, half - 1) + half
    )
    return (
        (step_x[..., None] == levels).astype(jnp.float32),
        (step_y[..., None] == levels).astype(jnp.float32),
    )


def body(
    tokens,
    first_gain,
    first_shift,
    query_weight,
    query_bias,
    key_weight,
    value_weight,
    value_bias,
    out_weight,
    out_bias,
    second_gain,
    second_shift,
    up_weight,
    up_bias,
    down_weight,
    down_bias,
    box_table,
    segments,
    validity,
    seg_boxes,
    cotangent,
):
    stream = lax.axis_index("stream")
    me = lax.axis_index("dp")
    shards = lax.axis_size("dp")
    width = tokens.shape[2]
    hidden = up_weight.shape[2]
    pages, page_len = segments.shape[1], segments.shape[2]
    length = pages * page_len
    relative = shards == 16
    me_ref = me.reshape(1).astype(jnp.int32)
    x = tokens[0]

    stacked = jnp.concatenate([key_weight[0], value_weight[0]], 0).reshape(4, width // 2, width)
    far_weights = partner_weights(stacked, me).reshape(2, width, width)
    far_rows = swapped(jnp.concatenate([first_gain, first_shift, value_bias], 0), "stream", 1)
    far_x = swapped(x, "stream", 1)

    own_seg = pick_stream(segments, stream)
    far_seg = pick_stream(segments, 1 - stream)
    own_keep = pick_stream(validity, stream)
    far_keep = pick_stream(validity, 1 - stream)
    levels = jnp.arange(64, dtype=jnp.int32)
    hot_q = (own_seg[:, :, None] == levels).astype(bf16)
    hot_kt = (far_seg[:, None, :] == levels[None, :, None]).astype(bf16)
    wide_levels = jnp.arange(128, dtype=jnp.int32)
    hot_k = jnp.where(
        wide_levels == 64,
        jnp.where(far_keep[:, :, None] > 0, 0.0, mask_fill),
        (far_seg[:, :, None] == wide_levels).astype(f32),
    ).astype(bf16)
    hot_x, hot_y = box_onehots(seg_boxes, BUCKETS)
    tables = box_table[0].reshape(2, HEADS, BUCKETS)
    seg_bias = (
        jnp.einsum("pabn,hn->phab", hot_x, tables[0], precision=precise_variant)
        + jnp.einsum("pabn,hn->phab", hot_y, tables[1], precision=precise_variant)
    ).astype(bf16)
    ones = (jnp.arange(64) == 0).astype(bf16)
    seg_bias = jnp.concatenate([seg_bias, jnp.broadcast_to(ones, seg_bias.shape)], -1)

    normed, query = query_call(x, first_gain, first_shift, query_weight[0], query_bias)
    far_normed, keys, value_rows = pair_call(
        far_x, far_rows[0:1], far_rows[1:2], far_weights[0], far_weights[1], far_rows[2:3]
    )
    mixed, log_total = attend_call(query, keys, value_rows, seg_bias, hot_q, hot_k)

    keep_column = own_keep.reshape(length, 1).astype(f32)
    output, grad_middle, grad_mixed, grad_up_bias, small, kept, sent, out_kept, out_sent = (
        feed_call(
            me_ref,
            x,
            mixed,
            cotangent[0],
            keep_column,
            out_weight[0],
            out_bias,
            second_gain,
            second_shift,
            up_weight[0],
            up_bias,
            down_weight[0],
            down_bias,
            relative,
        )
    )
    blocks = hidden // width

    grad_query, grad_keys, grad_values, grad_bias = attend_back_call(
        query, keys, value_rows, seg_bias, hot_q, hot_k, hot_kt, log_total, mixed, grad_mixed
    )
    own_grad, far_grad, small_two, kept_two, sent_two = weights_call(
        me_ref,
        x,
        far_x,
        normed,
        far_normed,
        grad_query,
        grad_keys,
        grad_values,
        query_weight[0],
        far_weights[0],
        far_weights[1],
        relative,
    )
    grad_tokens = tokens_call(
        x, first_gain, grad_middle, own_grad, swapped(far_grad, "stream", 1)
    )
    grad_table = jnp.concatenate(
        [
            jnp.einsum("pabn,phba->hn", hot_x, grad_bias, precision=precise_variant),
            jnp.einsum("pabn,phba->hn", hot_y, grad_bias, precision=precise_variant),
        ],
        0,
    ).reshape(1, -1)

    back = swapped(small_two[3:6], "stream", 1)
    counted = jnp.sum(own_keep).astype(f32)
    stats = jnp.concatenate(
        [jnp.sum(small[4:7], 1), counted[None], jnp.zeros((width - 4,), f32)]
    )
    rows = jnp.concatenate(
        [
            small[0:4],
            small_two[0:1],
            small_two[1:3] + back[1:3],
            back[0:1],
            grad_table,
            grad_up_bias.reshape(blocks, width),
            stats[None],
        ],
        0,
    )
    rows = everywhere(rows)
    part = width // shards
    lanes = lax.dynamic_slice_in_dim(rows, me * part, part, 1)
    up_part = lax.dynamic_slice_in_dim(
        rows[9 : 9 + blocks].reshape(1, hidden), me * (hidden // shards), hidden // shards, 1
    )
    totals = rows[9 + blocks]
    root_means = jnp.sqrt(totals[:3] / (totals[3] * width) + 1e-06).reshape(1, 3)

    if relative:
        near = [near_sums(kept[j], sent[j]) for j in range(blocks)]
        near_out = near_sums(out_kept, out_sent)
        down_parts = jnp.stack([value[192:] for value in near])
        down_parts = down_parts[jnp.arange(4) ^ (me >> 2)]
        first = jnp.concatenate(
            [value[:192].reshape(4, 48, width) for value in near]
            + [near_out.reshape(4, 48, width), down_parts],
            1,
        )
        first = far_sums(first)
        sum_up = jnp.concatenate([first[48 * j : 48 * (j + 1)] for j in range(blocks)], 1)
        sum_out = first[48 * blocks : 48 * blocks + 48]
        sum_down = first[48 * blocks + 48 :]
        near_two = near_sums(kept_two, sent_two)
        second = jnp.concatenate(
            [near_two[192 * j : 192 * (j + 1)].reshape(4, 48, width) for j in range(3)], 1
        )
        second = far_sums(second)
        sum_query = second[:48]
        sum_pair = second[48:].astype(bf16)
    else:

        def scattered(value):
            return lax.psum_scatter(value, "dp", scatter_dimension=0, tiled=True)

        grad_up = jnp.concatenate([kept[j, :width] for j in range(blocks)], 1)
        grad_down = jnp.concatenate([kept[j, width:] for j in range(blocks)], 0)
        sum_up = scattered(grad_up.astype(f32))
        sum_down = scattered(grad_down.astype(f32))
        sum_out = scattered(out_kept.astype(f32))
        sum_query = scattered(kept_two[:width].astype(f32))
        sum_pair = jnp.concatenate(
            [
                scattered(kept_two[width : 2 * width].astype(f32)),
                scattered(kept_two[2 * width :].astype(f32)),
            ],
            0,
        ).astype(bf16)
    sum_pair = swapped(sum_pair, "stream", 1).astype(f32)
    sum_keys, sum_values = sum_pair[:part], sum_pair[part:]

    return (
        output[None],
        grad_tokens[None],
        lanes[5:6],
        lanes[6:7],
        sum_query[None],
        lanes[4:5],
        sum_keys[None],
        sum_values[None],
        lanes[7:8],
        sum_out[None],
        lanes[0:1],
        lanes[1:2],
        lanes[2:3],
        sum_up[None],
        up_part,
        sum_down[None],
        lanes[3:4],
        lanes[8:9],
        root_means,
    )


def solution(mesh):
    whole, split = P("stream", None), P("stream", "dp")
    cube, cut = P("stream", None, None), P("stream", "dp", None)
    pages = P(None, "dp", None)
    in_specs = (
        cut, whole, whole, cube, whole, cube, cube, whole, cube, whole, whole, whole,
        cube, whole, cube, whole, whole, pages, pages, P("dp", None, None), cut,
    )
    out_specs = (
        cut, cut, split, split, cut, split, cut, cut, split, cut, split, split, split,
        cut, split, cut, split, split, whole,
    )
    return jax.shard_map(body, mesh=mesh, in_specs=in_specs, out_specs=out_specs, check_vma=False)
```

```python
import functools

import jax
import jax.numpy as jnp
from jax import lax
from jax.experimental import pallas as pl
from jax.experimental.pallas import tpu as pltpu
from jax.sharding import PartitionSpec as P

HEADS = 12
BUCKETS = 32
SMALL = 24

score_scale = 0.125
norm_eps = 1e-05
mask_fill = -1000000000.0
box_step = 32
precise_variant = lax.Precision.HIGHEST
f32 = jnp.float32
bf16 = jnp.bfloat16
VMEM_BYTES = 60 * 1024 * 1024


def nn(a, b):
    return lax.dot_general(a, b, (((1,), (0,)), ((), ())), preferred_element_type=f32)


def nt(a, b):
    return lax.dot_general(a, b, (((1,), (1,)), ((), ())), preferred_element_type=f32)


def tn(a, b):
    return lax.dot_general(a, b, (((0,), (0,)), ((), ())), preferred_element_type=f32)


def normal_rows(rows):
    centre = rows - jnp.mean(rows, -1, keepdims=True)
    spread = jnp.mean(centre * centre, -1, keepdims=True)
    scale = lax.rsqrt(spread + norm_eps)
    return centre * scale, scale


def params(**kw):
    return pltpu.CompilerParams(vmem_limit_bytes=VMEM_BYTES, **kw)


def cost(flops, moved, trans=0):
    return pl.CostEstimate(flops=int(flops), bytes_accessed=int(moved), transcendentals=int(trans))


def full(shape):
    zeros = (0,) * len(shape)
    return pl.BlockSpec(shape, lambda *_: zeros)


def query_kernel(x_ref, gain_ref, shift_ref, w_ref, b_ref, n_ref, q_ref):
    norm, _ = normal_rows(x_ref[...].astype(f32))
    low = (norm * gain_ref[...] + shift_ref[...]).astype(bf16)
    n_ref[...] = low
    query = (nn(low, w_ref[...]) + b_ref[...]).astype(bf16)
    q_ref[...] = (query.astype(f32) * score_scale).astype(bf16)


def query_call(x, gain, shift, weight, bias):
    length, width = x.shape
    tile = 256
    rows = pl.BlockSpec((tile, width), lambda i: (i, 0))
    return pl.pallas_call(
        query_kernel,
        grid=(length // tile,),
        in_specs=[rows, full((1, width)), full((1, width)), full(weight.shape), full((1, width))],
        out_specs=[rows, rows],
        out_shape=[jax.ShapeDtypeStruct(x.shape, bf16)] * 2,
        compiler_params=params(),
        cost_estimate=cost(2 * length * width * width, 6 * length * width + 2 * width * width),
        name="query",
    )(x, gain, shift, weight, bias)


def pair_kernel(me_ref, x_ref, rows_ref, *rest, count):
    pieces, (n_ref, k_ref, v_ref, w_ref) = rest[:count], rest[-4:]
    if count == 4:

        @pl.when(pl.program_id(0) == 0)
        def _():
            low = me_ref[0] & 3
            for place in range(4):
                w_ref[place ^ low] = pieces[place][...]

        weights = w_ref
    else:
        weights = pieces[0]
    half = weights.shape[1]
    norm, _ = normal_rows(x_ref[...].astype(f32))
    low = (norm * rows_ref[0:1, :] + rows_ref[1:2, :]).astype(bf16)
    n_ref[...] = low
    left, right = low[:, :half], low[:, half:]
    k_ref[...] = (nn(left, weights[0]) + nn(right, weights[1])).astype(bf16)
    v_ref[...] = (nn(left, weights[2]) + nn(right, weights[3]) + rows_ref[2:3, :]).astype(bf16)


def pair_call(page, length, me, x, rows, pieces, before):
    page_len, width = x.shape
    tile = 256
    first = page * page_len // tile
    placed = pl.BlockSpec((tile, width), lambda i, *_: (i + first, 0))
    left = pl.BlockSpec(memory_space=pl.ANY)
    weights = (4, width // 2, width)
    out_specs = [placed] * 3
    shapes = [jax.ShapeDtypeStruct((length, width), bf16)] * 3
    scratch = []
    if len(pieces) == 4:
        out_specs = out_specs + [full(weights)]
        shapes = shapes + [jax.ShapeDtypeStruct(weights, bf16)]
    else:
        scratch = [pltpu.VMEM((8, 128), f32)]
    grid_spec = pltpu.PrefetchScalarGridSpec(
        num_scalar_prefetch=1,
        grid=(page_len // tile,),
        in_specs=[
            pl.BlockSpec((tile, width), lambda i, *_: (i, 0)),
            full(rows.shape),
        ]
        + [full(piece.shape) for piece in pieces]
        + [left] * len(before),
        out_specs=out_specs,
        scratch_shapes=scratch,
    )
    return pl.pallas_call(
        functools.partial(pair_kernel, count=len(pieces)),
        grid_spec=grid_spec,
        out_shape=shapes,
        input_output_aliases={3 + len(pieces) + i: i for i in range(len(before))},
        compiler_params=params(),
        cost_estimate=cost(4 * page_len * width * width, 8 * page_len * width),
        name="pair",
    )(me, x, rows, *pieces, *before)


def head_lanes(value, head, head_dim):
    lane = lax.broadcasted_iota(jnp.int32, value.shape, 1)
    mine = (lane >= head * head_dim) & (lane < (head + 1) * head_dim)
    return jnp.where(mine, value, jnp.zeros_like(value))


def attend_kernel(q_ref, k_ref, v_ref, bias_ref, hq_ref, hk_ref, *rest):
    o_ref, lse_ref = rest[-2:]
    q, v = q_ref[...], v_ref[...]
    left = jnp.concatenate([k_ref[...], hk_ref[0]], 1)
    v_turned = v.astype(f32).T.astype(bf16)
    parts = []
    for head in range(2):
        picked = nn(hq_ref[0], bias_ref[0, head]).astype(bf16)
        right = jnp.concatenate([head_lanes(q, head, 64), picked], 1)
        scores = nt(left, right)
        peak = jnp.max(scores, 0, keepdims=True)
        raised = jnp.exp(scores - peak)
        total = jnp.sum(raised, 0, keepdims=True)
        probs = (raised * (1.0 / total)).astype(bf16)
        parts.append(nn(v_turned[head * 64 : (head + 1) * 64], probs))
        lse_ref[0, 0, head : head + 1, :] = peak + jnp.log(total)
    o_ref[...] = jnp.concatenate(parts, 0).T.astype(bf16)


def attend_specs(page_len, page, pair):
    rows = pl.BlockSpec((page_len, 128), lambda p, h: (p + page, h + pair))
    bias = pl.BlockSpec((1, 2, 64, 128), lambda p, h: (p + page, h + pair, 0, 0))
    lse = pl.BlockSpec((1, 1, 2, page_len), lambda p, h: (p + page, h + pair, 0, 0))

    def hot(*shape):
        return pl.BlockSpec((1,) + shape, lambda p, h: (p + page, 0, 0))

    return rows, bias, lse, hot


def attend_call(page, q, k, v, bias, hot_q, hot_k, before):
    length, width = q.shape
    pages, page_len = hot_q.shape[0], hot_q.shape[1]
    rows, bias_spec, lse, hot = attend_specs(page_len, page, 0)
    left = pl.BlockSpec(memory_space=pl.ANY)
    return pl.pallas_call(
        attend_kernel,
        grid=(1, width // 128),
        in_specs=[rows, rows, rows, bias_spec, hot(page_len, 64), hot(page_len, 128)]
        + [left] * len(before),
        out_specs=[rows, lse],
        out_shape=[
            jax.ShapeDtypeStruct((length, width), bf16),
            jax.ShapeDtypeStruct((pages, width // 128, 2, page_len), f32),
        ],
        input_output_aliases={6 + i: i for i in range(len(before))},
        compiler_params=params(),
        cost_estimate=cost(
            16 * page_len * page_len * width,
            8 * page_len * width,
            page_len * page_len * HEADS,
        ),
        name="attend",
    )(q, k, v, bias, hot_q, hot_k, *before)


def attend_back_kernel(
    q_ref,
    k_ref,
    v_ref,
    bias_ref,
    hq_ref,
    hk_ref,
    hkt_ref,
    lse_ref,
    o_ref,
    do_ref,
    dq_ref,
    dk_ref,
    dv_ref,
    gb_ref,
):
    q, k, v, do = q_ref[...], k_ref[...], v_ref[...], do_ref[...]
    hot_q = hq_ref[0]
    left = jnp.concatenate([k, hk_ref[0]], 1)
    k_turned = k.astype(f32).T.astype(bf16)
    overlap = do.astype(f32) * o_ref[...].astype(f32)
    row = lax.broadcasted_iota(jnp.int32, (8, 128), 0)
    lane = lax.broadcasted_iota(jnp.int32, (8, 128), 1)
    chooser = (row == lane // 64).astype(f32)
    delta = lax.dot_general(
        chooser,
        overlap,
        (((1,), (1,)), ((), ())),
        preferred_element_type=f32,
        precision=precise_variant,
    )
    parts, dk, dv = [], 0.0, 0.0
    for head in range(2):
        q_head, do_head = head_lanes(q, head, 64), head_lanes(do, head, 64)
        picked = nn(hot_q, bias_ref[0, head]).astype(bf16)
        right = jnp.concatenate([q_head, picked], 1)
        probs = jnp.exp(nt(left, right) - lse_ref[0, 0, head : head + 1, :])
        slope = nt(v, do_head)
        turn = (probs * (slope - delta[head : head + 1, :])).astype(bf16)
        dv = dv + nn(probs.astype(bf16), do_head)
        dk = dk + nn(turn, q_head)
        both = nn(jnp.concatenate([k_turned[head * 64 : (head + 1) * 64], hkt_ref[0]], 0), turn)
        parts.append(both[:64])
        sums = both[64:]
        high = sums.astype(bf16)
        rest = (sums - high.astype(f32)).astype(bf16)
        gb_ref[0, head] = nn(high, hot_q) + nn(rest, hot_q)
    dq_ref[...] = (jnp.concatenate(parts, 0) * score_scale).T.astype(bf16)
    dk_ref[...] = dk.astype(bf16)
    dv_ref[...] = dv.astype(bf16)


def attend_back_call(group, groups, q, k, v, bias, hot_q, hot_k, hot_kt, lse_in, o, do):
    length, width = q.shape
    pages, page_len = hot_q.shape[0], hot_q.shape[1]
    pairs = width // 128 // groups
    rows, bias_spec, lse, hot = attend_specs(page_len, 0, group * pairs)
    given = pl.BlockSpec((page_len, 128), lambda p, h: (p, h))
    grad_bias = pl.BlockSpec((1, 2, 64, 64), lambda p, h: (p, h, 0, 0))
    wide = jax.ShapeDtypeStruct((length, width // groups), bf16)
    return pl.pallas_call(
        attend_back_kernel,
        grid=(pages, pairs),
        in_specs=[
            rows,
            rows,
            rows,
            bias_spec,
            hot(page_len, 64),
            hot(page_len, 128),
            hot(64, page_len),
            lse,
            rows,
            rows,
        ],
        out_specs=[given, given, given, grad_bias],
        out_shape=[
            wide,
            wide,
            wide,
            jax.ShapeDtypeStruct((pages, HEADS // groups, 64, 64), f32),
        ],
        compiler_params=params(),
        cost_estimate=cost(
            40 * length * page_len * width // groups,
            16 * length * width // groups,
            length * page_len * HEADS // groups,
        ),
        name="attend_back",
    )(q, k, v, bias, hot_q, hot_k, hot_kt, lse_in, o, do)


def put_rows(scratch, keep, send, at, me, relative):
    if not relative:
        keep[pl.ds(at, scratch.shape[0]), :] = scratch[...].astype(bf16)
        return
    step = scratch.shape[0] // 16
    for place in range(16):
        owner = place ^ me
        rows = scratch[pl.ds(pl.multiple_of(owner * step, step), step), :].astype(bf16)
        target = send if place & 1 else keep
        low = at + (place >> 2) * step
        target[(place >> 1) & 1, low : low + step, :] = rows


def put_quarter(scratch, keep, send, at, me, relative):
    if not relative:
        keep[pl.ds(at, scratch.shape[0]), :] = scratch[...].astype(bf16)
        return
    step = scratch.shape[0] // 4
    for place in range(4):
        owner = place ^ (me & 3)
        rows = scratch[pl.ds(pl.multiple_of(owner * step, step), step), :].astype(bf16)
        target = send if place & 1 else keep
        target[place >> 1, at : at + step, :] = rows


def block_shapes(rows, width, relative):
    if relative:
        return (2, rows // 4, width), (2, rows // 4, width)
    return (rows, width), (16, 128)


def middle_kernel(
    x_ref, mixed_ref, keep_ref, wo_ref, bo_ref, gain_ref, shift_ref, middle_ref, n2_ref, small_ref
):
    @pl.when(pl.program_id(0) == 0)
    def _():
        small_ref[...] = jnp.zeros_like(small_ref)

    branch = nn(mixed_ref[...], wo_ref[...]) + bo_ref[...]
    middle = x_ref[...].astype(f32) + branch
    middle_ref[...] = middle
    norm, _ = normal_rows(middle)
    n2_ref[...] = (norm * gain_ref[...] + shift_ref[...]).astype(bf16)
    small_ref[15:16, :] += jnp.sum(branch * branch * keep_ref[...], 0, keepdims=True)
    small_ref[17:18, :] += jnp.broadcast_to(
        jnp.sum(keep_ref[...], 0, keepdims=True), (1, small_ref.shape[1])
    )


def middle_call(x, mixed, keep, wo, bo, gain, shift):
    length, width = x.shape
    tile = 256
    rows = pl.BlockSpec((tile, width), lambda i: (i, 0))
    row = full((1, width))
    shape = jax.ShapeDtypeStruct
    return pl.pallas_call(
        middle_kernel,
        grid=(length // tile,),
        in_specs=[
            rows,
            rows,
            pl.BlockSpec((tile, 1), lambda i: (i, 0)),
            full((width, width)),
            row,
            row,
            row,
        ],
        out_specs=[rows, rows, full((SMALL, width))],
        out_shape=[
            shape((length, width), f32),
            shape((length, width), bf16),
            shape((SMALL, width), f32),
        ],
        compiler_params=params(),
        cost_estimate=cost(4 * length * width * width, 10 * length * width),
        name="middle",
    )(x, mixed, keep, wo, bo, gain, shift)


def feed_kernel(
    me_ref,
    n2_ref,
    cot_ref,
    cots_ref,
    n2s_ref,
    up_ref,
    upb_ref,
    down_ref,
    old_ref,
    *rest,
    block,
    relative,
    tile,
):
    before, rest = rest[:-8], rest[-8:]
    feed_ref, gn_ref, small_ref, kept_ref, sent_ref, act_ref, gh_ref, dw_ref = rest
    step = pl.program_id(0)
    up, down = up_ref[...], down_ref[...]

    @pl.when(step == 0)
    def _():
        small_ref[...] = old_ref[...]

    at = pl.ds(pl.multiple_of(step * tile, tile), tile)
    hidden = nn(n2_ref[...], up) + upb_ref[...]
    gate = 0.5 * (1.0 + lax.erf(hidden * 0.7071067811865476))
    bell = jnp.exp(hidden * hidden * -0.5) * 0.3989422804014327
    act = (hidden * gate).astype(bf16)
    act_ref[at, :] = act
    gh = (nt(cot_ref[...], down) * (gate + hidden * bell)).astype(bf16)
    gh_ref[at, :] = gh
    small_ref[10 + block : 11 + block, :] += jnp.sum(gh.astype(f32), 0, keepdims=True)
    feed, gn = nn(act, down), nt(gh, up)
    if before:
        feed, gn = feed + before[0][...], gn + before[1][...]
    feed_ref[...] = feed
    gn_ref[...] = gn

    @pl.when(step == pl.num_programs(0) - 1)
    def _():
        me = me_ref[0]
        dw_ref[...] = tn(n2s_ref[...], gh_ref[...])
        put_rows(dw_ref, kept_ref, sent_ref, 0, me, relative)
        dw_ref[...] = tn(act_ref[...], cots_ref[...])
        put_quarter(dw_ref, kept_ref, sent_ref, 192 if relative else 768, me, relative)


def feed_call(block, me, n2, cot, up, upb, down, small, before, relative):
    length, width = n2.shape
    tile = 256
    rows = pl.BlockSpec((tile, width), lambda i, *_: (i, 0))
    whole = full((length, width))
    kept, sent = block_shapes(2 * width, width, relative)
    shape = jax.ShapeDtypeStruct
    grid_spec = pltpu.PrefetchScalarGridSpec(
        num_scalar_prefetch=1,
        grid=(length // tile,),
        in_specs=[
            rows,
            rows,
            whole,
            whole,
            pl.BlockSpec((width, width), lambda i, *_: (0, block)),
            pl.BlockSpec((1, width), lambda i, *_: (0, block)),
            pl.BlockSpec((width, width), lambda i, *_: (block, 0)),
            full((SMALL, width)),
        ]
        + [rows] * len(before),
        out_specs=[rows, rows, full((SMALL, width)), full(kept), full(sent)],
        scratch_shapes=[
            pltpu.VMEM((length, width), bf16),
            pltpu.VMEM((length, width), bf16),
            pltpu.VMEM((width, width), f32),
        ],
    )
    return pl.pallas_call(
        functools.partial(feed_kernel, block=block, relative=relative, tile=tile),
        grid_spec=grid_spec,
        out_shape=[
            shape((length, width), f32),
            shape((length, width), f32),
            shape((SMALL, width), f32),
            shape(kept, bf16),
            shape(sent, bf16),
        ],
        input_output_aliases={9 + i: i for i in range(len(before))},
        compiler_params=params(),
        cost_estimate=cost(
            12 * length * width * width, 20 * length * width, 2 * length * width
        ),
        name="feed",
    )(me, n2, cot, cot, n2, up, upb, down, small, *before)


def finish_kernel(
    me_ref,
    feed_ref,
    gn_ref,
    middle_ref,
    cot_ref,
    keep_ref,
    mixed_ref,
    wo_ref,
    gain_ref,
    downb_ref,
    old_ref,
    out_ref,
    gm_ref,
    gx_ref,
    small_ref,
    kept_ref,
    sent_ref,
    low_ref,
    dw_ref,
    *,
    relative,
    tile,
):
    step = pl.program_id(0)

    @pl.when(step == 0)
    def _():
        small_ref[...] = old_ref[...]

    at = pl.ds(pl.multiple_of(step * tile, tile), tile)
    feed = feed_ref[...] + downb_ref[...]
    middle = middle_ref[...]
    output = middle + feed
    out_ref[...] = output.astype(bf16)
    weight = keep_ref[...]
    cot = cot_ref[...].astype(f32)
    norm, scale = normal_rows(middle)
    grad = gn_ref[...]
    inner = grad * gain_ref[...]
    grad_middle = cot + scale * (
        inner
        - jnp.mean(inner, -1, keepdims=True)
        - norm * jnp.mean(inner * norm, -1, keepdims=True)
    )
    gm_ref[...] = grad_middle
    low = grad_middle.astype(bf16)
    low_ref[at, :] = low
    gx_ref[...] = nt(low, wo_ref[...]).astype(bf16)
    small_ref[0:1, :] += jnp.sum(low.astype(f32), 0, keepdims=True)
    small_ref[1:2, :] += jnp.sum(grad * norm, 0, keepdims=True)
    small_ref[2:3, :] += jnp.sum(grad, 0, keepdims=True)
    small_ref[3:4, :] += jnp.sum(cot, 0, keepdims=True)
    small_ref[14:15, :] += jnp.sum(output * output * weight, 0, keepdims=True)
    small_ref[16:17, :] += jnp.sum(feed * feed * weight, 0, keepdims=True)

    @pl.when(step == pl.num_programs(0) - 1)
    def _():
        dw_ref[...] = tn(mixed_ref[...], low_ref[...])
        put_rows(dw_ref, kept_ref, sent_ref, 0, me_ref[0], relative)


def finish_call(me, feed, gn, middle, cot, keep, mixed, wo, gain, downb, small, relative):
    length, width = mixed.shape
    tile = 256
    rows = pl.BlockSpec((tile, width), lambda i, *_: (i, 0))
    row = full((1, width))
    kept, sent = block_shapes(width, width, relative)
    shape = jax.ShapeDtypeStruct
    grid_spec = pltpu.PrefetchScalarGridSpec(
        num_scalar_prefetch=1,
        grid=(length // tile,),
        in_specs=[
            rows,
            rows,
            rows,
            rows,
            pl.BlockSpec((tile, 1), lambda i, *_: (i, 0)),
            full((length, width)),
            full((width, width)),
            row,
            row,
            full((SMALL, width)),
        ],
        out_specs=[rows, rows, rows, full((SMALL, width)), full(kept), full(sent)],
        scratch_shapes=[pltpu.VMEM((length, width), bf16), pltpu.VMEM((width, width), f32)],
    )
    return pl.pallas_call(
        functools.partial(finish_kernel, relative=relative, tile=tile),
        grid_spec=grid_spec,
        out_shape=[
            shape((length, width), bf16),
            shape((length, width), f32),
            shape((length, width), bf16),
            shape((SMALL, width), f32),
            shape(kept, bf16),
            shape(sent, bf16),
        ],
        compiler_params=params(),
        cost_estimate=cost(4 * length * width * width, 24 * length * width),
        name="finish",
    )(me, feed, gn, middle, cot, keep, mixed, wo, gain, downb, small)


def weights_kernel(
    me_ref,
    x_ref,
    xp_ref,
    n_ref,
    np_ref,
    dq_ref,
    dk_ref,
    dv_ref,
    wq_ref,
    wp_ref,
    old_ref,
    *rest,
    group,
    relative,
    tile,
    last,
):
    before, rest = rest[:-6], rest[-6:]
    gq_ref, gp_ref, small_ref, kept_ref, sent_ref, dw_ref = rest
    me = me_ref[0]
    length, width = x_ref.shape
    part = dq_ref.shape[1]
    lanes = slice(group * part, (group + 1) * part)
    small_ref[...] = old_ref[...]
    wk = wp_ref[0:2].reshape(width, part)
    wv = wp_ref[2:4].reshape(width, part)

    @pl.loop(0, length // tile)
    def _(i):
        at = pl.ds(pl.multiple_of(i * tile, tile), tile)
        dq, dk, dv = dq_ref[at, :], dk_ref[at, :], dv_ref[at, :]
        far = nt(dk, wk) + nt(dv, wv)
        own = nt(dq, wq_ref[...])
        if before:
            own, far = own + before[0][at, :], far + before[1][at, :]
        gq_ref[at, :] = own
        gp_ref[at, :] = far.astype(gp_ref.dtype)
        small_ref[4:5, lanes] += jnp.sum(dq.astype(f32), 0, keepdims=True)
        small_ref[7:8, lanes] += jnp.sum(dv.astype(f32), 0, keepdims=True)
        if last:
            norm, _ = normal_rows(x_ref[at, :].astype(f32))
            far_norm, _ = normal_rows(xp_ref[at, :].astype(f32))
            small_ref[5:6, :] += jnp.sum(own * norm, 0, keepdims=True)
            small_ref[6:7, :] += jnp.sum(own, 0, keepdims=True)
            small_ref[8:9, :] += jnp.sum(far * far_norm, 0, keepdims=True)
            small_ref[9:10, :] += jnp.sum(far, 0, keepdims=True)

    step = 192 if relative else 768
    dw_ref[...] = tn(n_ref[...], dq_ref[...])
    put_rows(dw_ref, kept_ref, sent_ref, 0, me, relative)
    dw_ref[...] = tn(np_ref[...], dk_ref[...])
    put_rows(dw_ref, kept_ref, sent_ref, step, me, relative)
    dw_ref[...] = tn(np_ref[...], dv_ref[...])
    put_rows(dw_ref, kept_ref, sent_ref, 2 * step, me, relative)


def weights_call(group, groups, me, x, xp, n, n_far, dq, dk, dv, wq, wp, small, before, relative):
    length, width = x.shape
    part = width // groups
    last = group == groups - 1
    rows, some = full((length, width)), full((length, part))
    columns = pl.BlockSpec((width, part), lambda i, *_: (0, group))
    far_columns = pl.BlockSpec((4, width // 2, part), lambda i, *_: (0, 0, group))
    kept, sent = block_shapes(3 * width, part, relative)
    shape = jax.ShapeDtypeStruct
    grid_spec = pltpu.PrefetchScalarGridSpec(
        num_scalar_prefetch=1,
        grid=(1,),
        in_specs=[rows] * 4
        + [some] * 3
        + [columns, far_columns, full((SMALL, width))]
        + [rows] * len(before),
        out_specs=[rows, rows, full((SMALL, width)), full(kept), full(sent)],
        scratch_shapes=[pltpu.VMEM((width, part), f32)],
    )
    return pl.pallas_call(
        functools.partial(
            weights_kernel, group=group, relative=relative, tile=256, last=last
        ),
        grid_spec=grid_spec,
        out_shape=[
            shape((length, width), f32),
            shape((length, width), bf16 if last else f32),
            shape((SMALL, width), f32),
            shape(kept, bf16),
            shape(sent, bf16),
        ],
        compiler_params=params(),
        cost_estimate=cost(12 * length * width * part, 24 * length * width),
        name="weights",
    )(me, x, xp, n, n_far, dq, dk, dv, wq, wp, small, *before)


def tokens_kernel(x_ref, gain_ref, gm_ref, gq_ref, gf_ref, out_ref):
    norm, scale = normal_rows(x_ref[...].astype(f32))
    inner = (gq_ref[...] + gf_ref[...].astype(f32)) * gain_ref[...]
    out_ref[...] = gm_ref[...] + scale * (
        inner
        - jnp.mean(inner, -1, keepdims=True)
        - norm * jnp.mean(inner * norm, -1, keepdims=True)
    )


def tokens_call(x, gain, gm, gq, gf):
    length, width = x.shape
    rows = pl.BlockSpec((256, width), lambda i: (i, 0))
    return pl.pallas_call(
        tokens_kernel,
        grid=(length // 256,),
        in_specs=[rows, full((1, width)), rows, rows, rows],
        out_specs=rows,
        out_shape=jax.ShapeDtypeStruct((length, width), f32),
        compiler_params=params(),
        cost_estimate=cost(20 * length * width, 16 * length * width),
        name="tokens",
    )(x, gain, gm, gq, gf)


def swapped(value, axis, mask):
    pairs = [(source, source ^ mask) for source in range(lax.axis_size(axis))]
    return lax.ppermute(value, axis, pairs)


def added(a, b, dtype=bf16):
    return (a.astype(f32) + b.astype(f32)).astype(dtype)


def together(kernel, inputs, moves):
    inputs, values = lax.optimization_barrier((inputs, [value for value, _, _ in moves]))
    came = [swapped(value, *way[1:]) for value, way in zip(values, moves)]
    results = kernel(*inputs) if kernel else []
    return lax.optimization_barrier((results, came))


def core_add(pair, came):
    return added(pair[0][0], came[0]), added(pair[0][1], came[1])


def z_parts(value):
    return value[0::2], value[1::2]


def everywhere(value):
    mask = 1
    while mask < lax.axis_size("dp"):
        value = value + swapped(value, "dp", mask)
        mask *= 2
    return value


def pick_stream(pair, stream):
    return jnp.where(stream == 0, pair[0], pair[1])


def box_onehots(seg_boxes, buckets):
    half = buckets // 2
    levels = jnp.arange(buckets, dtype=jnp.int32)
    centre_x = (seg_boxes[..., 0] + seg_boxes[..., 2]) // 2
    centre_y = (seg_boxes[..., 1] + seg_boxes[..., 3]) // 2
    step_x = (
        jnp.clip((centre_x[:, None, :] - centre_x[:, :, None]) // box_step, -half, half - 1) + half
    )
    step_y = (
        jnp.clip((centre_y[:, None, :] - centre_y[:, :, None]) // box_step, -half, half - 1) + half
    )
    return (
        (step_x[..., None] == levels).astype(jnp.float32),
        (step_y[..., None] == levels).astype(jnp.float32),
    )


def body(
    tokens,
    first_gain,
    first_shift,
    query_weight,
    query_bias,
    key_weight,
    value_weight,
    value_bias,
    out_weight,
    out_bias,
    second_gain,
    second_shift,
    up_weight,
    up_bias,
    down_weight,
    down_bias,
    box_table,
    segments,
    validity,
    seg_boxes,
    cotangent,
):
    stream = lax.axis_index("stream")
    me = lax.axis_index("dp")
    shards = lax.axis_size("dp")
    width = tokens.shape[2]
    hidden = up_weight.shape[2]
    pages, page_len = segments.shape[1], segments.shape[2]
    length = pages * page_len
    relative = shards == 16
    me_ref = me.reshape(1).astype(jnp.int32)
    x = tokens[0]

    own_seg = pick_stream(segments, stream)
    far_seg = pick_stream(segments, 1 - stream)
    own_keep = pick_stream(validity, stream)
    far_keep = pick_stream(validity, 1 - stream)
    levels = jnp.arange(64, dtype=jnp.int32)
    hot_q = (own_seg[:, :, None] == levels).astype(bf16)
    hot_kt = (far_seg[:, None, :] == levels[None, :, None]).astype(bf16)
    wide_levels = jnp.arange(128, dtype=jnp.int32)
    hot_k = jnp.where(
        wide_levels == 64,
        jnp.where(far_keep[:, :, None] > 0, 0.0, mask_fill),
        (far_seg[:, :, None] == wide_levels).astype(f32),
    ).astype(bf16)
    hot_x, hot_y = box_onehots(seg_boxes, BUCKETS)
    tables = box_table[0].reshape(2, HEADS, BUCKETS)
    seg_bias = (
        jnp.einsum("pabn,hn->phab", hot_x, tables[0], precision=precise_variant)
        + jnp.einsum("pabn,hn->phab", hot_y, tables[1], precision=precise_variant)
    ).astype(bf16)
    ones = (jnp.arange(64) == 0).astype(bf16)
    seg_bias = jnp.concatenate([seg_bias, jnp.broadcast_to(ones, seg_bias.shape)], -1)

    keep_column = own_keep.reshape(length, 1).astype(f32)
    blocks, groups = hidden // width, 2
    part, chunk = width // groups, width // shards
    cot = cotangent[0]
    Y, CORE, X, Z1, Z2 = ("stream", 1), ("dp", 1), ("dp", 2), ("dp", 4), ("dp", 8)

    low = me & 3
    half = width // 2

    def quarter(weight):
        return lax.dynamic_slice_in_dim(weight[0], (low & 1) * half, half, 0)

    piece = jnp.where(low < 2, quarter(key_weight), quarter(value_weight))
    vectors = jnp.concatenate([first_gain, first_shift, value_bias], 0)
    (normed, query), (piece, far_rows) = together(
        query_call,
        (x, first_gain, first_shift, query_weight[0], query_bias),
        [(piece, *Y), (vectors, *Y)],
    )
    page_x = [x[page * page_len : (page + 1) * page_len] for page in range(pages)]
    (seg_bias, hot_q, hot_k), (x_piece, core_piece, came_x) = together(
        lambda *same: same,
        (seg_bias, hot_q, hot_k),
        [(piece, *X), (piece, *CORE), (page_x[0], *Y)],
    )
    far_pages = [came_x]
    pieces = [piece, core_piece, x_piece, swapped(x_piece, *CORE)]
    far, mixing = (), ()
    for page in range(pages):

        def page_step(came, pieces, far, mixing, page=page):
            far = pair_call(page, length, me_ref, came, far_rows, pieces, far)
            return far, attend_call(page, query, far[1], far[2], seg_bias, hot_q, hot_k, mixing)

        moves = [(page_x[page + 1], *Y)] if page + 1 < pages else []
        (result, mixing), came = together(
            page_step, (far_pages[page], pieces, tuple(far), tuple(mixing)), moves
        )
        far, mixing = result[:3], mixing
        if page == 0:
            pieces = [result[3]]
        far_pages += came
    far_normed, keys, value_rows = far
    far_weights = pieces[0]
    mixed, log_total = mixing

    middle, normed_two, small = middle_call(
        x, mixed, keep_column, out_weight[0], out_bias, second_gain, second_shift
    )

    def feed_block(block):
        def call(n2, small, *sums):
            return feed_call(
                block, me_ref, n2, cot, up_weight[0], up_bias, down_weight[0], small, sums, relative
            )

        return call

    def finish(feed, gn, small):
        return finish_call(
            me_ref, feed, gn, middle, cot, keep_column, mixed, out_weight[0], second_gain,
            down_bias, small, relative,
        )

    def back_group(group):
        def call(grad_mixed):
            return attend_back_call(
                group, groups, query, keys, value_rows, seg_bias, hot_q, hot_k, hot_kt, log_total,
                mixed, grad_mixed,
            )

        return call

    far_x = jnp.concatenate(far_pages, 0)

    def weights_group(group):
        def call(small, dq, dk, dv, *before):
            return weights_call(
                group, groups, me_ref, x, far_x, normed, far_normed, dq, dk, dv,
                query_weight[0], far_weights, small, before, relative,
            )

        return call

    def table_rows(small, grad_bias):
        grad_table = jnp.concatenate(
            [
                jnp.einsum("pabn,phba->hn", hot_x, grad_bias, precision=precise_variant),
                jnp.einsum("pabn,phba->hn", hot_y, grad_bias, precision=precise_variant),
            ],
            0,
        ).reshape(1, -1)
        return small + jnp.pad(grad_table, ((18, SMALL - 19), (0, 0)))

    if relative:
        (*sums, small, k0, s0), _ = together(feed_block(0), (normed_two, small), [])
        (*sums, small, k1, s1), (c0,) = together(
            feed_block(1), (normed_two, small, *sums), [(s0, *CORE)]
        )
        m0, t0 = core_add((k0,), c0)
        (*sums, small, k2, s2), (c1, x0) = together(
            feed_block(2), (normed_two, small, *sums), [(s1, *CORE), (t0, *X)]
        )
        n0 = added(m0, x0)
        m1, t1 = core_add((k1,), c1)
        (*sums, small, k3, s3), (c2, x1) = together(
            feed_block(3), (normed_two, small, *sums), [(s2, *CORE), (t1, *X)]
        )
        n1 = added(m1, x1)
        m2, t2 = core_add((k2,), c2)

        def quads(*values):
            return jnp.concatenate([value.reshape(4, 48, -1) for value in values], 1)

        up_keep, up_go = z_parts(quads(n0[:192], n1[:192]))
        (output, grad_middle, grad_mixed, small, ko, so), (c3, x2, z0) = together(
            finish, (*sums, small), [(s3, *CORE), (t2, *X), (up_go, *Z1)]
        )
        n2 = added(m2, x2)
        m3, t3 = core_add((k3,), c3)
        up_half = added(up_keep, z0)
        (dq, dk, dv, grad_bias), (co, x3, z0) = together(
            back_group(0), (grad_mixed,), [(so, *CORE), (t3, *X), (up_half[1], *Z2)]
        )
        up_low = added(up_half[0], z0, f32)
        n3 = added(m3, x3)
        mo, to = core_add((ko,), co)
        down = jnp.stack([value[192:] for value in (n0, n1, n2, n3)])
        down_keep, down_go = z_parts(down[jnp.arange(4) ^ (me >> 2)])
        (*sums, small, kq, sq), (xo, z0) = together(
            weights_group(0), (small, dq, dk, dv), [(to, *X), (down_go, *Z1)]
        )
        no = added(mo, xo)
        down_half = added(down_keep, z0)
        rest_keep, rest_go = z_parts(quads(n2[:192], n3[:192], no))
        (dq, dk, dv, grad_bias_two), (cq, z0, z1) = together(
            back_group(1),
            (grad_mixed,),
            [(sq, *CORE), (down_half[1], *Z2), (rest_go, *Z1)],
        )
        sum_down = added(down_half[0], z0, f32)
        rest_half = added(rest_keep, z1)
        mq, tq = core_add((kq,), cq)
        (own_grad, far_grad, small, kr, sr), (xq, z0) = together(
            weights_group(1), (small, dq, dk, dv, *sums), [(tq, *X), (rest_half[1], *Z2)]
        )
        rest = added(rest_half[0], z0, f32)
        sum_up = jnp.concatenate([up_low[:48], up_low[48:], rest[:48], rest[48:96]], 1)
        sum_out = rest[96:]
        small = table_rows(small, jnp.concatenate([grad_bias, grad_bias_two], 1))
        came_grad = swapped(far_grad, *Y)
        nq = added(mq, xq)
        q_keep, q_go = z_parts(quads(nq[:192], nq[192:384], nq[384:]))
        _, (cr, z0, came) = together(None, (), [(sr, *CORE), (q_go, *Z1), (small, *CORE)])
        small = small + came
        mr, tr = core_add((kr,), cr)
        q_half = added(q_keep, z0)
        _, (xr, z0, came) = together(None, (), [(tr, *X), (q_half[1], *Z2), (small, *X)])
        small = small + came
        first = added(q_half[0], z0, f32)
        nr = added(mr, xr)
        r_keep, r_go = z_parts(quads(nr[:192], nr[192:384], nr[384:]))
        _, (z0, came) = together(None, (), [(r_go, *Z1), (small, *Z1)])
        small = small + came
        r_half = added(r_keep, z0)
        _, (z0, came) = together(None, (), [(r_half[1], *Z2), (small, *Z2)])
        small = small + came
        second = added(r_half[0], z0, f32)
        three = jnp.concatenate([first, second], 1)
        sum_query, sum_pair = three[:48], three[48:].astype(bf16)
    else:
        sums, grads = (), []
        for block in range(blocks):
            *sums, small, kept, sent = feed_block(block)(normed_two, small, *sums)
            grads.append(kept)
        output, grad_middle, grad_mixed, small, out_kept, _ = finish(*sums, small)
        back_sums, grad_biases, parts = (), [], []
        for group in range(groups):
            dq, dk, dv, grad_bias = back_group(group)(grad_mixed)
            *back_sums, small, kept, _ = weights_group(group)(small, dq, dk, dv, *back_sums)
            grad_biases.append(grad_bias)
            parts.append(kept)
        own_grad, far_grad = back_sums
        came_grad = swapped(far_grad, *Y)
        small = everywhere(table_rows(small, jnp.concatenate(grad_biases, 1)))

        def scattered(value):
            return lax.psum_scatter(value.astype(f32), "dp", scatter_dimension=0, tiled=True)

        sum_up = scattered(jnp.concatenate([kept[:width] for kept in grads], 1))
        sum_down = scattered(jnp.concatenate([kept[width:] for kept in grads], 0))
        sum_out = scattered(out_kept)
        three = jnp.concatenate(parts, 1)
        sum_query = scattered(three[:width])
        sum_pair = jnp.concatenate(
            [scattered(three[width : 2 * width]), scattered(three[2 * width :])], 0
        ).astype(bf16)

    lanes = lax.dynamic_slice_in_dim(small, me * chunk, chunk, 1)
    grad_tokens = tokens_call(x, first_gain, grad_middle, own_grad, came_grad)
    sum_pair, back = swapped((sum_pair, lanes[7:10]), *Y)
    sum_keys, sum_values = sum_pair[:chunk].astype(f32), sum_pair[chunk:].astype(f32)
    up_part = lax.dynamic_slice_in_dim(
        small[10 : 10 + blocks].reshape(1, hidden), me * (hidden // shards), hidden // shards, 1
    )
    totals = jnp.sum(small[14:17], 1)
    root_means = jnp.sqrt(totals / (small[17, 0] * width) + 1e-06).reshape(1, 3)

    return (
        output[None],
        grad_tokens[None],
        lanes[5:6] + back[1:2],
        lanes[6:7] + back[2:3],
        sum_query[None],
        lanes[4:5],
        sum_keys[None],
        sum_values[None],
        back[0:1],
        sum_out[None],
        lanes[0:1],
        lanes[1:2],
        lanes[2:3],
        sum_up[None],
        up_part,
        sum_down[None],
        lanes[3:4],
        lanes[18:19],
        root_means,
    )


def solution(mesh):
    whole, split = P("stream", None), P("stream", "dp")
    cube, cut = P("stream", None, None), P("stream", "dp", None)
    pages = P(None, "dp", None)
    in_specs = (
        cut, whole, whole, cube, whole, cube, cube, whole, cube, whole, whole, whole,
        cube, whole, cube, whole, whole, pages, pages, P("dp", None, None), cut,
    )
    out_specs = (
        cut, cut, split, split, cut, split, cut, cut, split, cut, split, split, split,
        cut, split, cut, split, split, whole,
    )
    return jax.shard_map(body, mesh=mesh, in_specs=in_specs, out_specs=out_specs, check_vma=False)
```

```python
import functools

import jax
import jax.numpy as jnp
from jax import lax
from jax.experimental import pallas as pl
from jax.experimental.pallas import tpu as pltpu
from jax.sharding import PartitionSpec as P

HEADS = 12
BUCKETS = 32
SMALL = 24

score_scale = 0.125
norm_eps = 1e-05
mask_fill = -1000000000.0
box_step = 32
precise_variant = lax.Precision.HIGHEST
f32 = jnp.float32
bf16 = jnp.bfloat16


def nn(a, b):
    return lax.dot_general(a, b, (((1,), (0,)), ((), ())), preferred_element_type=f32)


def nt(a, b):
    return lax.dot_general(a, b, (((1,), (1,)), ((), ())), preferred_element_type=f32)


def tn(a, b):
    return lax.dot_general(a, b, (((0,), (0,)), ((), ())), preferred_element_type=f32)


def normal_rows(rows):
    centre = rows - jnp.mean(rows, -1, keepdims=True)
    spread = jnp.mean(centre * centre, -1, keepdims=True)
    scale = lax.rsqrt(spread + norm_eps)
    return centre * scale, scale


def params(mib=60):
    return pltpu.CompilerParams(vmem_limit_bytes=mib * 1024 * 1024)


def cost(flops, moved, trans=0, scale=1 / 64):
    return pl.CostEstimate(
        flops=int(flops * scale),
        bytes_accessed=int(moved * scale),
        transcendentals=int(trans * scale),
    )


def full(shape):
    zeros = (0,) * len(shape)
    return pl.BlockSpec(shape, lambda *_: zeros)


def query_kernel(x_ref, gain_ref, shift_ref, w_ref, b_ref, n_ref, q_ref):
    norm, _ = normal_rows(x_ref[...].astype(f32))
    low = (norm * gain_ref[...] + shift_ref[...]).astype(bf16)
    n_ref[...] = low
    query = (nn(low, w_ref[...]) + b_ref[...]).astype(bf16)
    q_ref[...] = (query.astype(f32) * score_scale).astype(bf16)


def query_call(x, gain, shift, weight, bias):
    length, width = x.shape
    tile = 256
    rows = pl.BlockSpec((tile, width), lambda i: (i, 0))
    return pl.pallas_call(
        query_kernel,
        grid=(length // tile,),
        in_specs=[rows, full((1, width)), full((1, width)), full(weight.shape), full((1, width))],
        out_specs=[rows, rows],
        out_shape=[jax.ShapeDtypeStruct(x.shape, bf16)] * 2,
        compiler_params=params(),
        cost_estimate=cost(2 * length * width * width, 6 * length * width + 2 * width * width),
        name="query",
    )(x, gain, shift, weight, bias)


def pair_kernel(me_ref, x_ref, rows_ref, *rest, count):
    pieces, (n_ref, k_ref, v_ref, copy_ref, w_ref) = rest[:count], rest[-5:]
    if count == 4:

        @pl.when(pl.program_id(0) == 0)
        def _():
            low = me_ref[0] & 3
            for place in range(4):
                w_ref[place ^ low] = pieces[place][...]

        weights = w_ref
    else:
        weights = pieces[0]
    half = weights.shape[1]
    copy_ref[...] = x_ref[...]
    norm, _ = normal_rows(x_ref[...].astype(f32))
    low = (norm * rows_ref[0:1, :] + rows_ref[1:2, :]).astype(bf16)
    n_ref[...] = low
    left, right = low[:, :half], low[:, half:]
    k_ref[...] = (nn(left, weights[0]) + nn(right, weights[1])).astype(bf16)
    v_ref[...] = (nn(left, weights[2]) + nn(right, weights[3]) + rows_ref[2:3, :]).astype(bf16)


def pair_call(page, length, me, x, rows, pieces, before):
    page_len, width = x.shape
    tile = 256
    first = page * page_len // tile
    placed = pl.BlockSpec((tile, width), lambda i, *_: (i + first, 0))
    left = pl.BlockSpec(memory_space=pl.ANY)
    weights = (4, width // 2, width)
    out_specs = [placed] * 4
    shapes = [jax.ShapeDtypeStruct((length, width), bf16)] * 4
    scratch = []
    if len(pieces) == 4:
        out_specs = out_specs + [full(weights)]
        shapes = shapes + [jax.ShapeDtypeStruct(weights, bf16)]
    else:
        scratch = [pltpu.VMEM((8, 128), f32)]
    grid_spec = pltpu.PrefetchScalarGridSpec(
        num_scalar_prefetch=1,
        grid=(page_len // tile,),
        in_specs=[
            pl.BlockSpec((tile, width), lambda i, *_: (i, 0)),
            full(rows.shape),
        ]
        + [full(piece.shape) for piece in pieces]
        + [left] * len(before),
        out_specs=out_specs,
        scratch_shapes=scratch,
    )
    return pl.pallas_call(
        functools.partial(pair_kernel, count=len(pieces)),
        grid_spec=grid_spec,
        out_shape=shapes,
        input_output_aliases={3 + len(pieces) + i: i for i in range(len(before))},
        compiler_params=params(),
        cost_estimate=cost(4 * page_len * width * width, 8 * page_len * width),
        name="pair",
    )(me, x, rows, *pieces, *before)


def head_lanes(value, head, head_dim):
    lane = lax.broadcasted_iota(jnp.int32, value.shape, 1)
    mine = (lane >= head * head_dim) & (lane < (head + 1) * head_dim)
    return jnp.where(mine, value, jnp.zeros_like(value))


def picks_kernel(hq_ref, bias_ref, out_ref):
    for pair in range(out_ref.shape[1] // 256):
        both = jnp.concatenate([bias_ref[0, 2 * pair], bias_ref[0, 2 * pair + 1]], 1)
        out_ref[:, 256 * pair : 256 * (pair + 1)] = nn(hq_ref[0], both).astype(bf16)


def picks_call(hot_q, bias):
    pages, page_len = hot_q.shape[0], hot_q.shape[1]
    return pl.pallas_call(
        picks_kernel,
        grid=(pages, 3),
        in_specs=[
            pl.BlockSpec((1, page_len, 64), lambda p, h: (p, 0, 0)),
            pl.BlockSpec((1, 4, 64, 128), lambda p, h: (p, h, 0, 0)),
        ],
        out_specs=pl.BlockSpec((page_len, 512), lambda p, h: (p, h)),
        out_shape=jax.ShapeDtypeStruct((pages * page_len, HEADS * 128), bf16),
        compiler_params=params(),
        cost_estimate=cost(2 * pages * page_len * HEADS * 128 * 64, pages * page_len * HEADS * 256),
        name="picks",
    )(hot_q, bias)


def pair_right(q, picks):
    heads = [head_lanes(q, head, 64) for head in range(2)]
    sides = [
        jnp.concatenate([heads[head], picks[:, 128 * head : 128 * (head + 1)]], 1)
        for head in range(2)
    ]
    return jnp.concatenate(heads, 0), jnp.concatenate(sides, 0)


def attend_kernel(q_ref, k_ref, v_ref, picks_ref, hk_ref, *rest):
    o_ref, lse_ref = rest[-2:]
    page_len = q_ref.shape[0]
    for pair in range(q_ref.shape[1] // 128):
        lanes = slice(128 * pair, 128 * (pair + 1))
        left = jnp.concatenate([k_ref[:, lanes], hk_ref[0]], 1)
        v_turned = v_ref[:, lanes].astype(f32).T.astype(bf16)
        _, right = pair_right(q_ref[:, lanes], picks_ref[:, 256 * pair : 256 * (pair + 1)])
        scores = nt(left, right)
        peak = jnp.max(scores, 0, keepdims=True)
        raised = jnp.exp(scores - peak)
        total = jnp.sum(raised, 0, keepdims=True)
        probs = (raised * (1.0 / total)).astype(bf16)
        lse = peak + jnp.log(total)
        parts = []
        for head in range(2):
            mine = slice(head * page_len, (head + 1) * page_len)
            parts.append(nn(v_turned[head * 64 : (head + 1) * 64], probs[:, mine]))
            lse_ref[0, pair, head : head + 1, :] = lse[:, mine]
        o_ref[:, lanes] = jnp.concatenate(parts, 0).T.astype(bf16)


PAIRS = 2


def attend_specs(page_len, page, first):
    rows = pl.BlockSpec((page_len, 128 * PAIRS), lambda p, h: (p + page, h + first))
    picks = pl.BlockSpec((page_len, 256 * PAIRS), lambda p, h: (p + page, h + first))
    lse = pl.BlockSpec((1, PAIRS, 2, page_len), lambda p, h: (p + page, h + first, 0, 0))

    def hot(*shape):
        return pl.BlockSpec((1,) + shape, lambda p, h: (p + page, 0, 0))

    return rows, picks, lse, hot


def attend_call(page, q, k, v, picks, hot_k, before):
    length, width = q.shape
    pages, page_len = hot_k.shape[0], hot_k.shape[1]
    rows, picks_spec, lse, hot = attend_specs(page_len, page, 0)
    left = pl.BlockSpec(memory_space=pl.ANY)
    return pl.pallas_call(
        attend_kernel,
        grid=(1, width // 128 // PAIRS),
        in_specs=[rows, rows, rows, picks_spec, hot(page_len, 128)] + [left] * len(before),
        out_specs=[rows, lse],
        out_shape=[
            jax.ShapeDtypeStruct((length, width), bf16),
            jax.ShapeDtypeStruct((pages, width // 128, 2, page_len), f32),
        ],
        input_output_aliases={5 + i: i for i in range(len(before))},
        compiler_params=params(),
        cost_estimate=cost(
            16 * page_len * page_len * width,
            8 * page_len * width,
            page_len * page_len * HEADS,
        ),
        name="attend",
    )(q, k, v, picks, hot_k, *before)


def attend_back_kernel(
    q_ref,
    k_ref,
    v_ref,
    picks_ref,
    hq_ref,
    hk_ref,
    hkt_ref,
    lse_ref,
    o_ref,
    do_ref,
    dq_ref,
    dk_ref,
    dv_ref,
    gb_ref,
):
    page_len = q_ref.shape[0]
    row = lax.broadcasted_iota(jnp.int32, (8, 128), 0)
    lane = lax.broadcasted_iota(jnp.int32, (8, 128), 1)
    chooser = (row == lane // 64).astype(bf16)
    for pair in range(q_ref.shape[1] // 128):
        lanes = slice(128 * pair, 128 * (pair + 1))
        k, v, do = k_ref[:, lanes], v_ref[:, lanes], do_ref[:, lanes]
        left = jnp.concatenate([k, hk_ref[0]], 1)
        k_turned = k.astype(f32).T.astype(bf16)
        overlap = do.astype(f32) * o_ref[:, lanes].astype(f32)
        high = overlap.astype(bf16)
        rest = (overlap - high.astype(f32)).astype(bf16)
        delta = nt(chooser, high) + nt(chooser, rest)
        delta = jnp.concatenate([delta[0:1], delta[1:2]], 1)
        lse = jnp.concatenate([lse_ref[0, pair, 0:1, :], lse_ref[0, pair, 1:2, :]], 1)
        queries, right = pair_right(q_ref[:, lanes], picks_ref[:, 256 * pair : 256 * (pair + 1)])
        do_heads = jnp.concatenate([head_lanes(do, head, 64) for head in range(2)], 0)
        probs = jnp.exp(nt(left, right) - lse)
        turn = (probs * (nt(v, do_heads) - delta)).astype(bf16)
        dv_ref[:, lanes] = nn(probs.astype(bf16), do_heads).astype(bf16)
        dk_ref[:, lanes] = nn(turn, queries).astype(bf16)
        parts, sums = [], []
        for head in range(2):
            both = nn(
                jnp.concatenate([k_turned[head * 64 : (head + 1) * 64], hkt_ref[0]], 0),
                turn[:, head * page_len : (head + 1) * page_len],
            )
            parts.append(both[:64])
            sums.append(both[64:])
        dq_ref[:, lanes] = (jnp.concatenate(parts, 0) * score_scale).T.astype(bf16)
        sums = jnp.concatenate(sums, 0)
        high = sums.astype(bf16)
        rest = (sums - high.astype(f32)).astype(bf16)
        grads = nn(jnp.concatenate([high, rest], 0), hq_ref[0])
        grads = grads[:128] + grads[128:]
        for head in range(2):
            gb_ref[0, 2 * pair + head] = grads[64 * head : 64 * (head + 1)]


def attend_back_call(pair, pairs, q, k, v, picks, hot_q, hot_k, hot_kt, lse_in, o, do):
    length, width = q.shape
    pages, page_len = hot_q.shape[0], hot_q.shape[1]
    rows, picks_spec, lse, hot = attend_specs(page_len, 0, pair // PAIRS)
    given = pl.BlockSpec((page_len, 128 * PAIRS), lambda p, h: (p, h))
    grad_bias = pl.BlockSpec((1, 2 * PAIRS, 64, 64), lambda p, h: (p, h, 0, 0))
    wide = jax.ShapeDtypeStruct((length, pairs * 128), bf16)
    return pl.pallas_call(
        attend_back_kernel,
        grid=(pages, pairs // PAIRS),
        in_specs=[
            rows,
            rows,
            rows,
            picks_spec,
            hot(page_len, 64),
            hot(page_len, 128),
            hot(64, page_len),
            lse,
            rows,
            rows,
        ],
        out_specs=[given, given, given, grad_bias],
        out_shape=[wide, wide, wide, jax.ShapeDtypeStruct((pages, 2 * pairs, 64, 64), f32)],
        compiler_params=params(),
        cost_estimate=cost(
            40 * length * page_len * pairs * 128,
            16 * length * pairs * 128,
            length * page_len * 2 * pairs,
            64,
        ),
        name="attend_back",
    )(q, k, v, picks, hot_q, hot_k, hot_kt, lse_in, o, do)


def put_rows(scratch, keep, send, at, me, relative, lanes=slice(None), source=slice(None)):
    if not relative:
        keep[pl.ds(at, scratch.shape[0]), lanes] = scratch[:, source].astype(bf16)
        return
    step = scratch.shape[0] // 16
    for place in range(16):
        owner = place ^ me
        rows = scratch[pl.ds(pl.multiple_of(owner * step, step), step), source].astype(bf16)
        target = send if place & 1 else keep
        low = at + (place >> 2) * step
        target[(place >> 1) & 1, low : low + step, lanes] = rows


def put_quarter(scratch, keep, send, at, me, relative):
    if not relative:
        keep[pl.ds(at, scratch.shape[0]), :] = scratch[...].astype(bf16)
        return
    step = scratch.shape[0] // 4
    for place in range(4):
        owner = place ^ (me & 3)
        rows = scratch[pl.ds(pl.multiple_of(owner * step, step), step), :].astype(bf16)
        target = send if place & 1 else keep
        target[place >> 1, at : at + step, :] = rows


def block_shapes(rows, width, relative):
    if relative:
        return (2, rows // 4, width), (2, rows // 4, width)
    return (rows, width), (16, 128)


def feed_kernel(me_ref, *rest, first, blocks, relative, tile):
    ins, rest = rest[: 12 if first else 6], rest[12 if first else 6 :]
    if first:
        x_ref, mixed_ref, keep_ref, wo_ref, bo_ref, gain_ref, shift_ref = ins[:7]
        cot_ref, up_ref, upb_ref, down_ref, old_ref = ins[7:]
        middle_ref, n2_ref = rest[:2]
        rest = rest[2:]
    else:
        n2_ref, cot_ref, up_ref, upb_ref, down_ref, old_ref = ins
    act_ref, gh_ref, small_ref, kept_ref, sent_ref, dw_ref = rest
    step = pl.program_id(0)
    length = cot_ref.shape[0]

    @pl.when(step == 0)
    def _():
        small_ref[...] = old_ref[...]
        if first:

            @pl.loop(0, length // 256)
            def _(i):
                at = pl.ds(pl.multiple_of(i * 256, 256), 256)
                branch = nn(mixed_ref[at, :], wo_ref[...]) + bo_ref[...]
                middle = x_ref[at, :].astype(f32) + branch
                middle_ref[at, :] = middle
                norm, _ = normal_rows(middle)
                n2_ref[at, :] = (norm * gain_ref[...] + shift_ref[...]).astype(bf16)
                small_ref[21:22, :] += jnp.sum(branch * branch * keep_ref[at, :], 0, keepdims=True)
                small_ref[23:24, :] += jnp.broadcast_to(
                    jnp.sum(keep_ref[at, :], 0, keepdims=True), (1, small_ref.shape[1])
                )

    row = (0 if first else blocks) + 16 + step

    for i in range(length // tile):
        at = slice(i * tile, (i + 1) * tile)
        hidden = nn(n2_ref[at, :], up_ref[...]) + upb_ref[...]
        slope = nt(cot_ref[at, :], down_ref[...])
        gate = 0.5 * (1.0 + lax.erf(hidden * 0.7071067811865476))
        bell = jnp.exp(hidden * hidden * -0.5) * 0.3989422804014327
        act_ref[at, :] = (hidden * gate).astype(bf16)
        gh = (slope * (gate + hidden * bell)).astype(bf16)
        gh_ref[at, :] = gh
        small_ref[pl.ds(row, 1), :] += jnp.sum(gh.astype(f32), 0, keepdims=True)

    me = me_ref[0]
    dw_ref[...] = tn(n2_ref[...], gh_ref[...])
    put_rows(dw_ref, kept_ref.at[0], sent_ref.at[0], 0, me, relative)
    dw_ref[...] = tn(act_ref[...], cot_ref[...])
    put_quarter(dw_ref, kept_ref.at[0], sent_ref.at[0], 192 if relative else 768, me, relative)


def feed_call(part, parts, me, given, cot, up, upb, down, small, relative):
    length, width = cot.shape
    first = part == 0
    blocks = up.shape[1] // width // parts
    start = part * blocks
    whole, row = full((length, width)), full((1, width))
    kept, sent = block_shapes(2 * width, width, relative)
    shape = jax.ShapeDtypeStruct
    if first:
        specs = [whole, whole, full((length, 1)), full((width, width)), row, row, row]
        outs = [whole, whole]
        shapes = [shape((length, width), f32), shape((length, width), bf16)]
    else:
        specs, outs, shapes = [whole], [], []
    columns = pl.BlockSpec((length, width), lambda j, *_: (0, j))

    def placed(dims):
        return pl.BlockSpec((1,) + dims, lambda j, *_: (j,) + (0,) * len(dims))

    grid_spec = pltpu.PrefetchScalarGridSpec(
        num_scalar_prefetch=1,
        grid=(blocks,),
        in_specs=specs
        + [
            whole,
            pl.BlockSpec((width, width), lambda j, *_: (0, j + start)),
            pl.BlockSpec((1, width), lambda j, *_: (0, j + start)),
            pl.BlockSpec((width, width), lambda j, *_: (j + start, 0)),
            full((SMALL, width)),
        ],
        out_specs=outs + [columns, columns, full((SMALL, width)), placed(kept), placed(sent)],
        scratch_shapes=[pltpu.VMEM((width, width), f32)],
    )
    return pl.pallas_call(
        functools.partial(
            feed_kernel, first=first, blocks=blocks, relative=relative, tile=512
        ),
        grid_spec=grid_spec,
        out_shape=shapes
        + [
            shape((length, blocks * width), bf16),
            shape((length, blocks * width), bf16),
            shape((SMALL, width), f32),
            shape((blocks,) + kept, bf16),
            shape((blocks,) + sent, bf16),
        ],
        compiler_params=params(),
        cost_estimate=cost(
            8 * length * width * width * blocks, 20 * length * width, 2 * length * width
        ),
        name="feed",
    )(me, *given, cot, up, upb, down, small)


def finish_kernel(
    me_ref,
    act_ref,
    gh_ref,
    act_two_ref,
    gh_two_ref,
    up_ref,
    down_ref,
    middle_ref,
    cot_ref,
    keep_ref,
    mixed_ref,
    wo_ref,
    gain_ref,
    downb_ref,
    old_ref,
    out_ref,
    gm_ref,
    gx_ref,
    small_ref,
    kept_ref,
    sent_ref,
    feed_ref,
    gn_ref,
    dw_ref,
    *,
    blocks,
    tile,
    relative,
):
    step = pl.program_id(0)

    @pl.when(step == 0)
    def _():
        small_ref[...] = old_ref[...]
        feed_ref[...] = nn(act_ref[...], down_ref[...])
        gn_ref[...] = nt(gh_ref[...], up_ref[...])

    @pl.when((step > 0) & (step < blocks // 2))
    def _():
        feed_ref[...] += nn(act_ref[...], down_ref[...])
        gn_ref[...] += nt(gh_ref[...], up_ref[...])

    @pl.when((step >= blocks // 2) & (step < blocks))
    def _():
        feed_ref[...] += nn(act_two_ref[...], down_ref[...])
        gn_ref[...] += nt(gh_two_ref[...], up_ref[...])

    @pl.when(step >= blocks)
    def _():
        lows = []
        for i in range(tile // 256):
            here = slice(i * 256, (i + 1) * 256)
            at = pl.ds(pl.multiple_of((step - blocks) * tile + i * 256, 256), 256)
            feed = feed_ref[at, :] + downb_ref[...]
            middle = middle_ref[here, :]
            output = middle + feed
            out_ref[here, :] = output.astype(bf16)
            weight = keep_ref[here, :]
            cot = cot_ref[here, :].astype(f32)
            norm, scale = normal_rows(middle)
            grad = gn_ref[at, :]
            inner = grad * gain_ref[...]
            grad_middle = cot + scale * (
                inner
                - jnp.mean(inner, -1, keepdims=True)
                - norm * jnp.mean(inner * norm, -1, keepdims=True)
            )
            gm_ref[here, :] = grad_middle
            low = grad_middle.astype(bf16)
            gx_ref[here, :] = nt(low, wo_ref[...]).astype(bf16)
            lows.append(low)
            small_ref[0:1, :] += jnp.sum(low.astype(f32), 0, keepdims=True)
            small_ref[1:2, :] += jnp.sum(grad * norm, 0, keepdims=True)
            small_ref[2:3, :] += jnp.sum(grad, 0, keepdims=True)
            small_ref[3:4, :] += jnp.sum(cot, 0, keepdims=True)
            small_ref[20:21, :] += jnp.sum(output * output * weight, 0, keepdims=True)
            small_ref[22:23, :] += jnp.sum(feed * feed * weight, 0, keepdims=True)
        part = tn(mixed_ref[...], jnp.concatenate(lows, 0))

        @pl.when(step == blocks)
        def _():
            dw_ref[...] = part

        @pl.when(step > blocks)
        def _():
            dw_ref[...] += part

    @pl.when(step == pl.num_programs(0) - 1)
    def _():
        put_rows(dw_ref, kept_ref, sent_ref, 0, me_ref[0], relative)


def finish_call(me, acts, up, down, middle, cot, keep, mixed, wo, gain, downb, small, relative):
    length, width = mixed.shape
    blocks = up.shape[1] // width
    half, end = blocks // 2, blocks - 1
    tile = 512
    whole, row = full((length, width)), full((1, width))
    kept, sent = block_shapes(width, width, relative)
    early = pl.BlockSpec((length, width), lambda j, *_: (0, jnp.minimum(j, half - 1)))
    late = pl.BlockSpec((length, width), lambda j, *_: (0, jnp.clip(j - half, 0, half - 1)))

    def tiled(lanes):
        return pl.BlockSpec((tile, lanes), lambda j, *_: (jnp.maximum(j - blocks, 0), 0))

    rows = tiled(width)
    shape = jax.ShapeDtypeStruct
    grid_spec = pltpu.PrefetchScalarGridSpec(
        num_scalar_prefetch=1,
        grid=(blocks + length // tile,),
        in_specs=[
            early,
            early,
            late,
            late,
            pl.BlockSpec((width, width), lambda j, *_: (0, jnp.minimum(j, end))),
            pl.BlockSpec((width, width), lambda j, *_: (jnp.minimum(j, end), 0)),
            rows,
            rows,
            tiled(1),
            rows,
            full((width, width)),
            row,
            row,
            full((SMALL, width)),
        ],
        out_specs=[rows, rows, rows, full((SMALL, width)), full(kept), full(sent)],
        scratch_shapes=[
            pltpu.VMEM((length, width), f32),
            pltpu.VMEM((length, width), f32),
            pltpu.VMEM((width, width), f32),
        ],
    )
    return pl.pallas_call(
        functools.partial(finish_kernel, blocks=blocks, tile=tile, relative=relative),
        grid_spec=grid_spec,
        out_shape=[
            shape((length, width), bf16),
            shape((length, width), f32),
            shape((length, width), bf16),
            shape((SMALL, width), f32),
            shape(kept, bf16),
            shape(sent, bf16),
        ],
        compiler_params=params(),
        cost_estimate=cost(4 * length * width * width, 24 * length * width),
        name="finish",
    )(me, *acts, up, down, middle, cot, keep, mixed, wo, gain, downb, small)


UNIT = 256


def units_of(part):
    each = part // UNIT
    places = [(grad, unit) for grad in range(3) for unit in range(each)]
    return [(grad, unit, i // 3, i % 3) for i, (grad, unit) in enumerate(places)]


def spread_small(small, total, chunk):
    sums = jnp.broadcast_to(jnp.sum(small[20:24, :], 1, keepdims=True), (4, chunk))
    for owner in range(16):
        lanes = slice(owner * chunk, (owner + 1) * chunk)
        block, start = owner // 4, (owner % 4) * 4 * chunk
        ups = [
            small[16 + block : 17 + block, start + i * chunk : start + (i + 1) * chunk]
            for i in range(4)
        ]
        piece = jnp.concatenate([small[0:16, lanes], *ups, sums], 0)
        high = piece.astype(bf16).astype(f32)
        whole = jnp.concatenate([high, piece - high], 0)
        for i in range(3):
            total[owner * 16 : (owner + 1) * 16, i * 128 : i * 128 + chunk] = whole[
                i * 16 : (i + 1) * 16
            ]


def weights_kernel(me_ref, n_ref, np_ref, *rest, start, count, relative):
    refs, rest = rest[: 3 * count], rest[3 * count :]
    last = count > 1
    old_ref, rest = rest[0], rest[1:]
    if last:
        x_ref, xp_ref, wq_ref, wp_ref, gq_ref, gp_ref = rest[:6]
        rest = rest[6:]
    small_ref, kept_ref, sent_ref, *totals = rest
    step = pl.program_id(0)
    grads = [ref[...] for ref in refs[-3:]]
    part = grads[0].shape[1]
    lanes = slice(start, start + part)
    sources = [n_ref[...], np_ref[...], np_ref[...]]

    @pl.when(step == 0)
    def _():
        small_ref[...] = old_ref[...]
        for total in totals[:3]:
            total[...] = jnp.zeros_like(total)

    for total, source, grad in zip(totals, sources, grads):
        total[...] += tn(source, grad)
    small_ref[4:5, lanes] += jnp.sum(grads[0].astype(f32), 0, keepdims=True)
    small_ref[7:8, lanes] += jnp.sum(grads[2].astype(f32), 0, keepdims=True)
    if last:
        dq, dk, dv = [jnp.concatenate([ref[...] for ref in refs[i::3]], 1) for i in range(3)]
        width = wq_ref.shape[0]
        far = nt(dk, wp_ref[0:2].reshape(width, width))
        far = far + nt(dv, wp_ref[2:4].reshape(width, width))
        own = nt(dq, wq_ref[...])
        gq_ref[...] = own
        gp_ref[...] = far.astype(bf16)
        norm, _ = normal_rows(x_ref[...].astype(f32))
        far_norm, _ = normal_rows(xp_ref[...].astype(f32))
        small_ref[5:6, :] += jnp.sum(own * norm, 0, keepdims=True)
        small_ref[6:7, :] += jnp.sum(own, 0, keepdims=True)
        small_ref[8:9, :] += jnp.sum(far * far_norm, 0, keepdims=True)
        small_ref[9:10, :] += jnp.sum(far, 0, keepdims=True)

    @pl.when(step == pl.num_programs(0) - 1)
    def _():
        me = me_ref[0]
        height = 192 if relative else 768
        for grad, unit, block, place in units_of(part):
            put_rows(
                totals[grad], kept_ref, sent_ref, block * height, me, relative,
                slice(place * UNIT, (place + 1) * UNIT), slice(unit * UNIT, (unit + 1) * UNIT),
            )
        if last and relative:
            spread = totals[3]
            spread[...] = jnp.zeros_like(spread)
            spread_small(small_ref[...], spread, small_ref.shape[1] // 16)
            put_rows(spread, kept_ref, sent_ref, height * part // UNIT, me, relative)


def weights_call(start, me, n, n_far, grads, small, more, relative):
    length, width = n.shape
    count = len(grads) // 3
    last = count > 1
    part = grads[-1].shape[1]
    tile = 512
    rows = pl.BlockSpec((tile, width), lambda i, *_: (i, 0))
    extra = last and relative
    kept, sent = block_shapes(width * part // UNIT + (256 if extra else 0), width, relative)
    shape = jax.ShapeDtypeStruct
    specs = [rows, rows]
    specs += [pl.BlockSpec((tile, grad.shape[1]), lambda i, *_: (i, 0)) for grad in grads]
    specs += [full((SMALL, width))]
    outs, shapes = [], []
    if last:
        specs += [rows, rows, full(more[2].shape), full(more[3].shape)]
        outs = [rows, rows]
        shapes = [shape((length, width), f32), shape((length, width), bf16)]
    grid_spec = pltpu.PrefetchScalarGridSpec(
        num_scalar_prefetch=1,
        grid=(length // tile,),
        in_specs=specs,
        out_specs=outs + [full((SMALL, width)), full(kept), full(sent)],
        scratch_shapes=[pltpu.VMEM((width, part), f32)] * 3
        + ([pltpu.VMEM((256, width), f32)] if extra else []),
    )
    return pl.pallas_call(
        functools.partial(weights_kernel, start=start, count=count, relative=relative),
        grid_spec=grid_spec,
        out_shape=shapes
        + [shape((SMALL, width), f32), shape(kept, bf16), shape(sent, bf16)],
        compiler_params=params(),
        cost_estimate=cost(6 * length * width * part, 24 * length * width),
        name="weights",
    )(me, n, n_far, *grads, small, *more)


def tokens_kernel(x_ref, gain_ref, gm_ref, gq_ref, gf_ref, out_ref):
    norm, scale = normal_rows(x_ref[...].astype(f32))
    inner = (gq_ref[...] + gf_ref[...].astype(f32)) * gain_ref[...]
    out_ref[...] = gm_ref[...] + scale * (
        inner
        - jnp.mean(inner, -1, keepdims=True)
        - norm * jnp.mean(inner * norm, -1, keepdims=True)
    )


def tokens_call(x, gain, gm, gq, gf):
    length, width = x.shape
    rows = pl.BlockSpec((256, width), lambda i: (i, 0))
    return pl.pallas_call(
        tokens_kernel,
        grid=(length // 256,),
        in_specs=[rows, full((1, width)), rows, rows, rows],
        out_specs=rows,
        out_shape=jax.ShapeDtypeStruct((length, width), f32),
        compiler_params=params(),
        cost_estimate=cost(20 * length * width, 16 * length * width),
        name="tokens",
    )(x, gain, gm, gq, gf)


def swapped(value, axis, mask):
    pairs = [(source, source ^ mask) for source in range(lax.axis_size(axis))]
    return lax.ppermute(value, axis, pairs)


def added(a, b, dtype=bf16):
    return (a.astype(f32) + b.astype(f32)).astype(dtype)


def together(kernel, inputs, moves=(), later=(), due=()):
    count = len(moves)
    moves = list(moves) + list(later)
    inputs, values = lax.optimization_barrier((inputs, [value for value, _, _ in moves]))
    came = [swapped(value, *way[1:]) for value, way in zip(values, moves)]
    results = kernel(*inputs) if kernel else []
    results, now, due = lax.optimization_barrier((results, came[:count], list(due)))
    return results, now, came[count:], due


def core_add(pair, came):
    return added(pair[0][0], came[0]), added(pair[0][1], came[1])


def z_parts(value):
    return value[0::2], value[1::2]


def everywhere(value):
    mask = 1
    while mask < lax.axis_size("dp"):
        value = value + swapped(value, "dp", mask)
        mask *= 2
    return value


def pick_stream(pair, stream):
    return jnp.where(stream == 0, pair[0], pair[1])


def box_onehots(seg_boxes, buckets):
    half = buckets // 2
    levels = jnp.arange(buckets, dtype=jnp.int32)
    centre_x = (seg_boxes[..., 0] + seg_boxes[..., 2]) // 2
    centre_y = (seg_boxes[..., 1] + seg_boxes[..., 3]) // 2
    step_x = (
        jnp.clip((centre_x[:, None, :] - centre_x[:, :, None]) // box_step, -half, half - 1) + half
    )
    step_y = (
        jnp.clip((centre_y[:, None, :] - centre_y[:, :, None]) // box_step, -half, half - 1) + half
    )
    return (
        (step_x[..., None] == levels).astype(jnp.float32),
        (step_y[..., None] == levels).astype(jnp.float32),
    )


def body(
    tokens,
    first_gain,
    first_shift,
    query_weight,
    query_bias,
    key_weight,
    value_weight,
    value_bias,
    out_weight,
    out_bias,
    second_gain,
    second_shift,
    up_weight,
    up_bias,
    down_weight,
    down_bias,
    box_table,
    segments,
    validity,
    seg_boxes,
    cotangent,
):
    stream = lax.axis_index("stream")
    me = lax.axis_index("dp")
    shards = lax.axis_size("dp")
    width = tokens.shape[2]
    hidden = up_weight.shape[2]
    pages, page_len = segments.shape[1], segments.shape[2]
    length = pages * page_len
    relative = shards == 16
    me_ref = me.reshape(1).astype(jnp.int32)
    x = tokens[0]

    own_seg = pick_stream(segments, stream)
    far_seg = pick_stream(segments, 1 - stream)
    own_keep = pick_stream(validity, stream)
    far_keep = pick_stream(validity, 1 - stream)
    levels = jnp.arange(64, dtype=jnp.int32)
    hot_q = (own_seg[:, :, None] == levels).astype(bf16)
    hot_kt = (far_seg[:, None, :] == levels[None, :, None]).astype(bf16)
    wide_levels = jnp.arange(128, dtype=jnp.int32)
    hot_k = jnp.where(
        wide_levels == 64,
        jnp.where(far_keep[:, :, None] > 0, 0.0, mask_fill),
        (far_seg[:, :, None] == wide_levels).astype(f32),
    ).astype(bf16)
    hot_x, hot_y = box_onehots(seg_boxes, BUCKETS)
    tables = box_table[0].reshape(2, HEADS, BUCKETS)
    seg_bias = (
        jnp.einsum("pabn,hn->phab", hot_x, tables[0], precision=precise_variant)
        + jnp.einsum("pabn,hn->phab", hot_y, tables[1], precision=precise_variant)
    ).astype(bf16)
    ones = (jnp.arange(64) == 0).astype(bf16)
    seg_bias = jnp.concatenate([seg_bias, jnp.broadcast_to(ones, seg_bias.shape)], -1)

    keep_column = own_keep.reshape(length, 1).astype(f32)
    blocks, chunk = hidden // width, width // shards
    cot = cotangent[0]
    Y, CORE, X, Z1, Z2 = ("stream", 1), ("dp", 1), ("dp", 2), ("dp", 4), ("dp", 8)

    low = me & 3
    half = width // 2

    def quarter(weight):
        return lax.dynamic_slice_in_dim(weight[0], (low & 1) * half, half, 0)

    piece = jnp.where(low < 2, quarter(key_weight), quarter(value_weight))
    vectors = jnp.concatenate([first_gain, first_shift, value_bias], 0)
    (normed, query), (piece, far_rows), _, _ = together(
        query_call,
        (x, first_gain, first_shift, query_weight[0], query_bias),
        [(piece, *Y), (vectors, *Y)],
    )
    page_x = [x[page * page_len : (page + 1) * page_len] for page in range(pages)]
    (picks, hot_q, hot_k), (x_piece, core_piece, came_x), _, _ = together(
        lambda bias, hot_q, hot_k: (picks_call(hot_q, bias), hot_q, hot_k),
        (seg_bias, hot_q, hot_k),
        [(piece, *X), (piece, *CORE), (page_x[0], *Y)],
    )
    far_pages = [came_x]
    pieces = [piece, core_piece, x_piece, swapped(x_piece, *CORE)]
    far, mixing = (), ()
    for page in range(pages):

        def page_step(came, pieces, far, mixing, page=page):
            far = pair_call(page, length, me_ref, came, far_rows, pieces, far)
            return far, attend_call(page, query, far[1], far[2], picks, hot_k, mixing)

        moves = [(page_x[page + 1], *Y)] if page + 1 < pages else []
        (result, mixing), came, _, _ = together(
            page_step, (far_pages[page], pieces, tuple(far), tuple(mixing)), moves
        )
        far = result[:4]
        if page == 0:
            pieces = [result[4]]
        far_pages += came
    far_normed, keys, value_rows, far_x = far
    far_weights = pieces[0]
    mixed, log_total = mixing

    small = jnp.zeros((SMALL, width), f32)

    def feed_first(mixed, small):
        return feed_call(
            0, 2, me_ref,
            (x, mixed, keep_column, out_weight[0], out_bias, second_gain, second_shift),
            cot, up_weight[0], up_bias, down_weight[0], small, relative,
        )

    def feed_second(n2, small):
        return feed_call(
            1, 2, me_ref, (n2,), cot, up_weight[0], up_bias, down_weight[0], small, relative
        )

    def finish(middle, small, *acts):
        return finish_call(
            me_ref, acts, up_weight[0], down_weight[0], middle, cot, keep_column, mixed,
            out_weight[0], second_gain, down_bias, small, relative,
        )

    def back_some(pair, pairs):
        def call(grad_mixed):
            return attend_back_call(
                pair, pairs, query, keys, value_rows, picks, hot_q, hot_k, hot_kt, log_total,
                mixed, grad_mixed,
            )

        return call

    def weights_some(start, more=()):
        def call(small, *grads):
            return weights_call(start, me_ref, normed, far_normed, grads, small, more, relative)

        return call

    back_through = (x, far_x, query_weight[0], far_weights)
    pairs = (4, width // 128 - 4)

    def table_row(grad_bias):
        return jnp.concatenate(
            [
                jnp.einsum("pabn,phba->hn", hot_x, grad_bias, precision=precise_variant),
                jnp.einsum("pabn,phba->hn", hot_y, grad_bias, precision=precise_variant),
            ],
            0,
        ).reshape(1, -1)

    if relative:

        def quads(*values):
            return jnp.concatenate([value.reshape(4, 48, -1) for value in values], 1)

        (middle, normed_two, act0, gh0, small, ka, sa), _, _, _ = together(
            feed_first, (mixed, small), []
        )
        (act1, gh1, small, kb, sb), (ca,), _, _ = together(
            feed_second, (normed_two, small), [(sa, *CORE)]
        )
        z_low, z_high = (me >> 2) & 1, me >> 3

        def of_four(kept, came):
            ups = [
                added(kept[j, :, :192], came[j, :, :192]).reshape(2, 4, 48, width)
                for j in range(2)
            ]
            return jnp.concatenate(ups, 2)

        def downs_of(kept, came, place):
            return added(kept[:, place, 192:], came[:, place, 192:])

        def downs(pair):
            one, other = pair
            keep, go = jnp.where(z_low, other, one), jnp.where(z_low, one, other)
            return keep, go

        ups = of_four(ka, ca)
        down_stay, down_go = downs_of(ka, ca, 0), downs_of(ka, ca, 1)
        up_stay, up_go = ups[:, 0::2], ups[:, 1::2]
        (output, grad_middle, grad_mixed, small, ko, so), (cb, x0, z0), _, _ = together(
            finish,
            (middle, small, act0, gh0, act1, gh1),
            [(sb, *CORE), (down_go, *X), (up_go, *Z1)],
        )
        up_half = added(up_stay, z0)
        one_keep, one_go = downs(added(down_stay, x0))
        m2, m3 = added(kb[0, 0], cb[0, 0]), added(kb[1, 0], cb[1, 0])
        t2, t3 = added(kb[0, 1], cb[0, 1]), added(kb[1, 1], cb[1, 1])
        (*grads, grad_bias), (co, z0), (x2, x3), _ = together(
            back_some(0, pairs[0]),
            (grad_mixed,),
            [(so, *CORE), (up_half[:, 1], *Z2)],
            [(t2, *X), (t3, *X)],
        )
        up_low = added(up_half[:, 0], z0)
        mo, to = core_add((ko,), co)
        (small, kq, sq), (z0,), (x0, xo), (x2, x3) = together(
            weights_some(0),
            (small, *grads),
            [(one_go, *Z1)],
            [(up_low[1], *X), (to, *X)],
            [x2, x3],
        )
        down_one = added(one_keep, z0)
        n2, n3 = added(m2, x2), added(m3, x3)
        two_keep, two_go = downs((n2[192:], n3[192:]))
        (*grads_two, grad_bias_two), (cq, z1), _, (x0, xo) = together(
            back_some(*pairs), (grad_mixed,), [(sq, *CORE), (two_go, *Z1)], [], [x0, xo]
        )
        up_low = added(up_low[0], x0, f32)
        no = added(mo, xo)
        down_two = added(two_keep, z1)
        down_stay = jnp.where(z_high, down_two, down_one)
        down_go = jnp.where(z_high, down_one, down_two)
        mq, tq = core_add((kq,), cq)
        two_keep, two_go = z_parts(quads(n2[:192], n3[:192], no))
        (own_grad, far_grad, small, kr, sr), (xq, z1, z3), _, _ = together(
            weights_some(pairs[0] * 128, back_through),
            (small, *grads, *grads_two),
            [(tq, *X), (two_go, *Z1), (down_go, *Z2)],
        )
        two_half, nq = added(two_keep, z1), added(mq, xq)
        q_keep, q_go = z_parts(quads(nq[:192], nq[192:]))
        _, (cr,), (came_grad,), _ = together(None, (), [(sr, *CORE)], [(far_grad, *Y)])
        mr, tr = core_add((kr,), cr)
        table = table_row(jnp.concatenate([grad_bias, grad_bias_two], 1))
        _, (xr, z1, came), (z2,), _ = together(
            None, (), [(tr, *X), (q_go, *Z1), (table, *CORE)], [(two_half[1], *Z2)]
        )
        table = table + came
        nr, q_half = added(mr, xr), added(q_keep, z1)
        r_keep, r_go = z_parts(
            jnp.concatenate([quads(nr[:192]), nr[192:].reshape(4, 16, width)], 1)
        )
        _, (z1, came), (z4,), _ = together(
            None, (), [(r_go, *Z1), (table, *X)], [(q_half[1], *Z2)], []
        )
        table = table + came
        r_half = added(r_keep, z1)
        _, (z1, came), _, (z2, z4, came_grad) = together(
            None, (), [(r_half[1], *Z2), (table, *Z1)], [], [z2, z4, came_grad]
        )
        table = table + came
        sum_down = added(down_stay, z3, f32)
        rest = added(two_half[0], z2, f32)
        first = added(q_half[0], z4, f32)
        last = added(r_half[0], z1, f32)
        sum_up = jnp.concatenate([up_low[:48], up_low[48:], rest[:48], rest[48:96]], 1)
        sum_out = rest[96:]
        spread = last[48:]
        pieces = [spread[:, 128 * i : 128 * i + chunk] for i in range(3)]
        pieces = jnp.concatenate(pieces, 0)
        lanes = pieces[:SMALL] + pieces[SMALL:]
        up_part = lanes[16:20].reshape(1, hidden // shards)
        totals = lanes[20:24, 0]

        def unit(values, place):
            block, lane = place // 3, place % 3
            return values[48 * block : 48 * block + 48, UNIT * lane : UNIT * (lane + 1)]

        sum_query, sum_keys, sum_values = [
            jnp.concatenate([unit(first, 2 * i), unit(first, 2 * i + 1), unit(last, i)], 1)
            for i in range(3)
        ]
        sum_pair = jnp.concatenate([sum_keys, sum_values], 0).astype(bf16)
        grad_tokens, (sum_pair, back, came), _, _ = together(
            tokens_call,
            (x, first_gain, grad_middle, own_grad, came_grad),
            [(sum_pair, *Y), (lanes[7:10], *Y), (table, *Z2)],
        )
        table = table + came
    else:
        middle, normed_two, act0, gh0, small, ka, _ = feed_first(mixed, small)
        act1, gh1, small, kb, _ = feed_second(normed_two, small)
        output, grad_middle, grad_mixed, small, out_kept, _ = finish(
            middle, small, act0, gh0, act1, gh1
        )
        *grads, grad_bias = back_some(0, pairs[0])(grad_mixed)
        small, kq, _ = weights_some(0)(small, *grads)
        *grads_two, grad_bias_two = back_some(*pairs)(grad_mixed)
        table = everywhere(table_row(jnp.concatenate([grad_bias, grad_bias_two], 1)))
        own_grad, far_grad, small, kr, _ = weights_some(pairs[0] * 128, back_through)(
            small, *grads, *grads_two
        )
        came_grad = swapped(far_grad, *Y)
        grad_tokens = tokens_call(x, first_gain, grad_middle, own_grad, came_grad)
        small = everywhere(small)

        def scattered(value):
            return lax.psum_scatter(value.astype(f32), "dp", scatter_dimension=0, tiled=True)

        def unit(values, place):
            block, lane = place // 3, place % 3
            return values[width * block : width * (block + 1), UNIT * lane : UNIT * (lane + 1)]

        ups = jnp.concatenate([ka, kb], 0)
        sum_up = scattered(jnp.concatenate([ups[j, :width] for j in range(blocks)], 1))
        sum_down = scattered(jnp.concatenate([ups[j, width:] for j in range(blocks)], 0))
        sum_out = scattered(out_kept)
        sum_query, sum_keys, sum_values = [
            scattered(
                jnp.concatenate([unit(kq, 2 * i), unit(kq, 2 * i + 1), unit(kr, i)], 1)
            )
            for i in range(3)
        ]
        sum_pair = jnp.concatenate([sum_keys, sum_values], 0).astype(bf16)
        lanes = lax.dynamic_slice_in_dim(small, me * chunk, chunk, 1)
        up_part = lax.dynamic_slice_in_dim(
            small[16 : 16 + blocks].reshape(1, hidden), me * (hidden // shards), hidden // shards, 1
        )
        totals = jnp.sum(small[20:24], 1)
        sum_pair, back = swapped((sum_pair, lanes[7:10]), *Y)

    sum_keys, sum_values = sum_pair[:chunk].astype(f32), sum_pair[chunk:].astype(f32)
    root_means = jnp.sqrt(totals[:3] / totals[3] + 1e-06).reshape(1, 3)

    return (
        output[None],
        grad_tokens[None],
        lanes[5:6] + back[1:2],
        lanes[6:7] + back[2:3],
        sum_query[None],
        lanes[4:5],
        sum_keys[None],
        sum_values[None],
        back[0:1],
        sum_out[None],
        lanes[0:1],
        lanes[1:2],
        lanes[2:3],
        sum_up[None],
        up_part,
        sum_down[None],
        lanes[3:4],
        lax.dynamic_slice_in_dim(table, me * chunk, chunk, 1),
        root_means,
    )


def solution(mesh):
    whole, split = P("stream", None), P("stream", "dp")
    cube, cut = P("stream", None, None), P("stream", "dp", None)
    pages = P(None, "dp", None)
    in_specs = (
        cut, whole, whole, cube, whole, cube, cube, whole, cube, whole, whole, whole,
        cube, whole, cube, whole, whole, pages, pages, P("dp", None, None), cut,
    )
    out_specs = (
        cut, cut, split, split, cut, split, cut, cut, split, cut, split, split, split,
        cut, split, cut, split, split, whole,
    )
    return jax.shard_map(body, mesh=mesh, in_specs=in_specs, out_specs=out_specs, check_vma=False)
```

```python
import functools

import jax
import jax.numpy as jnp
from jax import lax
from jax.experimental import pallas as pl
from jax.experimental.pallas import tpu as pltpu
from jax.sharding import PartitionSpec as P

HEADS = 12
BUCKETS = 32
SMALL = 24

score_scale = 0.125
norm_eps = 1e-05
mask_fill = -1000000000.0
box_step = 32
precise_variant = lax.Precision.HIGHEST
f32 = jnp.float32
bf16 = jnp.bfloat16


def nn(a, b):
    return lax.dot_general(a, b, (((1,), (0,)), ((), ())), preferred_element_type=f32)


def nt(a, b):
    return lax.dot_general(a, b, (((1,), (1,)), ((), ())), preferred_element_type=f32)


def tn(a, b):
    return lax.dot_general(a, b, (((0,), (0,)), ((), ())), preferred_element_type=f32)


def normal_rows(rows):
    centre = rows - jnp.mean(rows, -1, keepdims=True)
    spread = jnp.mean(centre * centre, -1, keepdims=True)
    scale = lax.rsqrt(spread + norm_eps)
    return centre * scale, scale


def params(mib=60):
    return pltpu.CompilerParams(vmem_limit_bytes=mib * 1024 * 1024)


def cost(flops, moved, trans=0, scale=1 / 64):
    return pl.CostEstimate(
        flops=int(flops * scale),
        bytes_accessed=int(moved * scale),
        transcendentals=int(trans * scale),
    )


def full(shape):
    zeros = (0,) * len(shape)
    return pl.BlockSpec(shape, lambda *_: zeros)


def query_kernel(x_ref, gain_ref, shift_ref, w_ref, b_ref, n_ref, q_ref):
    norm, _ = normal_rows(x_ref[...].astype(f32))
    low = (norm * gain_ref[...] + shift_ref[...]).astype(bf16)
    n_ref[...] = low
    query = (nn(low, w_ref[...]) + b_ref[...]).astype(bf16)
    q_ref[...] = (query.astype(f32) * score_scale).astype(bf16)


def query_call(x, gain, shift, weight, bias):
    length, width = x.shape
    tile = 256
    rows = pl.BlockSpec((tile, width), lambda i: (i, 0))
    return pl.pallas_call(
        query_kernel,
        grid=(length // tile,),
        in_specs=[rows, full((1, width)), full((1, width)), full(weight.shape), full((1, width))],
        out_specs=[rows, rows],
        out_shape=[jax.ShapeDtypeStruct(x.shape, bf16)] * 2,
        compiler_params=params(),
        cost_estimate=cost(2 * length * width * width, 6 * length * width + 2 * width * width),
        name="query",
    )(x, gain, shift, weight, bias)


def pair_kernel(me_ref, x_ref, rows_ref, *rest, count):
    pieces, (n_ref, k_ref, v_ref, copy_ref, w_ref) = rest[:count], rest[-5:]
    if count == 4:

        @pl.when(pl.program_id(0) == 0)
        def _():
            low = me_ref[0] & 3
            for place in range(4):
                w_ref[place ^ low] = pieces[place][...]

        weights = w_ref
    else:
        weights = pieces[0]
    half = weights.shape[1]
    copy_ref[...] = x_ref[...]
    norm, _ = normal_rows(x_ref[...].astype(f32))
    low = (norm * rows_ref[0:1, :] + rows_ref[1:2, :]).astype(bf16)
    n_ref[...] = low
    left, right = low[:, :half], low[:, half:]
    k_ref[...] = (nn(left, weights[0]) + nn(right, weights[1])).astype(bf16)
    v_ref[...] = (nn(left, weights[2]) + nn(right, weights[3]) + rows_ref[2:3, :]).astype(bf16)


def pair_call(page, length, me, x, rows, pieces, before):
    page_len, width = x.shape
    tile = 256
    first = page * page_len // tile
    placed = pl.BlockSpec((tile, width), lambda i, *_: (i + first, 0))
    left = pl.BlockSpec(memory_space=pl.ANY)
    weights = (4, width // 2, width)
    out_specs = [placed] * 4
    shapes = [jax.ShapeDtypeStruct((length, width), bf16)] * 4
    scratch = []
    if len(pieces) == 4:
        out_specs = out_specs + [full(weights)]
        shapes = shapes + [jax.ShapeDtypeStruct(weights, bf16)]
    else:
        scratch = [pltpu.VMEM((8, 128), f32)]
    grid_spec = pltpu.PrefetchScalarGridSpec(
        num_scalar_prefetch=1,
        grid=(page_len // tile,),
        in_specs=[
            pl.BlockSpec((tile, width), lambda i, *_: (i, 0)),
            full(rows.shape),
        ]
        + [full(piece.shape) for piece in pieces]
        + [left] * len(before),
        out_specs=out_specs,
        scratch_shapes=scratch,
    )
    return pl.pallas_call(
        functools.partial(pair_kernel, count=len(pieces)),
        grid_spec=grid_spec,
        out_shape=shapes,
        input_output_aliases={3 + len(pieces) + i: i for i in range(len(before))},
        compiler_params=params(),
        cost_estimate=cost(4 * page_len * width * width, 8 * page_len * width),
        name="pair",
    )(me, x, rows, *pieces, *before)


def head_lanes(value, head, head_dim):
    lane = lax.broadcasted_iota(jnp.int32, value.shape, 1)
    mine = (lane >= head * head_dim) & (lane < (head + 1) * head_dim)
    return jnp.where(mine, value, jnp.zeros_like(value))


def picks_kernel(hq_ref, bias_ref, out_ref):
    for pair in range(out_ref.shape[1] // 256):
        both = jnp.concatenate([bias_ref[0, 2 * pair], bias_ref[0, 2 * pair + 1]], 1)
        out_ref[:, 256 * pair : 256 * (pair + 1)] = nn(hq_ref[0], both).astype(bf16)


def picks_call(hot_q, bias):
    pages, page_len = hot_q.shape[0], hot_q.shape[1]
    return pl.pallas_call(
        picks_kernel,
        grid=(pages, 3),
        in_specs=[
            pl.BlockSpec((1, page_len, 64), lambda p, h: (p, 0, 0)),
            pl.BlockSpec((1, 4, 64, 128), lambda p, h: (p, h, 0, 0)),
        ],
        out_specs=pl.BlockSpec((page_len, 512), lambda p, h: (p, h)),
        out_shape=jax.ShapeDtypeStruct((pages * page_len, HEADS * 128), bf16),
        compiler_params=params(),
        cost_estimate=cost(2 * pages * page_len * HEADS * 128 * 64, pages * page_len * HEADS * 256),
        name="picks",
    )(hot_q, bias)


def pair_right(q, picks):
    heads = [head_lanes(q, head, 64) for head in range(2)]
    sides = [
        jnp.concatenate([heads[head], picks[:, 128 * head : 128 * (head + 1)]], 1)
        for head in range(2)
    ]
    return jnp.concatenate(heads, 0), jnp.concatenate(sides, 0)


def attend_kernel(q_ref, k_ref, v_ref, picks_ref, hk_ref, *rest):
    o_ref, lse_ref = rest[-2:]
    page_len = q_ref.shape[0]
    for pair in range(q_ref.shape[1] // 128):
        lanes = slice(128 * pair, 128 * (pair + 1))
        left = jnp.concatenate([k_ref[:, lanes], hk_ref[0]], 1)
        v_turned = v_ref[:, lanes].astype(f32).T.astype(bf16)
        _, right = pair_right(q_ref[:, lanes], picks_ref[:, 256 * pair : 256 * (pair + 1)])
        scores = nt(left, right)
        peak = jnp.max(scores, 0, keepdims=True)
        raised = jnp.exp(scores - peak)
        total = jnp.sum(raised, 0, keepdims=True)
        probs = (raised * (1.0 / total)).astype(bf16)
        lse = peak + jnp.log(total)
        parts = []
        for head in range(2):
            mine = slice(head * page_len, (head + 1) * page_len)
            parts.append(nn(v_turned[head * 64 : (head + 1) * 64], probs[:, mine]))
            lse_ref[0, pair, head : head + 1, :] = lse[:, mine]
        o_ref[:, lanes] = jnp.concatenate(parts, 0).T.astype(bf16)


PAIRS = 2


def attend_specs(page_len, page, first):
    rows = pl.BlockSpec((page_len, 128 * PAIRS), lambda p, h: (p + page, h + first))
    picks = pl.BlockSpec((page_len, 256 * PAIRS), lambda p, h: (p + page, h + first))
    lse = pl.BlockSpec((1, PAIRS, 2, page_len), lambda p, h: (p + page, h + first, 0, 0))

    def hot(*shape):
        return pl.BlockSpec((1,) + shape, lambda p, h: (p + page, 0, 0))

    return rows, picks, lse, hot


def attend_call(page, q, k, v, picks, hot_k, before):
    length, width = q.shape
    pages, page_len = hot_k.shape[0], hot_k.shape[1]
    rows, picks_spec, lse, hot = attend_specs(page_len, page, 0)
    left = pl.BlockSpec(memory_space=pl.ANY)
    return pl.pallas_call(
        attend_kernel,
        grid=(1, width // 128 // PAIRS),
        in_specs=[rows, rows, rows, picks_spec, hot(page_len, 128)] + [left] * len(before),
        out_specs=[rows, lse],
        out_shape=[
            jax.ShapeDtypeStruct((length, width), bf16),
            jax.ShapeDtypeStruct((pages, width // 128, 2, page_len), f32),
        ],
        input_output_aliases={5 + i: i for i in range(len(before))},
        compiler_params=params(),
        cost_estimate=cost(
            16 * page_len * page_len * width,
            8 * page_len * width,
            page_len * page_len * HEADS,
        ),
        name="attend",
    )(q, k, v, picks, hot_k, *before)


def attend_back_kernel(
    q_ref,
    k_ref,
    v_ref,
    picks_ref,
    hq_ref,
    hk_ref,
    hkt_ref,
    lse_ref,
    o_ref,
    do_ref,
    dq_ref,
    dk_ref,
    dv_ref,
    gb_ref,
):
    page_len = q_ref.shape[0]
    row = lax.broadcasted_iota(jnp.int32, (8, 128), 0)
    lane = lax.broadcasted_iota(jnp.int32, (8, 128), 1)
    chooser = (row == lane // 64).astype(bf16)
    for pair in range(q_ref.shape[1] // 128):
        lanes = slice(128 * pair, 128 * (pair + 1))
        k, v, do = k_ref[:, lanes], v_ref[:, lanes], do_ref[:, lanes]
        left = jnp.concatenate([k, hk_ref[0]], 1)
        k_turned = k.astype(f32).T.astype(bf16)
        overlap = do.astype(f32) * o_ref[:, lanes].astype(f32)
        high = overlap.astype(bf16)
        rest = (overlap - high.astype(f32)).astype(bf16)
        delta = nt(chooser, high) + nt(chooser, rest)
        delta = jnp.concatenate([delta[0:1], delta[1:2]], 1)
        lse = jnp.concatenate([lse_ref[0, pair, 0:1, :], lse_ref[0, pair, 1:2, :]], 1)
        queries, right = pair_right(q_ref[:, lanes], picks_ref[:, 256 * pair : 256 * (pair + 1)])
        do_heads = jnp.concatenate([head_lanes(do, head, 64) for head in range(2)], 0)
        probs = jnp.exp(nt(left, right) - lse)
        turn = (probs * (nt(v, do_heads) - delta)).astype(bf16)
        dv_ref[:, lanes] = nn(probs.astype(bf16), do_heads).astype(bf16)
        dk_ref[:, lanes] = nn(turn, queries).astype(bf16)
        parts, sums = [], []
        for head in range(2):
            both = nn(
                jnp.concatenate([k_turned[head * 64 : (head + 1) * 64], hkt_ref[0]], 0),
                turn[:, head * page_len : (head + 1) * page_len],
            )
            parts.append(both[:64])
            sums.append(both[64:])
        dq_ref[:, lanes] = (jnp.concatenate(parts, 0) * score_scale).T.astype(bf16)
        sums = jnp.concatenate(sums, 0)
        high = sums.astype(bf16)
        rest = (sums - high.astype(f32)).astype(bf16)
        grads = nn(jnp.concatenate([high, rest], 0), hq_ref[0])
        grads = grads[:128] + grads[128:]
        for head in range(2):
            gb_ref[0, 2 * pair + head] = grads[64 * head : 64 * (head + 1)]


def attend_back_call(pair, pairs, q, k, v, picks, hot_q, hot_k, hot_kt, lse_in, o, do):
    length, width = q.shape
    pages, page_len = hot_q.shape[0], hot_q.shape[1]
    rows, picks_spec, lse, hot = attend_specs(page_len, 0, pair // PAIRS)
    given = pl.BlockSpec((page_len, 128 * PAIRS), lambda p, h: (p, h))
    grad_bias = pl.BlockSpec((1, 2 * PAIRS, 64, 64), lambda p, h: (p, h, 0, 0))
    wide = jax.ShapeDtypeStruct((length, pairs * 128), bf16)
    return pl.pallas_call(
        attend_back_kernel,
        grid=(pages, pairs // PAIRS),
        in_specs=[
            rows,
            rows,
            rows,
            picks_spec,
            hot(page_len, 64),
            hot(page_len, 128),
            hot(64, page_len),
            lse,
            rows,
            rows,
        ],
        out_specs=[given, given, given, grad_bias],
        out_shape=[wide, wide, wide, jax.ShapeDtypeStruct((pages, 2 * pairs, 64, 64), f32)],
        compiler_params=params(),
        cost_estimate=cost(
            40 * length * page_len * pairs * 128,
            16 * length * pairs * 128,
            length * page_len * 2 * pairs,
            64,
        ),
        name="attend_back",
    )(q, k, v, picks, hot_q, hot_k, hot_kt, lse_in, o, do)


def put_rows(
    scratch, keep, send, me, relative, at, x_step, z_step, lanes=slice(None), source=slice(None)
):
    if not relative:
        keep[pl.ds(at, scratch.shape[0]), lanes] = scratch[:, source].astype(bf16)
        return
    step = scratch.shape[0] // 16
    for place in range(16):
        owner = place ^ me
        rows = scratch[pl.ds(pl.multiple_of(owner * step, step), step), source].astype(bf16)
        target = send if place & 1 else keep
        z = ((place >> 2) & 1) * 2 + (place >> 3)
        low = at + ((place >> 1) & 1) * x_step + z * z_step
        target[pl.ds(pl.multiple_of(low, 16), step), lanes] = rows


def put_quarter(scratch, keep, send, me, relative, at, x_step):
    if not relative:
        keep[pl.ds(at, scratch.shape[0]), :] = scratch[...].astype(bf16)
        return
    step = scratch.shape[0] // 4
    for place in range(4):
        owner = place ^ (me & 3)
        rows = scratch[pl.ds(pl.multiple_of(owner * step, step), step), :].astype(bf16)
        target = send if place & 1 else keep
        target[pl.ds(pl.multiple_of(at + (place >> 1) * x_step, 16), step), :] = rows


def block_shapes(rows, width, relative):
    if relative:
        return (rows // 2, width), (rows // 2, width)
    return (rows, width), (16, 128)


def feed_kernel(me_ref, *rest, first, blocks, relative, tile):
    ins, rest = rest[: 12 if first else 6], rest[12 if first else 8 :]
    if first:
        x_ref, mixed_ref, keep_ref, wo_ref, bo_ref, gain_ref, shift_ref = ins[:7]
        cot_ref, up_ref, upb_ref, down_ref, old_ref = ins[7:]
        middle_ref, n2_ref = rest[:2]
        rest = rest[2:]
    else:
        n2_ref, cot_ref, up_ref, upb_ref, down_ref, old_ref = ins
    act_ref, gh_ref, small_ref, kept_ref, sent_ref, dw_ref = rest[-6:]
    step = pl.program_id(0)
    length = cot_ref.shape[0]

    @pl.when(step == 0)
    def _():
        small_ref[...] = old_ref[...]
        if first:

            @pl.loop(0, length // 256)
            def _(i):
                at = pl.ds(pl.multiple_of(i * 256, 256), 256)
                branch = nn(mixed_ref[at, :], wo_ref[...]) + bo_ref[...]
                middle = x_ref[at, :].astype(f32) + branch
                middle_ref[at, :] = middle
                norm, _ = normal_rows(middle)
                n2_ref[at, :] = (norm * gain_ref[...] + shift_ref[...]).astype(bf16)
                small_ref[21:22, :] += jnp.sum(branch * branch * keep_ref[at, :], 0, keepdims=True)
                small_ref[23:24, :] += jnp.broadcast_to(
                    jnp.sum(keep_ref[at, :], 0, keepdims=True), (1, small_ref.shape[1])
                )

    row = (0 if first else blocks) + 16 + step

    @pl.loop(0, length // tile)
    def _(i):
        at = pl.ds(pl.multiple_of(i * tile, tile), tile)
        hidden = nn(n2_ref[at, :], up_ref[...]) + upb_ref[...]
        slope = nt(cot_ref[at, :], down_ref[...])
        gate = 0.5 * (1.0 + lax.erf(hidden * 0.7071067811865476))
        bell = jnp.exp(hidden * hidden * -0.5) * 0.3989422804014327
        act_ref[at, :] = (hidden * gate).astype(bf16)
        gh = (slope * (gate + hidden * bell)).astype(bf16)
        gh_ref[at, :] = gh
        small_ref[pl.ds(row, 1), :] += jnp.sum(gh.astype(f32), 0, keepdims=True)

    me = me_ref[0]
    width = dw_ref.shape[0]
    up_at, down_at = (step * 48, step * 192) if relative else (step * 2 * width, 0)
    dw_ref[...] = tn(n2_ref[...], gh_ref[...])
    up_steps = (96, 192) if first else (768, 96)
    put_rows(dw_ref, kept_ref, sent_ref, me, relative, up_at, *up_steps)
    dw_ref[...] = tn(act_ref[...], cot_ref[...])
    if relative:
        down_at = down_at + (768 if first else 384)
    else:
        down_at = up_at + width
    put_quarter(dw_ref, kept_ref, sent_ref, me, relative, down_at, 384 if first else 768)


def feed_call(part, parts, me, given, cot, up, upb, down, small, before, relative):
    length, width = cot.shape
    first = part == 0
    hidden = up.shape[1]
    blocks = hidden // width // parts
    start = part * blocks
    whole, row = full((length, width)), full((1, width))
    kept, sent = block_shapes(2 * width * blocks, width, relative)
    shape = jax.ShapeDtypeStruct
    if first:
        specs = [whole, whole, full((length, 1)), full((width, width)), row, row, row]
        outs = [whole, whole]
        shapes = [shape((length, width), f32), shape((length, width), bf16)]
    else:
        specs, outs, shapes = [whole], [], []
    columns = pl.BlockSpec((length, width), lambda j, *_: (0, j + start))
    left = pl.BlockSpec(memory_space=pl.ANY)
    grid_spec = pltpu.PrefetchScalarGridSpec(
        num_scalar_prefetch=1,
        grid=(blocks,),
        in_specs=specs
        + [
            whole,
            pl.BlockSpec((width, width), lambda j, *_: (0, j + start)),
            pl.BlockSpec((1, width), lambda j, *_: (0, j + start)),
            pl.BlockSpec((width, width), lambda j, *_: (j + start, 0)),
            full((SMALL, width)),
        ]
        + [left] * len(before),
        out_specs=outs + [columns, columns, full((SMALL, width)), full(kept), full(sent)],
        scratch_shapes=[pltpu.VMEM((width, width), f32)],
    )
    count = 1 + len(specs) + 5
    return pl.pallas_call(
        functools.partial(
            feed_kernel, first=first, blocks=blocks, relative=relative, tile=512
        ),
        grid_spec=grid_spec,
        out_shape=shapes
        + [
            shape((length, hidden), bf16),
            shape((length, hidden), bf16),
            shape((SMALL, width), f32),
            shape(kept, bf16),
            shape(sent, bf16),
        ],
        input_output_aliases={count + i: i for i in range(len(before))},
        compiler_params=params(),
        cost_estimate=cost(
            8 * length * width * width * blocks, 20 * length * width, 2 * length * width
        ),
        name="feed",
    )(me, *given, cot, up, upb, down, small, *before)


def finish_kernel(
    me_ref,
    act_ref,
    gh_ref,
    up_ref,
    down_ref,
    middle_ref,
    cot_ref,
    keep_ref,
    mixed_ref,
    wo_ref,
    gain_ref,
    downb_ref,
    old_ref,
    out_ref,
    gm_ref,
    gx_ref,
    small_ref,
    kept_ref,
    sent_ref,
    feed_ref,
    gn_ref,
    dw_ref,
    *,
    blocks,
    tile,
    relative,
):
    step = pl.program_id(0)

    @pl.when(step == 0)
    def _():
        small_ref[...] = old_ref[...]
        feed_ref[...] = jnp.zeros_like(feed_ref)
        gn_ref[...] = jnp.zeros_like(gn_ref)

    @pl.when(step < blocks - 1)
    def _():
        feed_ref[...] += nn(act_ref[...], down_ref[...])
        gn_ref[...] += nt(gh_ref[...], up_ref[...])

    @pl.when(step >= blocks - 1)
    def _():
        lows = []
        for i in range(tile // 256):
            here = slice(i * 256, (i + 1) * 256)
            at = pl.ds(pl.multiple_of((step - blocks + 1) * tile + i * 256, 256), 256)
            feed = feed_ref[at, :] + nn(act_ref[at, :], down_ref[...]) + downb_ref[...]
            middle = middle_ref[here, :]
            output = middle + feed
            out_ref[here, :] = output.astype(bf16)
            weight = keep_ref[here, :]
            cot = cot_ref[here, :].astype(f32)
            norm, scale = normal_rows(middle)
            grad = gn_ref[at, :] + nt(gh_ref[at, :], up_ref[...])
            inner = grad * gain_ref[...]
            grad_middle = cot + scale * (
                inner
                - jnp.mean(inner, -1, keepdims=True)
                - norm * jnp.mean(inner * norm, -1, keepdims=True)
            )
            gm_ref[here, :] = grad_middle
            low = grad_middle.astype(bf16)
            gx_ref[here, :] = nt(low, wo_ref[...]).astype(bf16)
            lows.append(low)
            small_ref[0:1, :] += jnp.sum(low.astype(f32), 0, keepdims=True)
            small_ref[1:2, :] += jnp.sum(grad * norm, 0, keepdims=True)
            small_ref[2:3, :] += jnp.sum(grad, 0, keepdims=True)
            small_ref[3:4, :] += jnp.sum(cot, 0, keepdims=True)
            small_ref[20:21, :] += jnp.sum(output * output * weight, 0, keepdims=True)
            small_ref[22:23, :] += jnp.sum(feed * feed * weight, 0, keepdims=True)
        part = tn(mixed_ref[...], jnp.concatenate(lows, 0))

        @pl.when(step == blocks - 1)
        def _():
            dw_ref[...] = part

        @pl.when(step > blocks - 1)
        def _():
            dw_ref[...] += part

    @pl.when(step == pl.num_programs(0) - 1)
    def _():
        put_rows(dw_ref, kept_ref, sent_ref, me_ref[0], relative, 0, 192, 48)


def finish_call(me, acts, up, down, middle, cot, keep, mixed, wo, gain, downb, small, relative):
    length, width = mixed.shape
    blocks = up.shape[1] // width
    end = blocks - 1
    tile = 512
    whole, row = full((length, width)), full((1, width))
    kept, sent = block_shapes(width, width, relative)
    columns = pl.BlockSpec((length, width), lambda j, *_: (0, jnp.minimum(j, end)))

    def tiled(lanes):
        return pl.BlockSpec((tile, lanes), lambda j, *_: (jnp.maximum(j - end, 0), 0))

    rows = tiled(width)
    shape = jax.ShapeDtypeStruct
    grid_spec = pltpu.PrefetchScalarGridSpec(
        num_scalar_prefetch=1,
        grid=(end + length // tile,),
        in_specs=[
            columns,
            columns,
            pl.BlockSpec((width, width), lambda j, *_: (0, jnp.minimum(j, end))),
            pl.BlockSpec((width, width), lambda j, *_: (jnp.minimum(j, end), 0)),
            rows,
            rows,
            tiled(1),
            rows,
            full((width, width)),
            row,
            row,
            full((SMALL, width)),
        ],
        out_specs=[rows, rows, rows, full((SMALL, width)), full(kept), full(sent)],
        scratch_shapes=[
            pltpu.VMEM((length, width), f32),
            pltpu.VMEM((length, width), f32),
            pltpu.VMEM((width, width), f32),
        ],
    )
    return pl.pallas_call(
        functools.partial(finish_kernel, blocks=blocks, tile=tile, relative=relative),
        grid_spec=grid_spec,
        out_shape=[
            shape((length, width), bf16),
            shape((length, width), f32),
            shape((length, width), bf16),
            shape((SMALL, width), f32),
            shape(kept, bf16),
            shape(sent, bf16),
        ],
        compiler_params=params(),
        cost_estimate=cost(4 * length * width * width, 24 * length * width),
        name="finish",
    )(me, *acts, up, down, middle, cot, keep, mixed, wo, gain, downb, small)


UNIT = 256


def units_of(part):
    each = part // UNIT
    places = [(grad, unit) for grad in range(3) for unit in range(each)]
    return [(grad, unit, i // 3, i % 3) for i, (grad, unit) in enumerate(places)]


def spread_small(small, total, chunk):
    sums = jnp.broadcast_to(jnp.sum(small[20:24, :], 1, keepdims=True), (4, chunk))
    for owner in range(16):
        lanes = slice(owner * chunk, (owner + 1) * chunk)
        block, start = owner // 4, (owner % 4) * 4 * chunk
        ups = [
            small[16 + block : 17 + block, start + i * chunk : start + (i + 1) * chunk]
            for i in range(4)
        ]
        piece = jnp.concatenate([small[0:16, lanes], *ups, sums], 0)
        high = piece.astype(bf16).astype(f32)
        whole = jnp.concatenate([high, piece - high], 0)
        for i in range(3):
            total[owner * 16 : (owner + 1) * 16, i * 128 : i * 128 + chunk] = whole[
                i * 16 : (i + 1) * 16
            ]


def weights_kernel(me_ref, n_ref, np_ref, *rest, start, count, relative):
    refs, rest = rest[: 3 * count], rest[3 * count :]
    last = count > 1
    old_ref, rest = rest[0], rest[1:]
    if last:
        x_ref, xp_ref, wq_ref, wp_ref, gq_ref, gp_ref = rest[:6]
        rest = rest[6:]
    small_ref, kept_ref, sent_ref, *totals = rest
    step = pl.program_id(0)
    grads = [ref[...] for ref in refs[-3:]]
    part = grads[0].shape[1]
    lanes = slice(start, start + part)
    sources = [n_ref[...], np_ref[...], np_ref[...]]

    @pl.when(step == 0)
    def _():
        small_ref[...] = old_ref[...]
        for total in totals[:3]:
            total[...] = jnp.zeros_like(total)

    for total, source, grad in zip(totals, sources, grads):
        total[...] += tn(source, grad)
    small_ref[4:5, lanes] += jnp.sum(grads[0].astype(f32), 0, keepdims=True)
    small_ref[7:8, lanes] += jnp.sum(grads[2].astype(f32), 0, keepdims=True)
    if last:
        dq, dk, dv = [jnp.concatenate([ref[...] for ref in refs[i::3]], 1) for i in range(3)]
        width = wq_ref.shape[0]
        far = nt(dk, wp_ref[0:2].reshape(width, width))
        far = far + nt(dv, wp_ref[2:4].reshape(width, width))
        own = nt(dq, wq_ref[...])
        gq_ref[...] = own
        gp_ref[...] = far.astype(bf16)
        norm, _ = normal_rows(x_ref[...].astype(f32))
        far_norm, _ = normal_rows(xp_ref[...].astype(f32))
        small_ref[5:6, :] += jnp.sum(own * norm, 0, keepdims=True)
        small_ref[6:7, :] += jnp.sum(own, 0, keepdims=True)
        small_ref[8:9, :] += jnp.sum(far * far_norm, 0, keepdims=True)
        small_ref[9:10, :] += jnp.sum(far, 0, keepdims=True)

    @pl.when(step == pl.num_programs(0) - 1)
    def _():
        me = me_ref[0]
        z_step = 64 if last else 48 * part // UNIT
        for grad, unit, block, place in units_of(part):
            put_rows(
                totals[grad], kept_ref, sent_ref, me, relative,
                48 * block if relative else 768 * block, 4 * z_step, z_step,
                slice(place * UNIT, (place + 1) * UNIT), slice(unit * UNIT, (unit + 1) * UNIT),
            )
        if last and relative:
            spread = totals[3]
            spread[...] = jnp.zeros_like(spread)
            spread_small(small_ref[...], spread, small_ref.shape[1] // 16)
            put_rows(spread, kept_ref, sent_ref, me, relative, 48, 4 * z_step, z_step)


def weights_call(start, me, n, n_far, grads, small, more, relative):
    length, width = n.shape
    count = len(grads) // 3
    last = count > 1
    part = grads[-1].shape[1]
    tile = 512
    rows = pl.BlockSpec((tile, width), lambda i, *_: (i, 0))
    extra = last and relative
    kept, sent = block_shapes(width * part // UNIT + (256 if extra else 0), width, relative)
    shape = jax.ShapeDtypeStruct
    specs = [rows, rows]
    specs += [pl.BlockSpec((tile, grad.shape[1]), lambda i, *_: (i, 0)) for grad in grads]
    specs += [full((SMALL, width))]
    outs, shapes = [], []
    if last:
        specs += [rows, rows, full(more[2].shape), full(more[3].shape)]
        outs = [rows, rows]
        shapes = [shape((length, width), f32), shape((length, width), bf16)]
    grid_spec = pltpu.PrefetchScalarGridSpec(
        num_scalar_prefetch=1,
        grid=(length // tile,),
        in_specs=specs,
        out_specs=outs + [full((SMALL, width)), full(kept), full(sent)],
        scratch_shapes=[pltpu.VMEM((width, part), f32)] * 3
        + ([pltpu.VMEM((256, width), f32)] if extra else []),
    )
    return pl.pallas_call(
        functools.partial(weights_kernel, start=start, count=count, relative=relative),
        grid_spec=grid_spec,
        out_shape=shapes
        + [shape((SMALL, width), f32), shape(kept, bf16), shape(sent, bf16)],
        compiler_params=params(),
        cost_estimate=cost(6 * length * width * part, 24 * length * width),
        name="weights",
    )(me, n, n_far, *grads, small, *more)


def tokens_kernel(x_ref, gain_ref, gm_ref, gq_ref, gf_ref, out_ref):
    norm, scale = normal_rows(x_ref[...].astype(f32))
    inner = (gq_ref[...] + gf_ref[...].astype(f32)) * gain_ref[...]
    out_ref[...] = gm_ref[...] + scale * (
        inner
        - jnp.mean(inner, -1, keepdims=True)
        - norm * jnp.mean(inner * norm, -1, keepdims=True)
    )


def tokens_call(x, gain, gm, gq, gf):
    length, width = x.shape
    rows = pl.BlockSpec((256, width), lambda i: (i, 0))
    return pl.pallas_call(
        tokens_kernel,
        grid=(length // 256,),
        in_specs=[rows, full((1, width)), rows, rows, rows],
        out_specs=rows,
        out_shape=jax.ShapeDtypeStruct((length, width), f32),
        compiler_params=params(),
        cost_estimate=cost(20 * length * width, 16 * length * width),
        name="tokens",
    )(x, gain, gm, gq, gf)


def swapped(value, axis, mask):
    pairs = [(source, source ^ mask) for source in range(lax.axis_size(axis))]
    return lax.ppermute(value, axis, pairs)


def added(a, b, dtype=bf16):
    return (a.astype(f32) + b.astype(f32)).astype(dtype)


def together(kernel, inputs, moves=(), later=(), due=()):
    count = len(moves)
    moves = list(moves) + list(later)
    inputs, values = lax.optimization_barrier((inputs, [value for value, _, _ in moves]))
    came = [swapped(value, *way[1:]) for value, way in zip(values, moves)]
    results = kernel(*inputs) if kernel else []
    results, now, due = lax.optimization_barrier((results, came[:count], list(due)))
    return results, now, came[count:], due


def total(*values):
    return functools.reduce(jnp.add, [value.astype(f32) for value in values])


def quads(*values):
    values = [value.reshape(4, -1, value.shape[-1]) for value in values]
    return jnp.concatenate(values, 1).reshape(-1, values[0].shape[-1])


def everywhere(value):
    mask = 1
    while mask < lax.axis_size("dp"):
        value = value + swapped(value, "dp", mask)
        mask *= 2
    return value


def pick_stream(pair, stream):
    return jnp.where(stream == 0, pair[0], pair[1])


def box_onehots(seg_boxes, buckets):
    half = buckets // 2
    levels = jnp.arange(buckets, dtype=jnp.int32)
    centre_x = (seg_boxes[..., 0] + seg_boxes[..., 2]) // 2
    centre_y = (seg_boxes[..., 1] + seg_boxes[..., 3]) // 2
    step_x = (
        jnp.clip((centre_x[:, None, :] - centre_x[:, :, None]) // box_step, -half, half - 1) + half
    )
    step_y = (
        jnp.clip((centre_y[:, None, :] - centre_y[:, :, None]) // box_step, -half, half - 1) + half
    )
    return (
        (step_x[..., None] == levels).astype(jnp.float32),
        (step_y[..., None] == levels).astype(jnp.float32),
    )


def body(
    tokens,
    first_gain,
    first_shift,
    query_weight,
    query_bias,
    key_weight,
    value_weight,
    value_bias,
    out_weight,
    out_bias,
    second_gain,
    second_shift,
    up_weight,
    up_bias,
    down_weight,
    down_bias,
    box_table,
    segments,
    validity,
    seg_boxes,
    cotangent,
):
    stream = lax.axis_index("stream")
    me = lax.axis_index("dp")
    shards = lax.axis_size("dp")
    width = tokens.shape[2]
    hidden = up_weight.shape[2]
    pages, page_len = segments.shape[1], segments.shape[2]
    length = pages * page_len
    relative = shards == 16
    me_ref = me.reshape(1).astype(jnp.int32)
    x = tokens[0]

    own_seg = pick_stream(segments, stream)
    far_seg = pick_stream(segments, 1 - stream)
    own_keep = pick_stream(validity, stream)
    far_keep = pick_stream(validity, 1 - stream)
    levels = jnp.arange(64, dtype=jnp.int32)
    hot_q = (own_seg[:, :, None] == levels).astype(bf16)
    hot_kt = (far_seg[:, None, :] == levels[None, :, None]).astype(bf16)
    wide_levels = jnp.arange(128, dtype=jnp.int32)
    hot_k = jnp.where(
        wide_levels == 64,
        jnp.where(far_keep[:, :, None] > 0, 0.0, mask_fill),
        (far_seg[:, :, None] == wide_levels).astype(f32),
    ).astype(bf16)
    hot_x, hot_y = box_onehots(seg_boxes, BUCKETS)
    tables = box_table[0].reshape(2, HEADS, BUCKETS)
    seg_bias = (
        jnp.einsum("pabn,hn->phab", hot_x, tables[0], precision=precise_variant)
        + jnp.einsum("pabn,hn->phab", hot_y, tables[1], precision=precise_variant)
    ).astype(bf16)
    ones = (jnp.arange(64) == 0).astype(bf16)
    seg_bias = jnp.concatenate([seg_bias, jnp.broadcast_to(ones, seg_bias.shape)], -1)

    keep_column = own_keep.reshape(length, 1).astype(f32)
    blocks, chunk = hidden // width, width // shards
    cot = cotangent[0]
    Y, CORE, X, Z1, Z2 = ("stream", 1), ("dp", 1), ("dp", 2), ("dp", 4), ("dp", 8)

    low = me & 3
    half = width // 2

    def quarter(weight):
        return lax.dynamic_slice_in_dim(weight[0], (low & 1) * half, half, 0)

    piece = jnp.where(low < 2, quarter(key_weight), quarter(value_weight))
    vectors = jnp.concatenate([first_gain, first_shift, value_bias], 0)
    (normed, query), (piece, far_rows), _, _ = together(
        query_call,
        (x, first_gain, first_shift, query_weight[0], query_bias),
        [(piece, *Y), (vectors, *Y)],
    )
    page_x = [x[page * page_len : (page + 1) * page_len] for page in range(pages)]
    (picks, hot_q, hot_k), (x_piece, core_piece, came_x), _, _ = together(
        lambda bias, hot_q, hot_k: (picks_call(hot_q, bias), hot_q, hot_k),
        (seg_bias, hot_q, hot_k),
        [(piece, *X), (piece, *CORE), (page_x[0], *Y)],
    )
    far_pages = [came_x]
    pieces = [piece, core_piece, x_piece, swapped(x_piece, *CORE)]
    far, mixing = (), ()
    for page in range(pages):

        def page_step(came, pieces, far, mixing, page=page):
            far = pair_call(page, length, me_ref, came, far_rows, pieces, far)
            return far, attend_call(page, query, far[1], far[2], picks, hot_k, mixing)

        moves = [(page_x[page + 1], *Y)] if page + 1 < pages else []
        (result, mixing), came, _, _ = together(
            page_step, (far_pages[page], pieces, tuple(far), tuple(mixing)), moves
        )
        far = result[:4]
        if page == 0:
            pieces = [result[4]]
        far_pages += came
    far_normed, keys, value_rows, far_x = far
    far_weights = pieces[0]
    mixed, log_total = mixing

    small = jnp.zeros((SMALL, width), f32)

    def feed_first(mixed, small):
        return feed_call(
            0, 2, me_ref,
            (x, mixed, keep_column, out_weight[0], out_bias, second_gain, second_shift),
            cot, up_weight[0], up_bias, down_weight[0], small, (), relative,
        )

    def feed_second(n2, small, *acts):
        return feed_call(
            1, 2, me_ref, (n2,), cot, up_weight[0], up_bias, down_weight[0], small, acts, relative
        )

    def finish(middle, small, *acts):
        return finish_call(
            me_ref, acts, up_weight[0], down_weight[0], middle, cot, keep_column, mixed,
            out_weight[0], second_gain, down_bias, small, relative,
        )

    def back_some(pair, pairs):
        def call(grad_mixed):
            return attend_back_call(
                pair, pairs, query, keys, value_rows, picks, hot_q, hot_k, hot_kt, log_total,
                mixed, grad_mixed,
            )

        return call

    def weights_some(start, more=()):
        def call(small, *grads):
            return weights_call(start, me_ref, normed, far_normed, grads, small, more, relative)

        return call

    back_through = (x, far_x, query_weight[0], far_weights)
    pairs = (4, width // 128 - 4)

    def table_row(grad_bias):
        return jnp.concatenate(
            [
                jnp.einsum("pabn,phba->hn", hot_x, grad_bias, precision=precise_variant),
                jnp.einsum("pabn,phba->hn", hot_y, grad_bias, precision=precise_variant),
            ],
            0,
        ).reshape(1, -1)

    if relative:
        z_low, z_high = (me >> 2) & 1, me >> 3

        def downs(pair):
            one, other = pair[:192], pair[192:]
            return jnp.where(z_low, other, one), jnp.where(z_low, one, other)

        (middle, normed_two, act, gh, small, ka, sa), _, _, _ = together(
            feed_first, (mixed, small)
        )
        (act, gh, small, kb, sb), (ca,), _, _ = together(
            feed_second, (normed_two, small, act, gh), [(sa, *CORE)]
        )
        up_go, down_go = added(ka[384:768], ca[384:768]), added(ka[1152:], ca[1152:])
        (output, grad_middle, grad_mixed, small, ko, so), (cb, x0, z0), _, _ = together(
            finish,
            (middle, small, act, gh),
            [(sb, *CORE), (down_go, *X), (up_go, *Z1)],
        )
        up_go = total(ka[192:384], ca[192:384], z0[192:]).astype(bf16)
        up_stay = total(ka[:192], ca[:192], z0[:192])
        go = added(kb[768:], cb[768:])
        (*grads, grad_bias), (co, z0), (x2,), _ = together(
            back_some(0, pairs[0]), (grad_mixed,), [(so, *CORE), (up_go, *Z2)], [(go, *X)]
        )
        one = total(ka[768:1152], ca[768:1152], x0).astype(bf16)
        one_keep, one_go = downs(one)
        up_low = total(up_stay, z0)
        go = jnp.concatenate([up_low[96:].astype(bf16), added(ko[192:], co[192:])], 0)
        (small, kq, sq), (z0,), (xo,), (x2,) = together(
            weights_some(0), (small, *grads), [(one_go, *Z1)], [(go, *X)], [x2]
        )
        down_one = added(one_keep, z0)
        two = total(kb[:768], cb[:768], x2).astype(bf16)
        two_keep, two_go = downs(two[384:])
        (*grads_two, grad_bias_two), (cq, z1), _, (xo,) = together(
            back_some(*pairs), (grad_mixed,), [(sq, *CORE), (two_go, *Z1)], [], [xo]
        )
        down_two = added(two_keep, z1)
        down_stay = jnp.where(z_high, down_two, down_one)
        down_go = jnp.where(z_high, down_one, down_two)
        go = added(kq[384:], cq[384:])
        rest = quads(two[:384], total(ko[:192], co[:192], xo[96:]).astype(bf16))
        (own_grad, far_grad, small, kr, sr), (xq, z1, z3), _, _ = together(
            weights_some(pairs[0] * 128, back_through),
            (small, *grads, *grads_two),
            [(go, *X), (rest[288:], *Z1), (down_go, *Z2)],
        )
        _, (cr,), (came_grad,), _ = together(None, (), [(sr, *CORE)], [(far_grad, *Y)])
        go = added(kr[256:], cr[256:])
        rest_go = added(rest[144:288], z1[144:])
        group_go = total(kq[192:384], cq[192:384], xq[192:]).astype(bf16)
        z4, z2 = swapped(group_go, *Z1), swapped(rest_go, *Z2)
        table = table_row(jnp.concatenate([grad_bias, grad_bias_two], 1))
        _, (xr,), _, (z4, table) = together(None, (), [(go, *X)], [], [z4, table])
        r_go = total(kr[128:256], cr[128:256], xr[128:]).astype(bf16)
        group_go = total(kq[96:192], cq[96:192], xq[96:192], z4[96:]).astype(bf16)
        z5 = swapped(group_go, *Z2)
        _, (z1r, came), _, _ = together(None, (), [(r_go, *Z1), (table, *CORE)])
        table = table + came
        r_go = total(kr[64:128], cr[64:128], xr[64:128], z1r[64:]).astype(bf16)
        _, (z2r, came), _, (z2, z5, came_grad) = together(
            None, (), [(r_go, *Z2), (table, *X)], [], [z2, z5, came_grad]
        )
        table = table + came
        up_low = total(up_low[:96], xo[:96])
        sum_down = total(down_stay, z3)
        rest = total(rest[:144], z1[:144], z2)
        first = total(kq[:96], cq[:96], xq[:96], z4[:96], z5)
        last = total(kr[:64], cr[:64], xr[:64], z1r[:64], z2r)
        sum_up = jnp.concatenate([up_low[:48], up_low[48:], rest[:48], rest[48:96]], 1)
        sum_out = rest[96:]
        spread = last[48:]
        pieces = [spread[:, 128 * i : 128 * i + chunk] for i in range(3)]
        pieces = jnp.concatenate(pieces, 0)
        lanes = pieces[:SMALL] + pieces[SMALL:]
        up_part = lanes[16:20].reshape(1, hidden // shards)
        totals = lanes[20:24, 0]

        def unit(values, place):
            block, lane = place // 3, place % 3
            return values[48 * block : 48 * block + 48, UNIT * lane : UNIT * (lane + 1)]

        sum_query, sum_keys, sum_values = [
            jnp.concatenate([unit(first, 2 * i), unit(first, 2 * i + 1), unit(last, i)], 1)
            for i in range(3)
        ]
        sum_pair = jnp.concatenate([sum_keys, sum_values], 0).astype(bf16)
        root_means = jnp.sqrt(totals[:3] / totals[3] + 1e-06).reshape(1, 3)

        def ending(*tokens_given):
            return tokens_call(*tokens_given), up_part, root_means, sum_query, sum_up, sum_out

        ended, (sum_pair, back, came), _, _ = together(
            ending,
            (x, first_gain, grad_middle, own_grad, came_grad),
            [(sum_pair, *Y), (lanes[7:10], *Y), (table, *Z1)],
        )
        grad_tokens, up_part, root_means, sum_query, sum_up, sum_out = ended
        table = table + came
        table = table + swapped(table, *Z2)
    else:
        middle, normed_two, act, gh, small, ka, _ = feed_first(mixed, small)
        act, gh, small, kb, _ = feed_second(normed_two, small, act, gh)
        output, grad_middle, grad_mixed, small, out_kept, _ = finish(middle, small, act, gh)
        *grads, grad_bias = back_some(0, pairs[0])(grad_mixed)
        small, kq, _ = weights_some(0)(small, *grads)
        *grads_two, grad_bias_two = back_some(*pairs)(grad_mixed)
        table = everywhere(table_row(jnp.concatenate([grad_bias, grad_bias_two], 1)))
        own_grad, far_grad, small, kr, _ = weights_some(pairs[0] * 128, back_through)(
            small, *grads, *grads_two
        )
        came_grad = swapped(far_grad, *Y)
        grad_tokens = tokens_call(x, first_gain, grad_middle, own_grad, came_grad)
        small = everywhere(small)

        def scattered(value):
            return lax.psum_scatter(value.astype(f32), "dp", scatter_dimension=0, tiled=True)

        def unit(values, place):
            block, lane = place // 3, place % 3
            return values[width * block : width * (block + 1), UNIT * lane : UNIT * (lane + 1)]

        ups = jnp.concatenate([ka, kb], 0).reshape(blocks, 2 * width, width)
        sum_up = scattered(jnp.concatenate([ups[j, :width] for j in range(blocks)], 1))
        sum_down = scattered(jnp.concatenate([ups[j, width:] for j in range(blocks)], 0))
        sum_out = scattered(out_kept)
        sum_query, sum_keys, sum_values = [
            scattered(
                jnp.concatenate([unit(kq, 2 * i), unit(kq, 2 * i + 1), unit(kr, i)], 1)
            )
            for i in range(3)
        ]
        sum_pair = jnp.concatenate([sum_keys, sum_values], 0).astype(bf16)
        lanes = lax.dynamic_slice_in_dim(small, me * chunk, chunk, 1)
        up_part = lax.dynamic_slice_in_dim(
            small[16 : 16 + blocks].reshape(1, hidden), me * (hidden // shards), hidden // shards, 1
        )
        totals = jnp.sum(small[20:24], 1)
        sum_pair, back = swapped((sum_pair, lanes[7:10]), *Y)
        root_means = jnp.sqrt(totals[:3] / totals[3] + 1e-06).reshape(1, 3)

    sum_keys, sum_values = sum_pair[:chunk].astype(f32), sum_pair[chunk:].astype(f32)

    return (
        output[None],
        grad_tokens[None],
        lanes[5:6] + back[1:2],
        lanes[6:7] + back[2:3],
        sum_query[None],
        lanes[4:5],
        sum_keys[None],
        sum_values[None],
        back[0:1],
        sum_out[None],
        lanes[0:1],
        lanes[1:2],
        lanes[2:3],
        sum_up[None],
        up_part,
        sum_down[None],
        lanes[3:4],
        lax.dynamic_slice_in_dim(table, me * chunk, chunk, 1),
        root_means,
    )


def solution(mesh):
    whole, split = P("stream", None), P("stream", "dp")
    cube, cut = P("stream", None, None), P("stream", "dp", None)
    pages = P(None, "dp", None)
    in_specs = (
        cut, whole, whole, cube, whole, cube, cube, whole, cube, whole, whole, whole,
        cube, whole, cube, whole, whole, pages, pages, P("dp", None, None), cut,
    )
    out_specs = (
        cut, cut, split, split, cut, split, cut, cut, split, cut, split, split, split,
        cut, split, cut, split, split, whole,
    )
    return jax.shard_map(body, mesh=mesh, in_specs=in_specs, out_specs=out_specs, check_vma=False)
```

```python
import functools

import jax
import jax.numpy as jnp
from jax import lax
from jax.experimental import pallas as pl
from jax.experimental.pallas import tpu as pltpu
from jax.sharding import PartitionSpec as P

HEADS = 12
BUCKETS = 32
SMALL = 24

score_scale = 0.125
norm_eps = 1e-05
mask_fill = -1000000000.0
box_step = 32
precise_variant = lax.Precision.HIGHEST
f32 = jnp.float32
bf16 = jnp.bfloat16


def nn(a, b):
    return lax.dot_general(a, b, (((1,), (0,)), ((), ())), preferred_element_type=f32)


def nt(a, b):
    return lax.dot_general(a, b, (((1,), (1,)), ((), ())), preferred_element_type=f32)


def tn(a, b):
    return lax.dot_general(a, b, (((0,), (0,)), ((), ())), preferred_element_type=f32)


def normal_rows(rows):
    centre = rows - jnp.mean(rows, -1, keepdims=True)
    spread = jnp.mean(centre * centre, -1, keepdims=True)
    scale = lax.rsqrt(spread + norm_eps)
    return centre * scale, scale


def params(mib=60):
    return pltpu.CompilerParams(vmem_limit_bytes=mib * 1024 * 1024)


def cost(flops, moved, trans=0, scale=1 / 64):
    return pl.CostEstimate(
        flops=int(flops * scale),
        bytes_accessed=int(moved * scale),
        transcendentals=int(trans * scale),
    )


def full(shape):
    zeros = (0,) * len(shape)
    return pl.BlockSpec(shape, lambda *_: zeros)


def query_kernel(x_ref, gain_ref, shift_ref, w_ref, b_ref, n_ref, q_ref):
    norm, _ = normal_rows(x_ref[...].astype(f32))
    low = (norm * gain_ref[...] + shift_ref[...]).astype(bf16)
    n_ref[...] = low
    query = (nn(low, w_ref[...]) + b_ref[...]).astype(bf16)
    q_ref[...] = (query.astype(f32) * score_scale).astype(bf16)


def query_call(x, gain, shift, weight, bias):
    length, width = x.shape
    tile = 256
    rows = pl.BlockSpec((tile, width), lambda i: (i, 0))
    return pl.pallas_call(
        query_kernel,
        grid=(length // tile,),
        in_specs=[rows, full((1, width)), full((1, width)), full(weight.shape), full((1, width))],
        out_specs=[rows, rows],
        out_shape=[jax.ShapeDtypeStruct(x.shape, bf16)] * 2,
        compiler_params=params(),
        cost_estimate=cost(2 * length * width * width, 6 * length * width + 2 * width * width),
        name="query",
    )(x, gain, shift, weight, bias)


def pair_kernel(me_ref, x_ref, rows_ref, *rest, count):
    pieces, (n_ref, k_ref, v_ref, copy_ref, w_ref) = rest[:count], rest[-5:]
    if count == 4:

        @pl.when(pl.program_id(0) == 0)
        def _():
            low = me_ref[0] & 3
            for place in range(4):
                w_ref[place ^ low] = pieces[place][...]

        weights = w_ref
    else:
        weights = pieces[0]
    half = weights.shape[1]
    copy_ref[...] = x_ref[...]
    norm, _ = normal_rows(x_ref[...].astype(f32))
    low = (norm * rows_ref[0:1, :] + rows_ref[1:2, :]).astype(bf16)
    n_ref[...] = low
    left, right = low[:, :half], low[:, half:]
    k_ref[...] = (nn(left, weights[0]) + nn(right, weights[1])).astype(bf16)
    v_ref[...] = (nn(left, weights[2]) + nn(right, weights[3]) + rows_ref[2:3, :]).astype(bf16)


def pair_call(page, length, me, x, rows, pieces, before):
    page_len, width = x.shape
    tile = 256
    first = page * page_len // tile
    placed = pl.BlockSpec((tile, width), lambda i, *_: (i + first, 0))
    left = pl.BlockSpec(memory_space=pl.ANY)
    weights = (4, width // 2, width)
    out_specs = [placed] * 4
    shapes = [jax.ShapeDtypeStruct((length, width), bf16)] * 4
    scratch = []
    if len(pieces) == 4:
        out_specs = out_specs + [full(weights)]
        shapes = shapes + [jax.ShapeDtypeStruct(weights, bf16)]
    else:
        scratch = [pltpu.VMEM((8, 128), f32)]
    grid_spec = pltpu.PrefetchScalarGridSpec(
        num_scalar_prefetch=1,
        grid=(page_len // tile,),
        in_specs=[
            pl.BlockSpec((tile, width), lambda i, *_: (i, 0)),
            full(rows.shape),
        ]
        + [full(piece.shape) for piece in pieces]
        + [left] * len(before),
        out_specs=out_specs,
        scratch_shapes=scratch,
    )
    return pl.pallas_call(
        functools.partial(pair_kernel, count=len(pieces)),
        grid_spec=grid_spec,
        out_shape=shapes,
        input_output_aliases={3 + len(pieces) + i: i for i in range(len(before))},
        compiler_params=params(),
        cost_estimate=cost(4 * page_len * width * width, 8 * page_len * width),
        name="pair",
    )(me, x, rows, *pieces, *before)


def head_lanes(value, head, head_dim):
    lane = lax.broadcasted_iota(jnp.int32, value.shape, 1)
    mine = (lane >= head * head_dim) & (lane < (head + 1) * head_dim)
    return jnp.where(mine, value, jnp.zeros_like(value))


def picks_kernel(hq_ref, bias_ref, out_ref):
    for pair in range(out_ref.shape[1] // 256):
        both = jnp.concatenate([bias_ref[0, 2 * pair], bias_ref[0, 2 * pair + 1]], 1)
        out_ref[:, 256 * pair : 256 * (pair + 1)] = nn(hq_ref[0], both).astype(bf16)


def picks_call(hot_q, bias):
    pages, page_len = hot_q.shape[0], hot_q.shape[1]
    return pl.pallas_call(
        picks_kernel,
        grid=(pages, 3),
        in_specs=[
            pl.BlockSpec((1, page_len, 64), lambda p, h: (p, 0, 0)),
            pl.BlockSpec((1, 4, 64, 128), lambda p, h: (p, h, 0, 0)),
        ],
        out_specs=pl.BlockSpec((page_len, 512), lambda p, h: (p, h)),
        out_shape=jax.ShapeDtypeStruct((pages * page_len, HEADS * 128), bf16),
        compiler_params=params(),
        cost_estimate=cost(2 * pages * page_len * HEADS * 128 * 64, pages * page_len * HEADS * 256),
        name="picks",
    )(hot_q, bias)


def pair_right(q, picks):
    heads = [head_lanes(q, head, 64) for head in range(2)]
    sides = [
        jnp.concatenate([heads[head], picks[:, 128 * head : 128 * (head + 1)]], 1)
        for head in range(2)
    ]
    return jnp.concatenate(heads, 0), jnp.concatenate(sides, 0)


def attend_kernel(q_ref, k_ref, v_ref, picks_ref, hk_ref, *rest):
    o_ref, lse_ref = rest[-2:]
    page_len = q_ref.shape[0]
    for pair in range(q_ref.shape[1] // 128):
        lanes = slice(128 * pair, 128 * (pair + 1))
        left = jnp.concatenate([k_ref[:, lanes], hk_ref[0]], 1)
        v_turned = v_ref[:, lanes].astype(f32).T.astype(bf16)
        _, right = pair_right(q_ref[:, lanes], picks_ref[:, 256 * pair : 256 * (pair + 1)])
        scores = nt(left, right)
        peak = jnp.max(scores, 0, keepdims=True)
        raised = jnp.exp(scores - peak)
        total = jnp.sum(raised, 0, keepdims=True)
        probs = (raised * (1.0 / total)).astype(bf16)
        lse = peak + jnp.log(total)
        parts = []
        for head in range(2):
            mine = slice(head * page_len, (head + 1) * page_len)
            parts.append(nn(v_turned[head * 64 : (head + 1) * 64], probs[:, mine]))
            lse_ref[0, pair, head : head + 1, :] = lse[:, mine]
        o_ref[:, lanes] = jnp.concatenate(parts, 0).T.astype(bf16)


PAIRS = 2


def attend_specs(page_len, page, first):
    rows = pl.BlockSpec((page_len, 128 * PAIRS), lambda p, h: (p + page, h + first))
    picks = pl.BlockSpec((page_len, 256 * PAIRS), lambda p, h: (p + page, h + first))
    lse = pl.BlockSpec((1, PAIRS, 2, page_len), lambda p, h: (p + page, h + first, 0, 0))

    def hot(*shape):
        return pl.BlockSpec((1,) + shape, lambda p, h: (p + page, 0, 0))

    return rows, picks, lse, hot


def attend_call(page, q, k, v, picks, hot_k, before):
    length, width = q.shape
    pages, page_len = hot_k.shape[0], hot_k.shape[1]
    rows, picks_spec, lse, hot = attend_specs(page_len, page, 0)
    left = pl.BlockSpec(memory_space=pl.ANY)
    return pl.pallas_call(
        attend_kernel,
        grid=(1, width // 128 // PAIRS),
        in_specs=[rows, rows, rows, picks_spec, hot(page_len, 128)] + [left] * len(before),
        out_specs=[rows, lse],
        out_shape=[
            jax.ShapeDtypeStruct((length, width), bf16),
            jax.ShapeDtypeStruct((pages, width // 128, 2, page_len), f32),
        ],
        input_output_aliases={5 + i: i for i in range(len(before))},
        compiler_params=params(),
        cost_estimate=cost(
            16 * page_len * page_len * width,
            8 * page_len * width,
            page_len * page_len * HEADS,
        ),
        name="attend",
    )(q, k, v, picks, hot_k, *before)


def attend_back_kernel(
    q_ref,
    k_ref,
    v_ref,
    picks_ref,
    hq_ref,
    hk_ref,
    hkt_ref,
    lse_ref,
    o_ref,
    do_ref,
    dq_ref,
    dk_ref,
    dv_ref,
    gb_ref,
):
    page_len = q_ref.shape[0]
    row = lax.broadcasted_iota(jnp.int32, (8, 128), 0)
    lane = lax.broadcasted_iota(jnp.int32, (8, 128), 1)
    chooser = (row == lane // 64).astype(bf16)
    for pair in range(q_ref.shape[1] // 128):
        lanes = slice(128 * pair, 128 * (pair + 1))
        k, v, do = k_ref[:, lanes], v_ref[:, lanes], do_ref[:, lanes]
        left = jnp.concatenate([k, hk_ref[0]], 1)
        k_turned = k.astype(f32).T.astype(bf16)
        overlap = do.astype(f32) * o_ref[:, lanes].astype(f32)
        high = overlap.astype(bf16)
        rest = (overlap - high.astype(f32)).astype(bf16)
        delta = nt(chooser, high) + nt(chooser, rest)
        delta = jnp.concatenate([delta[0:1], delta[1:2]], 1)
        lse = jnp.concatenate([lse_ref[0, pair, 0:1, :], lse_ref[0, pair, 1:2, :]], 1)
        queries, right = pair_right(q_ref[:, lanes], picks_ref[:, 256 * pair : 256 * (pair + 1)])
        do_heads = jnp.concatenate([head_lanes(do, head, 64) for head in range(2)], 0)
        probs = jnp.exp(nt(left, right) - lse)
        turn = (probs * (nt(v, do_heads) - delta)).astype(bf16)
        dv_ref[:, lanes] = nn(probs.astype(bf16), do_heads).astype(bf16)
        dk_ref[:, lanes] = nn(turn, queries).astype(bf16)
        parts, sums = [], []
        for head in range(2):
            both = nn(
                jnp.concatenate([k_turned[head * 64 : (head + 1) * 64], hkt_ref[0]], 0),
                turn[:, head * page_len : (head + 1) * page_len],
            )
            parts.append(both[:64])
            sums.append(both[64:])
        dq_ref[:, lanes] = (jnp.concatenate(parts, 0) * score_scale).T.astype(bf16)
        sums = jnp.concatenate(sums, 0)
        high = sums.astype(bf16)
        rest = (sums - high.astype(f32)).astype(bf16)
        grads = nn(jnp.concatenate([high, rest], 0), hq_ref[0])
        grads = grads[:128] + grads[128:]
        for head in range(2):
            gb_ref[0, 2 * pair + head] = grads[64 * head : 64 * (head + 1)]


def attend_back_call(pair, pairs, q, k, v, picks, hot_q, hot_k, hot_kt, lse_in, o, do):
    length, width = q.shape
    pages, page_len = hot_q.shape[0], hot_q.shape[1]
    rows, picks_spec, lse, hot = attend_specs(page_len, 0, pair // PAIRS)
    given = pl.BlockSpec((page_len, 128 * PAIRS), lambda p, h: (p, h))
    grad_bias = pl.BlockSpec((1, 2 * PAIRS, 64, 64), lambda p, h: (p, h, 0, 0))
    wide = jax.ShapeDtypeStruct((length, pairs * 128), bf16)
    return pl.pallas_call(
        attend_back_kernel,
        grid=(pages, pairs // PAIRS),
        in_specs=[
            rows,
            rows,
            rows,
            picks_spec,
            hot(page_len, 64),
            hot(page_len, 128),
            hot(64, page_len),
            lse,
            rows,
            rows,
        ],
        out_specs=[given, given, given, grad_bias],
        out_shape=[wide, wide, wide, jax.ShapeDtypeStruct((pages, 2 * pairs, 64, 64), f32)],
        compiler_params=params(),
        cost_estimate=cost(
            40 * length * page_len * pairs * 128,
            16 * length * pairs * 128,
            length * page_len * 2 * pairs,
            64,
        ),
        name="attend_back",
    )(q, k, v, picks, hot_q, hot_k, hot_kt, lse_in, o, do)


def put_rows(
    scratch, keep, send, me, relative, at, x_step, z_step, lanes=slice(None), source=slice(None)
):
    if not relative:
        keep[pl.ds(at, scratch.shape[0]), lanes] = scratch[:, source].astype(bf16)
        return
    step = scratch.shape[0] // 16
    for place in range(16):
        owner = place ^ me
        rows = scratch[pl.ds(pl.multiple_of(owner * step, step), step), source].astype(bf16)
        target = send if place & 1 else keep
        z = ((place >> 2) & 1) * 2 + (place >> 3)
        low = at + ((place >> 1) & 1) * x_step + z * z_step
        target[pl.ds(pl.multiple_of(low, 16), step), lanes] = rows


def put_quarter(scratch, keep, send, me, relative, at, x_step):
    if not relative:
        keep[pl.ds(at, scratch.shape[0]), :] = scratch[...].astype(bf16)
        return
    step = scratch.shape[0] // 4
    for place in range(4):
        owner = place ^ (me & 3)
        rows = scratch[pl.ds(pl.multiple_of(owner * step, step), step), :].astype(bf16)
        target = send if place & 1 else keep
        target[pl.ds(pl.multiple_of(at + (place >> 1) * x_step, 16), step), :] = rows


def block_shapes(rows, width, relative):
    if relative:
        return (rows // 2, width), (rows // 2, width)
    return (rows, width), (16, 128)


def feed_kernel(me_ref, *rest, first, blocks, relative, tile):
    ins, rest = rest[: 12 if first else 6], rest[12 if first else 8 :]
    if first:
        x_ref, mixed_ref, keep_ref, wo_ref, bo_ref, gain_ref, shift_ref = ins[:7]
        cot_ref, up_ref, upb_ref, down_ref, old_ref = ins[7:]
        middle_ref, n2_ref = rest[:2]
        rest = rest[2:]
    else:
        n2_ref, cot_ref, up_ref, upb_ref, down_ref, old_ref = ins
    act_ref, gh_ref, small_ref, kept_ref, sent_ref, dw_ref = rest[-6:]
    step = pl.program_id(0)
    length = cot_ref.shape[0]

    @pl.when(step == 0)
    def _():
        small_ref[...] = old_ref[...]
        if first:

            for i in range(length // 256):
                at = slice(i * 256, (i + 1) * 256)
                branch = nn(mixed_ref[at, :], wo_ref[...]) + bo_ref[...]
                middle = x_ref[at, :].astype(f32) + branch
                middle_ref[at, :] = middle
                norm, _ = normal_rows(middle)
                n2_ref[at, :] = (norm * gain_ref[...] + shift_ref[...]).astype(bf16)
                small_ref[21:22, :] += jnp.sum(branch * branch * keep_ref[at, :], 0, keepdims=True)
                small_ref[23:24, :] += jnp.broadcast_to(
                    jnp.sum(keep_ref[at, :], 0, keepdims=True), (1, small_ref.shape[1])
                )

    row = (0 if first else blocks) + 16 + step

    @pl.loop(0, length // tile)
    def _(i):
        at = pl.ds(pl.multiple_of(i * tile, tile), tile)
        hidden = nn(n2_ref[at, :], up_ref[...]) + upb_ref[...]
        slope = nt(cot_ref[at, :], down_ref[...])
        gate = 0.5 * (1.0 + lax.erf(hidden * 0.7071067811865476))
        bell = jnp.exp(hidden * hidden * -0.5) * 0.3989422804014327
        act_ref[at, :] = (hidden * gate).astype(bf16)
        gh = (slope * (gate + hidden * bell)).astype(bf16)
        gh_ref[at, :] = gh
        small_ref[pl.ds(row, 1), :] += jnp.sum(gh.astype(f32), 0, keepdims=True)

    me = me_ref[0]
    width = dw_ref.shape[0]
    up_at, down_at = (step * 48, step * 192) if relative else (step * 2 * width, 0)
    dw_ref[...] = tn(n2_ref[...], gh_ref[...])
    up_steps = (96, 192) if first else (768, 96)
    put_rows(dw_ref, kept_ref, sent_ref, me, relative, up_at, *up_steps)
    dw_ref[...] = tn(act_ref[...], cot_ref[...])
    if relative:
        down_at = down_at + (768 if first else 384)
    else:
        down_at = up_at + width
    put_quarter(dw_ref, kept_ref, sent_ref, me, relative, down_at, 384 if first else 768)


def feed_call(part, parts, me, given, cot, up, upb, down, small, before, relative):
    length, width = cot.shape
    first = part == 0
    hidden = up.shape[1]
    blocks = hidden // width // parts
    start = part * blocks
    whole, row = full((length, width)), full((1, width))
    kept, sent = block_shapes(2 * width * blocks, width, relative)
    shape = jax.ShapeDtypeStruct
    if first:
        specs = [whole, whole, full((length, 1)), full((width, width)), row, row, row]
        outs = [whole, whole]
        shapes = [shape((length, width), f32), shape((length, width), bf16)]
    else:
        specs, outs, shapes = [whole], [], []
    columns = pl.BlockSpec((length, width), lambda j, *_: (0, j + start))
    left = pl.BlockSpec(memory_space=pl.ANY)
    grid_spec = pltpu.PrefetchScalarGridSpec(
        num_scalar_prefetch=1,
        grid=(blocks,),
        in_specs=specs
        + [
            whole,
            pl.BlockSpec((width, width), lambda j, *_: (0, j + start)),
            pl.BlockSpec((1, width), lambda j, *_: (0, j + start)),
            pl.BlockSpec((width, width), lambda j, *_: (j + start, 0)),
            full((SMALL, width)),
        ]
        + [left] * len(before),
        out_specs=outs + [columns, columns, full((SMALL, width)), full(kept), full(sent)],
        scratch_shapes=[pltpu.VMEM((width, width), f32)],
    )
    count = 1 + len(specs) + 5
    return pl.pallas_call(
        functools.partial(
            feed_kernel, first=first, blocks=blocks, relative=relative, tile=512
        ),
        grid_spec=grid_spec,
        out_shape=shapes
        + [
            shape((length, hidden), bf16),
            shape((length, hidden), bf16),
            shape((SMALL, width), f32),
            shape(kept, bf16),
            shape(sent, bf16),
        ],
        input_output_aliases={count + i: i for i in range(len(before))},
        compiler_params=params(),
        cost_estimate=cost(
            8 * length * width * width * blocks, 20 * length * width, 2 * length * width
        ),
        name="feed",
    )(me, *given, cot, up, upb, down, small, *before)


def finish_kernel(
    me_ref,
    act_ref,
    gh_ref,
    up_ref,
    down_ref,
    middle_ref,
    cot_ref,
    keep_ref,
    mixed_ref,
    wo_ref,
    gain_ref,
    downb_ref,
    old_ref,
    out_ref,
    gm_ref,
    gx_ref,
    small_ref,
    kept_ref,
    sent_ref,
    feed_ref,
    gn_ref,
    dw_ref,
    *,
    blocks,
    tile,
    relative,
):
    step = pl.program_id(0)

    @pl.when(step == 0)
    def _():
        small_ref[...] = old_ref[...]
        feed_ref[...] = jnp.zeros_like(feed_ref)
        gn_ref[...] = jnp.zeros_like(gn_ref)

    @pl.when(step < blocks - 1)
    def _():
        feed_ref[...] += nn(act_ref[...], down_ref[...])
        gn_ref[...] += nt(gh_ref[...], up_ref[...])

    @pl.when(step >= blocks - 1)
    def _():
        lows = []
        for i in range(tile // 256):
            here = slice(i * 256, (i + 1) * 256)
            at = pl.ds(pl.multiple_of((step - blocks + 1) * tile + i * 256, 256), 256)
            feed = feed_ref[at, :] + nn(act_ref[at, :], down_ref[...]) + downb_ref[...]
            middle = middle_ref[here, :]
            output = middle + feed
            out_ref[here, :] = output.astype(bf16)
            weight = keep_ref[here, :]
            cot = cot_ref[here, :].astype(f32)
            norm, scale = normal_rows(middle)
            grad = gn_ref[at, :] + nt(gh_ref[at, :], up_ref[...])
            inner = grad * gain_ref[...]
            grad_middle = cot + scale * (
                inner
                - jnp.mean(inner, -1, keepdims=True)
                - norm * jnp.mean(inner * norm, -1, keepdims=True)
            )
            gm_ref[here, :] = grad_middle
            low = grad_middle.astype(bf16)
            gx_ref[here, :] = nt(low, wo_ref[...]).astype(bf16)
            lows.append(low)
            small_ref[0:1, :] += jnp.sum(low.astype(f32), 0, keepdims=True)
            small_ref[1:2, :] += jnp.sum(grad * norm, 0, keepdims=True)
            small_ref[2:3, :] += jnp.sum(grad, 0, keepdims=True)
            small_ref[3:4, :] += jnp.sum(cot, 0, keepdims=True)
            small_ref[20:21, :] += jnp.sum(output * output * weight, 0, keepdims=True)
            small_ref[22:23, :] += jnp.sum(feed * feed * weight, 0, keepdims=True)
        part = tn(mixed_ref[...], jnp.concatenate(lows, 0))

        @pl.when(step == blocks - 1)
        def _():
            dw_ref[...] = part

        @pl.when(step > blocks - 1)
        def _():
            dw_ref[...] += part

    @pl.when(step == pl.num_programs(0) - 1)
    def _():
        put_rows(dw_ref, kept_ref, sent_ref, me_ref[0], relative, 0, 192, 48)


def finish_call(me, acts, up, down, middle, cot, keep, mixed, wo, gain, downb, small, relative):
    length, width = mixed.shape
    blocks = up.shape[1] // width
    end = blocks - 1
    tile = 512
    whole, row = full((length, width)), full((1, width))
    kept, sent = block_shapes(width, width, relative)
    columns = pl.BlockSpec((length, width), lambda j, *_: (0, jnp.minimum(j, end)))

    def tiled(lanes):
        return pl.BlockSpec((tile, lanes), lambda j, *_: (jnp.maximum(j - end, 0), 0))

    rows = tiled(width)
    shape = jax.ShapeDtypeStruct
    grid_spec = pltpu.PrefetchScalarGridSpec(
        num_scalar_prefetch=1,
        grid=(end + length // tile,),
        in_specs=[
            columns,
            columns,
            pl.BlockSpec((width, width), lambda j, *_: (0, jnp.minimum(j, end))),
            pl.BlockSpec((width, width), lambda j, *_: (jnp.minimum(j, end), 0)),
            rows,
            rows,
            tiled(1),
            rows,
            full((width, width)),
            row,
            row,
            full((SMALL, width)),
        ],
        out_specs=[rows, rows, rows, full((SMALL, width)), full(kept), full(sent)],
        scratch_shapes=[
            pltpu.VMEM((length, width), f32),
            pltpu.VMEM((length, width), f32),
            pltpu.VMEM((width, width), f32),
        ],
    )
    return pl.pallas_call(
        functools.partial(finish_kernel, blocks=blocks, tile=tile, relative=relative),
        grid_spec=grid_spec,
        out_shape=[
            shape((length, width), bf16),
            shape((length, width), f32),
            shape((length, width), bf16),
            shape((SMALL, width), f32),
            shape(kept, bf16),
            shape(sent, bf16),
        ],
        compiler_params=params(),
        cost_estimate=cost(4 * length * width * width, 24 * length * width),
        name="finish",
    )(me, *acts, up, down, middle, cot, keep, mixed, wo, gain, downb, small)


UNIT = 256


def units_of(part):
    each = part // UNIT
    places = [(grad, unit) for grad in range(3) for unit in range(each)]
    return [(grad, unit, i // 3, i % 3) for i, (grad, unit) in enumerate(places)]


def spread_small(small, total, chunk):
    sums = jnp.broadcast_to(jnp.sum(small[20:24, :], 1, keepdims=True), (4, chunk))
    for owner in range(16):
        lanes = slice(owner * chunk, (owner + 1) * chunk)
        block, start = owner // 4, (owner % 4) * 4 * chunk
        ups = [
            small[16 + block : 17 + block, start + i * chunk : start + (i + 1) * chunk]
            for i in range(4)
        ]
        piece = jnp.concatenate([small[0:16, lanes], *ups, sums], 0)
        high = piece.astype(bf16).astype(f32)
        whole = jnp.concatenate([high, piece - high], 0)
        for i in range(3):
            total[owner * 16 : (owner + 1) * 16, i * 128 : i * 128 + chunk] = whole[
                i * 16 : (i + 1) * 16
            ]


def weights_kernel(me_ref, n_ref, np_ref, *rest, start, count, relative):
    refs, rest = rest[: 3 * count], rest[3 * count :]
    last = count > 1
    old_ref, rest = rest[0], rest[1:]
    if last:
        x_ref, xp_ref, wq_ref, wp_ref, gq_ref, gp_ref = rest[:6]
        rest = rest[6:]
    small_ref, kept_ref, sent_ref, *totals = rest
    step = pl.program_id(0)
    grads = [ref[...] for ref in refs[-3:]]
    part = grads[0].shape[1]
    lanes = slice(start, start + part)
    sources = [n_ref[...], np_ref[...], np_ref[...]]

    @pl.when(step == 0)
    def _():
        small_ref[...] = old_ref[...]
        for total in totals[:3]:
            total[...] = jnp.zeros_like(total)

    for total, source, grad in zip(totals, sources, grads):
        total[...] += tn(source, grad)
    small_ref[4:5, lanes] += jnp.sum(grads[0].astype(f32), 0, keepdims=True)
    small_ref[7:8, lanes] += jnp.sum(grads[2].astype(f32), 0, keepdims=True)
    if last:
        dq, dk, dv = [jnp.concatenate([ref[...] for ref in refs[i::3]], 1) for i in range(3)]
        width = wq_ref.shape[0]
        far = nt(dk, wp_ref[0:2].reshape(width, width))
        far = far + nt(dv, wp_ref[2:4].reshape(width, width))
        own = nt(dq, wq_ref[...])
        gq_ref[...] = own
        gp_ref[...] = far.astype(bf16)
        norm, _ = normal_rows(x_ref[...].astype(f32))
        far_norm, _ = normal_rows(xp_ref[...].astype(f32))
        small_ref[5:6, :] += jnp.sum(own * norm, 0, keepdims=True)
        small_ref[6:7, :] += jnp.sum(own, 0, keepdims=True)
        small_ref[8:9, :] += jnp.sum(far * far_norm, 0, keepdims=True)
        small_ref[9:10, :] += jnp.sum(far, 0, keepdims=True)

    @pl.when(step == pl.num_programs(0) - 1)
    def _():
        me = me_ref[0]
        z_step = 64 if last else 48 * part // UNIT
        for grad, unit, block, place in units_of(part):
            put_rows(
                totals[grad], kept_ref, sent_ref, me, relative,
                48 * block if relative else 768 * block, 4 * z_step, z_step,
                slice(place * UNIT, (place + 1) * UNIT), slice(unit * UNIT, (unit + 1) * UNIT),
            )
        if last and relative:
            spread = totals[3]
            spread[...] = jnp.zeros_like(spread)
            spread_small(small_ref[...], spread, small_ref.shape[1] // 16)
            put_rows(spread, kept_ref, sent_ref, me, relative, 48, 4 * z_step, z_step)


def weights_call(start, me, n, n_far, grads, small, more, relative):
    length, width = n.shape
    count = len(grads) // 3
    last = count > 1
    part = grads[-1].shape[1]
    tile = 512
    rows = pl.BlockSpec((tile, width), lambda i, *_: (i, 0))
    extra = last and relative
    kept, sent = block_shapes(width * part // UNIT + (256 if extra else 0), width, relative)
    shape = jax.ShapeDtypeStruct
    specs = [rows, rows]
    specs += [pl.BlockSpec((tile, grad.shape[1]), lambda i, *_: (i, 0)) for grad in grads]
    specs += [full((SMALL, width))]
    outs, shapes = [], []
    if last:
        specs += [rows, rows, full(more[2].shape), full(more[3].shape)]
        outs = [rows, rows]
        shapes = [shape((length, width), f32), shape((length, width), bf16)]
    grid_spec = pltpu.PrefetchScalarGridSpec(
        num_scalar_prefetch=1,
        grid=(length // tile,),
        in_specs=specs,
        out_specs=outs + [full((SMALL, width)), full(kept), full(sent)],
        scratch_shapes=[pltpu.VMEM((width, part), f32)] * 3
        + ([pltpu.VMEM((256, width), f32)] if extra else []),
    )
    return pl.pallas_call(
        functools.partial(weights_kernel, start=start, count=count, relative=relative),
        grid_spec=grid_spec,
        out_shape=shapes
        + [shape((SMALL, width), f32), shape(kept, bf16), shape(sent, bf16)],
        compiler_params=params(),
        cost_estimate=cost(6 * length * width * part, 24 * length * width),
        name="weights",
    )(me, n, n_far, *grads, small, *more)


def tokens_kernel(x_ref, gain_ref, gm_ref, gq_ref, gf_ref, out_ref):
    norm, scale = normal_rows(x_ref[...].astype(f32))
    inner = (gq_ref[...] + gf_ref[...].astype(f32)) * gain_ref[...]
    out_ref[...] = gm_ref[...] + scale * (
        inner
        - jnp.mean(inner, -1, keepdims=True)
        - norm * jnp.mean(inner * norm, -1, keepdims=True)
    )


def tokens_call(x, gain, gm, gq, gf):
    length, width = x.shape
    rows = pl.BlockSpec((256, width), lambda i: (i, 0))
    return pl.pallas_call(
        tokens_kernel,
        grid=(length // 256,),
        in_specs=[rows, full((1, width)), rows, rows, rows],
        out_specs=rows,
        out_shape=jax.ShapeDtypeStruct((length, width), f32),
        compiler_params=params(),
        cost_estimate=cost(20 * length * width, 16 * length * width),
        name="tokens",
    )(x, gain, gm, gq, gf)


def swapped(value, axis, mask):
    pairs = [(source, source ^ mask) for source in range(lax.axis_size(axis))]
    return lax.ppermute(value, axis, pairs)


def added(a, b, dtype=bf16):
    return (a.astype(f32) + b.astype(f32)).astype(dtype)


def together(kernel, inputs, moves=(), later=(), due=()):
    count = len(moves)
    moves = list(moves) + list(later)
    inputs, values = lax.optimization_barrier((inputs, [value for value, _, _ in moves]))
    came = [swapped(value, *way[1:]) for value, way in zip(values, moves)]
    results = kernel(*inputs) if kernel else []
    results, now, due = lax.optimization_barrier((results, came[:count], list(due)))
    return results, now, came[count:], due


def total(*values):
    return functools.reduce(jnp.add, [value.astype(f32) for value in values])


def quads(*values):
    values = [value.reshape(4, -1, value.shape[-1]) for value in values]
    return jnp.concatenate(values, 1).reshape(-1, values[0].shape[-1])


def everywhere(value):
    mask = 1
    while mask < lax.axis_size("dp"):
        value = value + swapped(value, "dp", mask)
        mask *= 2
    return value


def pick_stream(pair, stream):
    return jnp.where(stream == 0, pair[0], pair[1])


def box_onehots(seg_boxes, buckets):
    half = buckets // 2
    levels = jnp.arange(buckets, dtype=jnp.int32)
    centre_x = (seg_boxes[..., 0] + seg_boxes[..., 2]) // 2
    centre_y = (seg_boxes[..., 1] + seg_boxes[..., 3]) // 2
    step_x = (
        jnp.clip((centre_x[:, None, :] - centre_x[:, :, None]) // box_step, -half, half - 1) + half
    )
    step_y = (
        jnp.clip((centre_y[:, None, :] - centre_y[:, :, None]) // box_step, -half, half - 1) + half
    )
    return (
        (step_x[..., None] == levels).astype(jnp.float32),
        (step_y[..., None] == levels).astype(jnp.float32),
    )


def body(
    tokens,
    first_gain,
    first_shift,
    query_weight,
    query_bias,
    key_weight,
    value_weight,
    value_bias,
    out_weight,
    out_bias,
    second_gain,
    second_shift,
    up_weight,
    up_bias,
    down_weight,
    down_bias,
    box_table,
    segments,
    validity,
    seg_boxes,
    cotangent,
):
    stream = lax.axis_index("stream")
    me = lax.axis_index("dp")
    shards = lax.axis_size("dp")
    width = tokens.shape[2]
    hidden = up_weight.shape[2]
    pages, page_len = segments.shape[1], segments.shape[2]
    length = pages * page_len
    relative = shards == 16
    me_ref = me.reshape(1).astype(jnp.int32)
    x = tokens[0]

    own_seg = pick_stream(segments, stream)
    far_seg = pick_stream(segments, 1 - stream)
    own_keep = pick_stream(validity, stream)
    far_keep = pick_stream(validity, 1 - stream)
    levels = jnp.arange(64, dtype=jnp.int32)
    hot_q = (own_seg[:, :, None] == levels).astype(bf16)
    hot_kt = (far_seg[:, None, :] == levels[None, :, None]).astype(bf16)
    wide_levels = jnp.arange(128, dtype=jnp.int32)
    hot_k = jnp.where(
        wide_levels == 64,
        jnp.where(far_keep[:, :, None] > 0, 0.0, mask_fill),
        (far_seg[:, :, None] == wide_levels).astype(f32),
    ).astype(bf16)
    hot_x, hot_y = box_onehots(seg_boxes, BUCKETS)
    tables = box_table[0].reshape(2, HEADS, BUCKETS)
    seg_bias = (
        jnp.einsum("pabn,hn->phab", hot_x, tables[0], precision=precise_variant)
        + jnp.einsum("pabn,hn->phab", hot_y, tables[1], precision=precise_variant)
    ).astype(bf16)
    ones = (jnp.arange(64) == 0).astype(bf16)
    seg_bias = jnp.concatenate([seg_bias, jnp.broadcast_to(ones, seg_bias.shape)], -1)

    keep_column = own_keep.reshape(length, 1).astype(f32)
    blocks, chunk = hidden // width, width // shards
    cot = cotangent[0]
    Y, CORE, X, Z1, Z2 = ("stream", 1), ("dp", 1), ("dp", 2), ("dp", 4), ("dp", 8)

    low = me & 3
    half = width // 2

    def quarter(weight):
        return lax.dynamic_slice_in_dim(weight[0], (low & 1) * half, half, 0)

    piece = jnp.where(low < 2, quarter(key_weight), quarter(value_weight))
    vectors = jnp.concatenate([first_gain, first_shift, value_bias], 0)
    (normed, query), (piece, far_rows), _, _ = together(
        query_call,
        (x, first_gain, first_shift, query_weight[0], query_bias),
        [(piece, *Y), (vectors, *Y)],
    )
    page_x = [x[page * page_len : (page + 1) * page_len] for page in range(pages)]
    (picks, hot_q, hot_k), (x_piece, core_piece, came_x), _, _ = together(
        lambda bias, hot_q, hot_k: (picks_call(hot_q, bias), hot_q, hot_k),
        (seg_bias, hot_q, hot_k),
        [(piece, *X), (piece, *CORE), (page_x[0], *Y)],
    )
    far_pages = [came_x]
    pieces = [piece, core_piece, x_piece, swapped(x_piece, *CORE)]
    far, mixing = (), ()
    for page in range(pages):

        def page_step(came, pieces, far, mixing, page=page):
            far = pair_call(page, length, me_ref, came, far_rows, pieces, far)
            return far, attend_call(page, query, far[1], far[2], picks, hot_k, mixing)

        moves = [(page_x[page + 1], *Y)] if page + 1 < pages else []
        (result, mixing), came, _, _ = together(
            page_step, (far_pages[page], pieces, tuple(far), tuple(mixing)), moves
        )
        far = result[:4]
        if page == 0:
            pieces = [result[4]]
        far_pages += came
    far_normed, keys, value_rows, far_x = far
    far_weights = pieces[0]
    mixed, log_total = mixing

    small = jnp.zeros((SMALL, width), f32)

    def feed_first(mixed, small):
        return feed_call(
            0, 2, me_ref,
            (x, mixed, keep_column, out_weight[0], out_bias, second_gain, second_shift),
            cot, up_weight[0], up_bias, down_weight[0], small, (), relative,
        )

    def feed_second(n2, small, *acts):
        return feed_call(
            1, 2, me_ref, (n2,), cot, up_weight[0], up_bias, down_weight[0], small, acts, relative
        )

    def finish(middle, small, *acts):
        return finish_call(
            me_ref, acts, up_weight[0], down_weight[0], middle, cot, keep_column, mixed,
            out_weight[0], second_gain, down_bias, small, relative,
        )

    def back_some(pair, pairs):
        def call(grad_mixed):
            return attend_back_call(
                pair, pairs, query, keys, value_rows, picks, hot_q, hot_k, hot_kt, log_total,
                mixed, grad_mixed,
            )

        return call

    def weights_some(start, more=()):
        def call(small, *grads):
            return weights_call(start, me_ref, normed, far_normed, grads, small, more, relative)

        return call

    back_through = (x, far_x, query_weight[0], far_weights)
    pairs = (4, width // 128 - 4)

    def table_row(grad_bias):
        return jnp.concatenate(
            [
                jnp.einsum("pabn,phba->hn", hot_x, grad_bias, precision=precise_variant),
                jnp.einsum("pabn,phba->hn", hot_y, grad_bias, precision=precise_variant),
            ],
            0,
        ).reshape(1, -1)

    if relative:
        z_low, z_high = (me >> 2) & 1, me >> 3

        def downs(pair):
            one, other = pair[:192], pair[192:]
            return jnp.where(z_low, other, one), jnp.where(z_low, one, other)

        (middle, normed_two, act, gh, small, ka, sa), _, _, _ = together(
            feed_first, (mixed, small)
        )
        (act, gh, small, kb, sb), (ca,), _, _ = together(
            feed_second, (normed_two, small, act, gh), [(sa, *CORE)]
        )
        up_go, down_go = added(ka[384:768], ca[384:768]), added(ka[1152:], ca[1152:])
        (output, grad_middle, grad_mixed, small, ko, so), (cb, x0, z0), _, _ = together(
            finish,
            (middle, small, act, gh),
            [(sb, *CORE), (down_go, *X), (up_go, *Z1)],
        )
        up_go = total(ka[192:384], ca[192:384], z0[192:]).astype(bf16)
        up_stay = total(ka[:192], ca[:192], z0[:192])
        go = added(kb[768:], cb[768:])
        (*grads, grad_bias), (co, z0), (x2,), _ = together(
            back_some(0, pairs[0]), (grad_mixed,), [(so, *CORE), (up_go, *Z2)], [(go, *X)]
        )
        one = total(ka[768:1152], ca[768:1152], x0).astype(bf16)
        one_keep, one_go = downs(one)
        up_low = total(up_stay, z0)
        go = jnp.concatenate([up_low[96:].astype(bf16), added(ko[192:], co[192:])], 0)
        (small, kq, sq), (z0,), (xo,), (x2,) = together(
            weights_some(0), (small, *grads), [(one_go, *Z1)], [(go, *X)], [x2]
        )
        down_one = added(one_keep, z0)
        two = total(kb[:768], cb[:768], x2).astype(bf16)
        two_keep, two_go = downs(two[384:])
        (*grads_two, grad_bias_two), (cq, z1), _, (xo,) = together(
            back_some(*pairs), (grad_mixed,), [(sq, *CORE), (two_go, *Z1)], [], [xo]
        )
        down_two = added(two_keep, z1)
        down_stay = jnp.where(z_high, down_two, down_one)
        down_go = jnp.where(z_high, down_one, down_two)
        go = added(kq[384:], cq[384:])
        rest = quads(two[:384], total(ko[:192], co[:192], xo[96:]).astype(bf16))
        (own_grad, far_grad, small, kr, sr), (xq, z1), (z3,), _ = together(
            weights_some(pairs[0] * 128, back_through),
            (small, *grads, *grads_two),
            [(go, *X), (rest[288:], *Z1)],
            [(down_go, *Z2)],
        )
        _, (cr,), (came_grad,), _ = together(None, (), [(sr, *CORE)], [(far_grad, *Y)])
        go, grad_bias, xq, z1 = lax.optimization_barrier(
            (added(kr[256:], cr[256:]), (grad_bias, grad_bias_two), xq, z1)
        )
        rest_go = added(rest[144:288], z1[144:])
        group_go = total(kq[192:384], cq[192:384], xq[192:]).astype(bf16)
        z4, z2 = swapped(group_go, *Z1), swapped(rest_go, *Z2)
        table = table_row(jnp.concatenate(grad_bias, 1))
        table = table + swapped(table, *CORE)
        _, (xr,), _, (z4, table) = together(None, (), [(go, *X)], [], [z4, table])
        r_go = total(kr[128:256], cr[128:256], xr[128:]).astype(bf16)
        group_go = total(kq[96:192], cq[96:192], xq[96:192], z4[96:]).astype(bf16)
        z5 = swapped(group_go, *Z2)
        _, (z1r, came), _, (z3,) = together(None, (), [(r_go, *Z1), (table, *X)], [], [z3])
        table = table + came
        r_go = total(kr[64:128], cr[64:128], xr[64:128], z1r[64:]).astype(bf16)
        _, (z2r, came), _, (z2, z5, came_grad) = together(
            None, (), [(r_go, *Z2), (table, *Z1)], [], [z2, z5, came_grad]
        )
        table = table + came
        up_low = total(up_low[:96], xo[:96])
        sum_down = total(down_stay, z3)
        rest = total(rest[:144], z1[:144], z2)
        first = total(kq[:96], cq[:96], xq[:96], z4[:96], z5)
        last = total(kr[:64], cr[:64], xr[:64], z1r[:64], z2r)
        sum_up = jnp.concatenate([up_low[:48], up_low[48:], rest[:48], rest[48:96]], 1)
        sum_out = rest[96:]

        def lanes_of(spread):
            pieces = [spread[:, 128 * i : 128 * i + chunk] for i in range(3)]
            pieces = jnp.concatenate(pieces, 0)
            return pieces[:SMALL] + pieces[SMALL:]

        def unit(values, place):
            block, lane = place // 3, place % 3
            return values[48 * block : 48 * block + 48, UNIT * lane : UNIT * (lane + 1)]

        def joined(first, last, i):
            return jnp.concatenate(
                [unit(first, 2 * i), unit(first, 2 * i + 1), unit(last, i)], 1
            )

        def ending(*given):
            lanes = lanes_of(last[48:])
            totals = lanes[20:24, 0]
            root_means = jnp.sqrt(totals[:3] / totals[3] + 1e-06).reshape(1, 3)
            up_part = lanes[16:20].reshape(1, hidden // shards)
            grad_tokens = tokens_call(*given)
            sum_query = joined(first, last, 0)
            return grad_tokens, lanes, root_means, up_part, sum_query, sum_up, sum_out, sum_down

        ended, (far_first, far_last, came), _, _ = together(
            ending,
            (x, first_gain, grad_middle, own_grad, came_grad),
            [(first.astype(bf16), *Y), (last, *Y), (table, *Z2)],
        )
        grad_tokens, lanes, root_means, up_part, sum_query, sum_up, sum_out, sum_down = ended
        table = table + came
        back = lanes_of(far_last[48:])[7:10]
        far_first = far_first.astype(f32)
        sum_keys, sum_values = joined(far_first, far_last, 1), joined(far_first, far_last, 2)
    else:
        middle, normed_two, act, gh, small, ka, _ = feed_first(mixed, small)
        act, gh, small, kb, _ = feed_second(normed_two, small, act, gh)
        output, grad_middle, grad_mixed, small, out_kept, _ = finish(middle, small, act, gh)
        *grads, grad_bias = back_some(0, pairs[0])(grad_mixed)
        small, kq, _ = weights_some(0)(small, *grads)
        *grads_two, grad_bias_two = back_some(*pairs)(grad_mixed)
        table = everywhere(table_row(jnp.concatenate([grad_bias, grad_bias_two], 1)))
        own_grad, far_grad, small, kr, _ = weights_some(pairs[0] * 128, back_through)(
            small, *grads, *grads_two
        )
        came_grad = swapped(far_grad, *Y)
        grad_tokens = tokens_call(x, first_gain, grad_middle, own_grad, came_grad)
        small = everywhere(small)

        def scattered(value):
            return lax.psum_scatter(value.astype(f32), "dp", scatter_dimension=0, tiled=True)

        def unit(values, place):
            block, lane = place // 3, place % 3
            return values[width * block : width * (block + 1), UNIT * lane : UNIT * (lane + 1)]

        ups = jnp.concatenate([ka, kb], 0).reshape(blocks, 2 * width, width)
        sum_up = scattered(jnp.concatenate([ups[j, :width] for j in range(blocks)], 1))
        sum_down = scattered(jnp.concatenate([ups[j, width:] for j in range(blocks)], 0))
        sum_out = scattered(out_kept)
        sum_query, sum_keys, sum_values = [
            scattered(
                jnp.concatenate([unit(kq, 2 * i), unit(kq, 2 * i + 1), unit(kr, i)], 1)
            )
            for i in range(3)
        ]
        sum_pair = jnp.concatenate([sum_keys, sum_values], 0).astype(bf16)
        lanes = lax.dynamic_slice_in_dim(small, me * chunk, chunk, 1)
        up_part = lax.dynamic_slice_in_dim(
            small[16 : 16 + blocks].reshape(1, hidden), me * (hidden // shards), hidden // shards, 1
        )
        totals = jnp.sum(small[20:24], 1)
        sum_pair, back = swapped((sum_pair, lanes[7:10]), *Y)
        root_means = jnp.sqrt(totals[:3] / totals[3] + 1e-06).reshape(1, 3)
        sum_keys, sum_values = sum_pair[:chunk].astype(f32), sum_pair[chunk:].astype(f32)

    return (
        output[None],
        grad_tokens[None],
        lanes[5:6] + back[1:2],
        lanes[6:7] + back[2:3],
        sum_query[None],
        lanes[4:5],
        sum_keys[None],
        sum_values[None],
        back[0:1],
        sum_out[None],
        lanes[0:1],
        lanes[1:2],
        lanes[2:3],
        sum_up[None],
        up_part,
        sum_down[None],
        lanes[3:4],
        lax.dynamic_slice_in_dim(table, me * chunk, chunk, 1),
        root_means,
    )


def solution(mesh):
    whole, split = P("stream", None), P("stream", "dp")
    cube, cut = P("stream", None, None), P("stream", "dp", None)
    pages = P(None, "dp", None)
    in_specs = (
        cut, whole, whole, cube, whole, cube, cube, whole, cube, whole, whole, whole,
        cube, whole, cube, whole, whole, pages, pages, P("dp", None, None), cut,
    )
    out_specs = (
        cut, cut, split, split, cut, split, cut, cut, split, cut, split, split, split,
        cut, split, cut, split, split, whole,
    )
    return jax.shard_map(body, mesh=mesh, in_specs=in_specs, out_specs=out_specs, check_vma=False)
```

```python
import functools

import jax
import jax.numpy as jnp
from jax import lax
from jax.experimental import pallas as pl
from jax.experimental.pallas import tpu as pltpu
from jax.sharding import PartitionSpec as P

HEADS = 12
BUCKETS = 32
SMALL = 24

score_scale = 0.125
norm_eps = 1e-05
mask_fill = -1000000000.0
box_step = 32
precise_variant = lax.Precision.HIGHEST
f32 = jnp.float32
bf16 = jnp.bfloat16


def nn(a, b):
    return lax.dot_general(a, b, (((1,), (0,)), ((), ())), preferred_element_type=f32)


def nt(a, b):
    return lax.dot_general(a, b, (((1,), (1,)), ((), ())), preferred_element_type=f32)


def tn(a, b):
    return lax.dot_general(a, b, (((0,), (0,)), ((), ())), preferred_element_type=f32)


def normal_rows(rows):
    centre = rows - jnp.mean(rows, -1, keepdims=True)
    spread = jnp.mean(centre * centre, -1, keepdims=True)
    scale = lax.rsqrt(spread + norm_eps)
    return centre * scale, scale


def params(mib=60):
    return pltpu.CompilerParams(vmem_limit_bytes=mib * 1024 * 1024)


def cost(flops, moved, trans=0, scale=1 / 64):
    return pl.CostEstimate(
        flops=int(flops * scale),
        bytes_accessed=int(moved * scale),
        transcendentals=int(trans * scale),
    )


def full(shape):
    zeros = (0,) * len(shape)
    return pl.BlockSpec(shape, lambda *_: zeros)


def query_kernel(x_ref, gain_ref, shift_ref, w_ref, b_ref, n_ref, q_ref):
    norm, _ = normal_rows(x_ref[...].astype(f32))
    low = (norm * gain_ref[...] + shift_ref[...]).astype(bf16)
    n_ref[...] = low
    query = (nn(low, w_ref[...]) + b_ref[...]).astype(bf16)
    q_ref[...] = (query.astype(f32) * score_scale).astype(bf16)


def query_call(x, gain, shift, weight, bias):
    length, width = x.shape
    tile = 256
    rows = pl.BlockSpec((tile, width), lambda i: (i, 0))
    return pl.pallas_call(
        query_kernel,
        grid=(length // tile,),
        in_specs=[rows, full((1, width)), full((1, width)), full(weight.shape), full((1, width))],
        out_specs=[rows, rows],
        out_shape=[jax.ShapeDtypeStruct(x.shape, bf16)] * 2,
        compiler_params=params(),
        cost_estimate=cost(2 * length * width * width, 6 * length * width + 2 * width * width),
        name="query",
    )(x, gain, shift, weight, bias)


def pair_kernel(me_ref, x_ref, rows_ref, *rest, count):
    pieces, (n_ref, k_ref, v_ref, copy_ref, w_ref) = rest[:count], rest[-5:]
    if count == 4:

        @pl.when(pl.program_id(0) == 0)
        def _():
            low = me_ref[0] & 3
            for place in range(4):
                w_ref[place ^ low] = pieces[place][...]

        weights = w_ref
    else:
        weights = pieces[0]
    half = weights.shape[1]
    copy_ref[...] = x_ref[...]
    norm, _ = normal_rows(x_ref[...].astype(f32))
    low = (norm * rows_ref[0:1, :] + rows_ref[1:2, :]).astype(bf16)
    n_ref[...] = low
    left, right = low[:, :half], low[:, half:]
    k_ref[...] = (nn(left, weights[0]) + nn(right, weights[1])).astype(bf16)
    v_ref[...] = (nn(left, weights[2]) + nn(right, weights[3]) + rows_ref[2:3, :]).astype(bf16)


def pair_call(page, length, me, x, rows, pieces, before):
    page_len, width = x.shape
    tile = 256
    first = page * page_len // tile
    placed = pl.BlockSpec((tile, width), lambda i, *_: (i + first, 0))
    left = pl.BlockSpec(memory_space=pl.ANY)
    weights = (4, width // 2, width)
    out_specs = [placed] * 4
    shapes = [jax.ShapeDtypeStruct((length, width), bf16)] * 4
    scratch = []
    if len(pieces) == 4:
        out_specs = out_specs + [full(weights)]
        shapes = shapes + [jax.ShapeDtypeStruct(weights, bf16)]
    else:
        scratch = [pltpu.VMEM((8, 128), f32)]
    grid_spec = pltpu.PrefetchScalarGridSpec(
        num_scalar_prefetch=1,
        grid=(page_len // tile,),
        in_specs=[
            pl.BlockSpec((tile, width), lambda i, *_: (i, 0)),
            full(rows.shape),
        ]
        + [full(piece.shape) for piece in pieces]
        + [left] * len(before),
        out_specs=out_specs,
        scratch_shapes=scratch,
    )
    return pl.pallas_call(
        functools.partial(pair_kernel, count=len(pieces)),
        grid_spec=grid_spec,
        out_shape=shapes,
        input_output_aliases={3 + len(pieces) + i: i for i in range(len(before))},
        compiler_params=params(),
        cost_estimate=cost(4 * page_len * width * width, 8 * page_len * width),
        name="pair",
    )(me, x, rows, *pieces, *before)


def head_lanes(value, head, head_dim):
    lane = lax.broadcasted_iota(jnp.int32, value.shape, 1)
    mine = (lane >= head * head_dim) & (lane < (head + 1) * head_dim)
    return jnp.where(mine, value, jnp.zeros_like(value))


def picks_kernel(hq_ref, bias_ref, out_ref):
    for pair in range(out_ref.shape[1] // 256):
        both = jnp.concatenate([bias_ref[0, 2 * pair], bias_ref[0, 2 * pair + 1]], 1)
        out_ref[:, 256 * pair : 256 * (pair + 1)] = nn(hq_ref[0], both).astype(bf16)


def picks_call(hot_q, bias):
    pages, page_len = hot_q.shape[0], hot_q.shape[1]
    return pl.pallas_call(
        picks_kernel,
        grid=(pages, 3),
        in_specs=[
            pl.BlockSpec((1, page_len, 64), lambda p, h: (p, 0, 0)),
            pl.BlockSpec((1, 4, 64, 128), lambda p, h: (p, h, 0, 0)),
        ],
        out_specs=pl.BlockSpec((page_len, 512), lambda p, h: (p, h)),
        out_shape=jax.ShapeDtypeStruct((pages * page_len, HEADS * 128), bf16),
        compiler_params=params(),
        cost_estimate=cost(2 * pages * page_len * HEADS * 128 * 64, pages * page_len * HEADS * 256),
        name="picks",
    )(hot_q, bias)


def pair_right(q, picks):
    heads = [head_lanes(q, head, 64) for head in range(2)]
    sides = [
        jnp.concatenate([heads[head], picks[:, 128 * head : 128 * (head + 1)]], 1)
        for head in range(2)
    ]
    return jnp.concatenate(heads, 0), jnp.concatenate(sides, 0)


def attend_kernel(q_ref, k_ref, v_ref, picks_ref, hk_ref, *rest):
    o_ref, lse_ref = rest[-2:]
    page_len = q_ref.shape[0]
    for pair in range(q_ref.shape[1] // 128):
        lanes = slice(128 * pair, 128 * (pair + 1))
        left = jnp.concatenate([k_ref[:, lanes], hk_ref[0]], 1)
        v_turned = v_ref[:, lanes].astype(f32).T.astype(bf16)
        _, right = pair_right(q_ref[:, lanes], picks_ref[:, 256 * pair : 256 * (pair + 1)])
        scores = nt(left, right)
        peak = jnp.max(scores, 0, keepdims=True)
        raised = jnp.exp(scores - peak)
        total = jnp.sum(raised, 0, keepdims=True)
        probs = (raised * (1.0 / total)).astype(bf16)
        lse = peak + jnp.log(total)
        parts = []
        for head in range(2):
            mine = slice(head * page_len, (head + 1) * page_len)
            parts.append(nn(v_turned[head * 64 : (head + 1) * 64], probs[:, mine]))
            lse_ref[0, pair, head : head + 1, :] = lse[:, mine]
        o_ref[:, lanes] = jnp.concatenate(parts, 0).T.astype(bf16)


PAIRS = 2


def attend_specs(page_len, page, first):
    rows = pl.BlockSpec((page_len, 128 * PAIRS), lambda p, h: (p + page, h + first))
    picks = pl.BlockSpec((page_len, 256 * PAIRS), lambda p, h: (p + page, h + first))
    lse = pl.BlockSpec((1, PAIRS, 2, page_len), lambda p, h: (p + page, h + first, 0, 0))

    def hot(*shape):
        return pl.BlockSpec((1,) + shape, lambda p, h: (p + page, 0, 0))

    return rows, picks, lse, hot


def attend_call(page, q, k, v, picks, hot_k, before):
    length, width = q.shape
    pages, page_len = hot_k.shape[0], hot_k.shape[1]
    rows, picks_spec, lse, hot = attend_specs(page_len, page, 0)
    left = pl.BlockSpec(memory_space=pl.ANY)
    return pl.pallas_call(
        attend_kernel,
        grid=(1, width // 128 // PAIRS),
        in_specs=[rows, rows, rows, picks_spec, hot(page_len, 128)] + [left] * len(before),
        out_specs=[rows, lse],
        out_shape=[
            jax.ShapeDtypeStruct((length, width), bf16),
            jax.ShapeDtypeStruct((pages, width // 128, 2, page_len), f32),
        ],
        input_output_aliases={5 + i: i for i in range(len(before))},
        compiler_params=params(),
        cost_estimate=cost(
            16 * page_len * page_len * width,
            8 * page_len * width,
            page_len * page_len * HEADS,
        ),
        name="attend",
    )(q, k, v, picks, hot_k, *before)


def attend_back_kernel(
    q_ref,
    k_ref,
    v_ref,
    picks_ref,
    hq_ref,
    hk_ref,
    hkt_ref,
    lse_ref,
    o_ref,
    do_ref,
    dq_ref,
    dk_ref,
    dv_ref,
    gb_ref,
):
    page_len = q_ref.shape[0]
    row = lax.broadcasted_iota(jnp.int32, (8, 128), 0)
    lane = lax.broadcasted_iota(jnp.int32, (8, 128), 1)
    chooser = (row == lane // 64).astype(bf16)
    for pair in range(q_ref.shape[1] // 128):
        lanes = slice(128 * pair, 128 * (pair + 1))
        k, v, do = k_ref[:, lanes], v_ref[:, lanes], do_ref[:, lanes]
        left = jnp.concatenate([k, hk_ref[0]], 1)
        k_turned = k.astype(f32).T.astype(bf16)
        overlap = do.astype(f32) * o_ref[:, lanes].astype(f32)
        high = overlap.astype(bf16)
        rest = (overlap - high.astype(f32)).astype(bf16)
        delta = nt(chooser, high) + nt(chooser, rest)
        delta = jnp.concatenate([delta[0:1], delta[1:2]], 1)
        lse = jnp.concatenate([lse_ref[0, pair, 0:1, :], lse_ref[0, pair, 1:2, :]], 1)
        queries, right = pair_right(q_ref[:, lanes], picks_ref[:, 256 * pair : 256 * (pair + 1)])
        do_heads = jnp.concatenate([head_lanes(do, head, 64) for head in range(2)], 0)
        probs = jnp.exp(nt(left, right) - lse)
        turn = (probs * (nt(v, do_heads) - delta)).astype(bf16)
        dv_ref[:, lanes] = nn(probs.astype(bf16), do_heads).astype(bf16)
        dk_ref[:, lanes] = nn(turn, queries).astype(bf16)
        parts, sums = [], []
        for head in range(2):
            both = nn(
                jnp.concatenate([k_turned[head * 64 : (head + 1) * 64], hkt_ref[0]], 0),
                turn[:, head * page_len : (head + 1) * page_len],
            )
            parts.append(both[:64])
            sums.append(both[64:])
        dq_ref[:, lanes] = (jnp.concatenate(parts, 0) * score_scale).T.astype(bf16)
        sums = jnp.concatenate(sums, 0)
        high = sums.astype(bf16)
        rest = (sums - high.astype(f32)).astype(bf16)
        grads = nn(jnp.concatenate([high, rest], 0), hq_ref[0])
        grads = grads[:128] + grads[128:]
        for head in range(2):
            gb_ref[0, 2 * pair + head] = grads[64 * head : 64 * (head + 1)]


def attend_back_call(pair, pairs, q, k, v, picks, hot_q, hot_k, hot_kt, lse_in, o, do):
    length, width = q.shape
    pages, page_len = hot_q.shape[0], hot_q.shape[1]
    rows, picks_spec, lse, hot = attend_specs(page_len, 0, pair // PAIRS)
    given = pl.BlockSpec((page_len, 128 * PAIRS), lambda p, h: (p, h))
    grad_bias = pl.BlockSpec((1, 2 * PAIRS, 64, 64), lambda p, h: (p, h, 0, 0))
    wide = jax.ShapeDtypeStruct((length, pairs * 128), bf16)
    return pl.pallas_call(
        attend_back_kernel,
        grid=(pages, pairs // PAIRS),
        in_specs=[
            rows,
            rows,
            rows,
            picks_spec,
            hot(page_len, 64),
            hot(page_len, 128),
            hot(64, page_len),
            lse,
            rows,
            rows,
        ],
        out_specs=[given, given, given, grad_bias],
        out_shape=[wide, wide, wide, jax.ShapeDtypeStruct((pages, 2 * pairs, 64, 64), f32)],
        compiler_params=params(),
        cost_estimate=cost(
            40 * length * page_len * pairs * 128,
            16 * length * pairs * 128,
            length * page_len * 2 * pairs,
            64,
        ),
        name="attend_back",
    )(q, k, v, picks, hot_q, hot_k, hot_kt, lse_in, o, do)


def put_rows(
    scratch, keep, send, me, relative, at, x_step, z_step, lanes=slice(None), source=slice(None)
):
    if not relative:
        keep[pl.ds(at, scratch.shape[0]), lanes] = scratch[:, source].astype(bf16)
        return
    step = scratch.shape[0] // 16
    for place in range(16):
        owner = place ^ me
        rows = scratch[pl.ds(pl.multiple_of(owner * step, step), step), source].astype(bf16)
        target = send if place & 1 else keep
        z = ((place >> 2) & 1) * 2 + (place >> 3)
        low = at + ((place >> 1) & 1) * x_step + z * z_step
        target[pl.ds(pl.multiple_of(low, 16), step), lanes] = rows


def put_quarter(scratch, keep, send, me, relative, at, x_step):
    if not relative:
        keep[pl.ds(at, scratch.shape[0]), :] = scratch[...].astype(bf16)
        return
    step = scratch.shape[0] // 4
    for place in range(4):
        owner = place ^ (me & 3)
        rows = scratch[pl.ds(pl.multiple_of(owner * step, step), step), :].astype(bf16)
        target = send if place & 1 else keep
        target[pl.ds(pl.multiple_of(at + (place >> 1) * x_step, 16), step), :] = rows


def block_shapes(rows, width, relative):
    if relative:
        return (rows // 2, width), (rows // 2, width)
    return (rows, width), (16, 128)


def feed_kernel(me_ref, *rest, first, blocks, relative, tile):
    ins, rest = rest[: 12 if first else 6], rest[12 if first else 8 :]
    if first:
        x_ref, mixed_ref, keep_ref, wo_ref, bo_ref, gain_ref, shift_ref = ins[:7]
        cot_ref, up_ref, upb_ref, down_ref, old_ref = ins[7:]
        middle_ref, n2_ref = rest[:2]
        rest = rest[2:]
    else:
        n2_ref, cot_ref, up_ref, upb_ref, down_ref, old_ref = ins
    act_ref, gh_ref, small_ref, kept_ref, sent_ref, dw_ref = rest[-6:]
    step = pl.program_id(0)
    length = cot_ref.shape[0]

    @pl.when(step == 0)
    def _():
        small_ref[...] = old_ref[...]
        if first:

            @pl.loop(0, length // 256)
            def _(i):
                at = pl.ds(pl.multiple_of(i * 256, 256), 256)
                branch = nn(mixed_ref[at, :], wo_ref[...]) + bo_ref[...]
                middle = x_ref[at, :].astype(f32) + branch
                middle_ref[at, :] = middle
                norm, _ = normal_rows(middle)
                n2_ref[at, :] = (norm * gain_ref[...] + shift_ref[...]).astype(bf16)
                small_ref[21:22, :] += jnp.sum(branch * branch * keep_ref[at, :], 0, keepdims=True)
                small_ref[23:24, :] += jnp.broadcast_to(
                    jnp.sum(keep_ref[at, :], 0, keepdims=True), (1, small_ref.shape[1])
                )

    row = (0 if first else blocks) + 16 + step

    @pl.loop(0, length // tile)
    def _(i):
        at = pl.ds(pl.multiple_of(i * tile, tile), tile)
        hidden = nn(n2_ref[at, :], up_ref[...]) + upb_ref[...]
        slope = nt(cot_ref[at, :], down_ref[...])
        gate = 0.5 * (1.0 + lax.erf(hidden * 0.7071067811865476))
        bell = jnp.exp(hidden * hidden * -0.5) * 0.3989422804014327
        act_ref[at, :] = (hidden * gate).astype(bf16)
        gh = (slope * (gate + hidden * bell)).astype(bf16)
        gh_ref[at, :] = gh
        small_ref[pl.ds(row, 1), :] += jnp.sum(gh.astype(f32), 0, keepdims=True)

    me = me_ref[0]
    width = dw_ref.shape[0]
    up_at, down_at = (step * 48, step * 192) if relative else (step * 2 * width, 0)
    dw_ref[...] = tn(n2_ref[...], gh_ref[...])
    up_steps = (96, 192) if first else (768, 96)
    put_rows(dw_ref, kept_ref, sent_ref, me, relative, up_at, *up_steps)
    dw_ref[...] = tn(act_ref[...], cot_ref[...])
    if relative:
        down_at = down_at + (768 if first else 384)
    else:
        down_at = up_at + width
    put_quarter(dw_ref, kept_ref, sent_ref, me, relative, down_at, 384 if first else 768)


def feed_call(part, parts, me, given, cot, up, upb, down, small, before, relative):
    length, width = cot.shape
    first = part == 0
    hidden = up.shape[1]
    blocks = hidden // width // parts
    start = part * blocks
    whole, row = full((length, width)), full((1, width))
    kept, sent = block_shapes(2 * width * blocks, width, relative)
    shape = jax.ShapeDtypeStruct
    if first:
        specs = [whole, whole, full((length, 1)), full((width, width)), row, row, row]
        outs = [whole, whole]
        shapes = [shape((length, width), f32), shape((length, width), bf16)]
    else:
        specs, outs, shapes = [whole], [], []
    columns = pl.BlockSpec((length, width), lambda j, *_: (0, j + start))
    left = pl.BlockSpec(memory_space=pl.ANY)
    grid_spec = pltpu.PrefetchScalarGridSpec(
        num_scalar_prefetch=1,
        grid=(blocks,),
        in_specs=specs
        + [
            whole,
            pl.BlockSpec((width, width), lambda j, *_: (0, j + start)),
            pl.BlockSpec((1, width), lambda j, *_: (0, j + start)),
            pl.BlockSpec((width, width), lambda j, *_: (j + start, 0)),
            full((SMALL, width)),
        ]
        + [left] * len(before),
        out_specs=outs + [columns, columns, full((SMALL, width)), full(kept), full(sent)],
        scratch_shapes=[pltpu.VMEM((width, width), f32)],
    )
    count = 1 + len(specs) + 5
    return pl.pallas_call(
        functools.partial(
            feed_kernel, first=first, blocks=blocks, relative=relative, tile=512
        ),
        grid_spec=grid_spec,
        out_shape=shapes
        + [
            shape((length, hidden), bf16),
            shape((length, hidden), bf16),
            shape((SMALL, width), f32),
            shape(kept, bf16),
            shape(sent, bf16),
        ],
        input_output_aliases={count + i: i for i in range(len(before))},
        compiler_params=params(),
        cost_estimate=cost(
            8 * length * width * width * blocks, 20 * length * width, 2 * length * width
        ),
        name="feed",
    )(me, *given, cot, up, upb, down, small, *before)


def finish_kernel(
    me_ref,
    act_ref,
    gh_ref,
    up_ref,
    down_ref,
    middle_ref,
    cot_ref,
    keep_ref,
    mixed_ref,
    wo_ref,
    gain_ref,
    downb_ref,
    old_ref,
    out_ref,
    gm_ref,
    gx_ref,
    small_ref,
    kept_ref,
    sent_ref,
    feed_ref,
    gn_ref,
    dw_ref,
    *,
    blocks,
    tile,
    relative,
):
    step = pl.program_id(0)

    @pl.when(step == 0)
    def _():
        small_ref[...] = old_ref[...]
        feed_ref[...] = jnp.zeros_like(feed_ref)
        gn_ref[...] = jnp.zeros_like(gn_ref)

    @pl.when(step < blocks - 1)
    def _():
        feed_ref[...] += nn(act_ref[...], down_ref[...])
        gn_ref[...] += nt(gh_ref[...], up_ref[...])

    @pl.when(step >= blocks - 1)
    def _():
        lows = []
        for i in range(tile // 256):
            here = slice(i * 256, (i + 1) * 256)
            at = pl.ds(pl.multiple_of((step - blocks + 1) * tile + i * 256, 256), 256)
            feed = feed_ref[at, :] + nn(act_ref[at, :], down_ref[...]) + downb_ref[...]
            middle = middle_ref[here, :]
            output = middle + feed
            out_ref[here, :] = output.astype(bf16)
            weight = keep_ref[here, :]
            cot = cot_ref[here, :].astype(f32)
            norm, scale = normal_rows(middle)
            grad = gn_ref[at, :] + nt(gh_ref[at, :], up_ref[...])
            inner = grad * gain_ref[...]
            grad_middle = cot + scale * (
                inner
                - jnp.mean(inner, -1, keepdims=True)
                - norm * jnp.mean(inner * norm, -1, keepdims=True)
            )
            gm_ref[here, :] = grad_middle
            low = grad_middle.astype(bf16)
            gx_ref[here, :] = nt(low, wo_ref[...]).astype(bf16)
            lows.append(low)
            small_ref[0:1, :] += jnp.sum(low.astype(f32), 0, keepdims=True)
            small_ref[1:2, :] += jnp.sum(grad * norm, 0, keepdims=True)
            small_ref[2:3, :] += jnp.sum(grad, 0, keepdims=True)
            small_ref[3:4, :] += jnp.sum(cot, 0, keepdims=True)
            small_ref[20:21, :] += jnp.sum(output * output * weight, 0, keepdims=True)
            small_ref[22:23, :] += jnp.sum(feed * feed * weight, 0, keepdims=True)
        part = tn(mixed_ref[...], jnp.concatenate(lows, 0))

        @pl.when(step == blocks - 1)
        def _():
            dw_ref[...] = part

        @pl.when(step > blocks - 1)
        def _():
            dw_ref[...] += part

    @pl.when(step == pl.num_programs(0) - 1)
    def _():
        put_rows(dw_ref, kept_ref, sent_ref, me_ref[0], relative, 0, 192, 48)


def finish_call(me, acts, up, down, middle, cot, keep, mixed, wo, gain, downb, small, relative):
    length, width = mixed.shape
    blocks = up.shape[1] // width
    end = blocks - 1
    tile = 512
    whole, row = full((length, width)), full((1, width))
    kept, sent = block_shapes(width, width, relative)
    columns = pl.BlockSpec((length, width), lambda j, *_: (0, jnp.minimum(j, end)))

    def tiled(lanes):
        return pl.BlockSpec((tile, lanes), lambda j, *_: (jnp.maximum(j - end, 0), 0))

    rows = tiled(width)
    shape = jax.ShapeDtypeStruct
    grid_spec = pltpu.PrefetchScalarGridSpec(
        num_scalar_prefetch=1,
        grid=(end + length // tile,),
        in_specs=[
            columns,
            columns,
            pl.BlockSpec((width, width), lambda j, *_: (0, jnp.minimum(j, end))),
            pl.BlockSpec((width, width), lambda j, *_: (jnp.minimum(j, end), 0)),
            rows,
            rows,
            tiled(1),
            rows,
            full((width, width)),
            row,
            row,
            full((SMALL, width)),
        ],
        out_specs=[rows, rows, rows, full((SMALL, width)), full(kept), full(sent)],
        scratch_shapes=[
            pltpu.VMEM((length, width), f32),
            pltpu.VMEM((length, width), f32),
            pltpu.VMEM((width, width), f32),
        ],
    )
    return pl.pallas_call(
        functools.partial(finish_kernel, blocks=blocks, tile=tile, relative=relative),
        grid_spec=grid_spec,
        out_shape=[
            shape((length, width), bf16),
            shape((length, width), f32),
            shape((length, width), bf16),
            shape((SMALL, width), f32),
            shape(kept, bf16),
            shape(sent, bf16),
        ],
        compiler_params=params(),
        cost_estimate=cost(4 * length * width * width, 24 * length * width),
        name="finish",
    )(me, *acts, up, down, middle, cot, keep, mixed, wo, gain, downb, small)


UNIT = 256


def units_of(part):
    each = part // UNIT
    places = [(grad, unit) for grad in range(3) for unit in range(each)]
    return [(grad, unit, i // 3, i % 3) for i, (grad, unit) in enumerate(places)]


def spread_small(small, total, chunk):
    sums = jnp.broadcast_to(jnp.sum(small[20:24, :], 1, keepdims=True), (4, chunk))
    for owner in range(16):
        lanes = slice(owner * chunk, (owner + 1) * chunk)
        block, start = owner // 4, (owner % 4) * 4 * chunk
        ups = [
            small[16 + block : 17 + block, start + i * chunk : start + (i + 1) * chunk]
            for i in range(4)
        ]
        piece = jnp.concatenate([small[0:16, lanes], *ups, sums], 0)
        high = piece.astype(bf16).astype(f32)
        whole = jnp.concatenate([high, piece - high], 0)
        for i in range(3):
            total[owner * 16 : (owner + 1) * 16, i * 128 : i * 128 + chunk] = whole[
                i * 16 : (i + 1) * 16
            ]


def weights_kernel(me_ref, n_ref, np_ref, *rest, start, count, relative):
    refs, rest = rest[: 3 * count], rest[3 * count :]
    last = count > 1
    old_ref, rest = rest[0], rest[1:]
    if last:
        x_ref, xp_ref, wq_ref, wp_ref, gq_ref, gp_ref = rest[:6]
        rest = rest[6:]
    small_ref, kept_ref, sent_ref, *totals = rest
    step = pl.program_id(0)
    grads = [ref[...] for ref in refs[-3:]]
    part = grads[0].shape[1]
    lanes = slice(start, start + part)
    sources = [n_ref[...], np_ref[...], np_ref[...]]

    @pl.when(step == 0)
    def _():
        small_ref[...] = old_ref[...]
        for total in totals[:3]:
            total[...] = jnp.zeros_like(total)

    for total, source, grad in zip(totals, sources, grads):
        total[...] += tn(source, grad)
    small_ref[4:5, lanes] += jnp.sum(grads[0].astype(f32), 0, keepdims=True)
    small_ref[7:8, lanes] += jnp.sum(grads[2].astype(f32), 0, keepdims=True)
    if last:
        dq, dk, dv = [jnp.concatenate([ref[...] for ref in refs[i::3]], 1) for i in range(3)]
        width = wq_ref.shape[0]
        far = nt(dk, wp_ref[0:2].reshape(width, width))
        far = far + nt(dv, wp_ref[2:4].reshape(width, width))
        own = nt(dq, wq_ref[...])
        gq_ref[...] = own
        gp_ref[...] = far.astype(bf16)
        norm, _ = normal_rows(x_ref[...].astype(f32))
        far_norm, _ = normal_rows(xp_ref[...].astype(f32))
        small_ref[5:6, :] += jnp.sum(own * norm, 0, keepdims=True)
        small_ref[6:7, :] += jnp.sum(own, 0, keepdims=True)
        small_ref[8:9, :] += jnp.sum(far * far_norm, 0, keepdims=True)
        small_ref[9:10, :] += jnp.sum(far, 0, keepdims=True)

    @pl.when(step == pl.num_programs(0) - 1)
    def _():
        me = me_ref[0]
        z_step = 64 if last else 48 * part // UNIT
        for grad, unit, block, place in units_of(part):
            put_rows(
                totals[grad], kept_ref, sent_ref, me, relative,
                48 * block if relative else 768 * block, 4 * z_step, z_step,
                slice(place * UNIT, (place + 1) * UNIT), slice(unit * UNIT, (unit + 1) * UNIT),
            )
        if last and relative:
            spread = totals[3]
            spread[...] = jnp.zeros_like(spread)
            spread_small(small_ref[...], spread, small_ref.shape[1] // 16)
            put_rows(spread, kept_ref, sent_ref, me, relative, 48, 4 * z_step, z_step)


def weights_call(start, me, n, n_far, grads, small, more, relative):
    length, width = n.shape
    count = len(grads) // 3
    last = count > 1
    part = grads[-1].shape[1]
    tile = 256 if last else 512
    rows = pl.BlockSpec((tile, width), lambda i, *_: (i, 0))
    extra = last and relative
    kept, sent = block_shapes(width * part // UNIT + (256 if extra else 0), width, relative)
    shape = jax.ShapeDtypeStruct
    specs = [rows, rows]
    specs += [pl.BlockSpec((tile, grad.shape[1]), lambda i, *_: (i, 0)) for grad in grads]
    specs += [full((SMALL, width))]
    outs, shapes = [], []
    if last:
        specs += [rows, rows, full(more[2].shape), full(more[3].shape)]
        outs = [rows, rows]
        shapes = [shape((length, width), f32), shape((length, width), bf16)]
    grid_spec = pltpu.PrefetchScalarGridSpec(
        num_scalar_prefetch=1,
        grid=(length // tile,),
        in_specs=specs,
        out_specs=outs + [full((SMALL, width)), full(kept), full(sent)],
        scratch_shapes=[pltpu.VMEM((width, part), f32)] * 3
        + ([pltpu.VMEM((256, width), f32)] if extra else []),
    )
    return pl.pallas_call(
        functools.partial(weights_kernel, start=start, count=count, relative=relative),
        grid_spec=grid_spec,
        out_shape=shapes
        + [shape((SMALL, width), f32), shape(kept, bf16), shape(sent, bf16)],
        compiler_params=params(),
        cost_estimate=cost(6 * length * width * part, 24 * length * width),
        name="weights",
    )(me, n, n_far, *grads, small, *more)


def tokens_kernel(x_ref, gain_ref, gm_ref, gq_ref, gf_ref, out_ref):
    norm, scale = normal_rows(x_ref[...].astype(f32))
    inner = (gq_ref[...] + gf_ref[...].astype(f32)) * gain_ref[...]
    out_ref[...] = gm_ref[...] + scale * (
        inner
        - jnp.mean(inner, -1, keepdims=True)
        - norm * jnp.mean(inner * norm, -1, keepdims=True)
    )


def tokens_call(x, gain, gm, gq, gf):
    length, width = x.shape
    rows = pl.BlockSpec((256, width), lambda i: (i, 0))
    return pl.pallas_call(
        tokens_kernel,
        grid=(length // 256,),
        in_specs=[rows, full((1, width)), rows, rows, rows],
        out_specs=rows,
        out_shape=jax.ShapeDtypeStruct((length, width), f32),
        compiler_params=params(),
        cost_estimate=cost(20 * length * width, 16 * length * width),
        name="tokens",
    )(x, gain, gm, gq, gf)


def swapped(value, axis, mask):
    pairs = [(source, source ^ mask) for source in range(lax.axis_size(axis))]
    return lax.ppermute(value, axis, pairs)


def added(a, b, dtype=bf16):
    return (a.astype(f32) + b.astype(f32)).astype(dtype)


def together(kernel, inputs, moves=(), later=(), due=()):
    count = len(moves)
    moves = list(moves) + list(later)
    inputs, values = lax.optimization_barrier((inputs, [value for value, _, _ in moves]))
    came = [swapped(value, *way[1:]) for value, way in zip(values, moves)]
    results = kernel(*inputs) if kernel else []
    results, now, due = lax.optimization_barrier((results, came[:count], list(due)))
    return results, now, came[count:], due


def total(*values):
    return functools.reduce(jnp.add, [value.astype(f32) for value in values])


def quads(*values):
    values = [value.reshape(4, -1, value.shape[-1]) for value in values]
    return jnp.concatenate(values, 1).reshape(-1, values[0].shape[-1])


def everywhere(value):
    mask = 1
    while mask < lax.axis_size("dp"):
        value = value + swapped(value, "dp", mask)
        mask *= 2
    return value


def pick_stream(pair, stream):
    return jnp.where(stream == 0, pair[0], pair[1])


def box_onehots(seg_boxes, buckets):
    half = buckets // 2
    levels = jnp.arange(buckets, dtype=jnp.int32)
    centre_x = (seg_boxes[..., 0] + seg_boxes[..., 2]) // 2
    centre_y = (seg_boxes[..., 1] + seg_boxes[..., 3]) // 2
    step_x = (
        jnp.clip((centre_x[:, None, :] - centre_x[:, :, None]) // box_step, -half, half - 1) + half
    )
    step_y = (
        jnp.clip((centre_y[:, None, :] - centre_y[:, :, None]) // box_step, -half, half - 1) + half
    )
    return (
        (step_x[..., None] == levels).astype(jnp.float32),
        (step_y[..., None] == levels).astype(jnp.float32),
    )


def body(
    tokens,
    first_gain,
    first_shift,
    query_weight,
    query_bias,
    key_weight,
    value_weight,
    value_bias,
    out_weight,
    out_bias,
    second_gain,
    second_shift,
    up_weight,
    up_bias,
    down_weight,
    down_bias,
    box_table,
    segments,
    validity,
    seg_boxes,
    cotangent,
):
    stream = lax.axis_index("stream")
    me = lax.axis_index("dp")
    shards = lax.axis_size("dp")
    width = tokens.shape[2]
    hidden = up_weight.shape[2]
    pages, page_len = segments.shape[1], segments.shape[2]
    length = pages * page_len
    relative = shards == 16
    me_ref = me.reshape(1).astype(jnp.int32)
    x = tokens[0]

    own_seg = pick_stream(segments, stream)
    far_seg = pick_stream(segments, 1 - stream)
    own_keep = pick_stream(validity, stream)
    far_keep = pick_stream(validity, 1 - stream)
    levels = jnp.arange(64, dtype=jnp.int32)
    hot_q = (own_seg[:, :, None] == levels).astype(bf16)
    hot_kt = (far_seg[:, None, :] == levels[None, :, None]).astype(bf16)
    wide_levels = jnp.arange(128, dtype=jnp.int32)
    hot_k = jnp.where(
        wide_levels == 64,
        jnp.where(far_keep[:, :, None] > 0, 0.0, mask_fill),
        (far_seg[:, :, None] == wide_levels).astype(f32),
    ).astype(bf16)
    hot_x, hot_y = box_onehots(seg_boxes, BUCKETS)
    tables = box_table[0].reshape(2, HEADS, BUCKETS)
    seg_bias = (
        jnp.einsum("pabn,hn->phab", hot_x, tables[0], precision=precise_variant)
        + jnp.einsum("pabn,hn->phab", hot_y, tables[1], precision=precise_variant)
    ).astype(bf16)
    ones = (jnp.arange(64) == 0).astype(bf16)
    seg_bias = jnp.concatenate([seg_bias, jnp.broadcast_to(ones, seg_bias.shape)], -1)

    keep_column = own_keep.reshape(length, 1).astype(f32)
    blocks, chunk = hidden // width, width // shards
    cot = cotangent[0]
    Y, CORE, X, Z1, Z2 = ("stream", 1), ("dp", 1), ("dp", 2), ("dp", 4), ("dp", 8)

    low = me & 3
    half = width // 2

    def quarter(weight):
        return lax.dynamic_slice_in_dim(weight[0], (low & 1) * half, half, 0)

    piece = jnp.where(low < 2, quarter(key_weight), quarter(value_weight))
    vectors = jnp.concatenate([first_gain, first_shift, value_bias], 0)
    (normed, query), (piece, far_rows), _, _ = together(
        query_call,
        (x, first_gain, first_shift, query_weight[0], query_bias),
        [(piece, *Y), (vectors, *Y)],
    )
    page_x = [x[page * page_len : (page + 1) * page_len] for page in range(pages)]
    (picks, hot_q, hot_k), (x_piece, core_piece, came_x), _, _ = together(
        lambda bias, hot_q, hot_k: (picks_call(hot_q, bias), hot_q, hot_k),
        (seg_bias, hot_q, hot_k),
        [(piece, *X), (piece, *CORE), (page_x[0], *Y)],
    )
    far_pages = [came_x]
    pieces = [piece, core_piece, x_piece, swapped(x_piece, *CORE)]
    far, mixing = (), ()
    for page in range(pages):

        def page_step(came, pieces, far, mixing, page=page):
            far = pair_call(page, length, me_ref, came, far_rows, pieces, far)
            return far, attend_call(page, query, far[1], far[2], picks, hot_k, mixing)

        moves = [(page_x[page + 1], *Y)] if page + 1 < pages else []
        (result, mixing), came, _, _ = together(
            page_step, (far_pages[page], pieces, tuple(far), tuple(mixing)), moves
        )
        far = result[:4]
        if page == 0:
            pieces = [result[4]]
        far_pages += came
    far_normed, keys, value_rows, far_x = far
    far_weights = pieces[0]
    mixed, log_total = mixing

    small = jnp.zeros((SMALL, width), f32)

    def feed_first(mixed, small):
        return feed_call(
            0, 2, me_ref,
            (x, mixed, keep_column, out_weight[0], out_bias, second_gain, second_shift),
            cot, up_weight[0], up_bias, down_weight[0], small, (), relative,
        )

    def feed_second(n2, small, *acts):
        return feed_call(
            1, 2, me_ref, (n2,), cot, up_weight[0], up_bias, down_weight[0], small, acts, relative
        )

    def finish(middle, small, *acts):
        return finish_call(
            me_ref, acts, up_weight[0], down_weight[0], middle, cot, keep_column, mixed,
            out_weight[0], second_gain, down_bias, small, relative,
        )

    def back_some(pair, pairs):
        def call(grad_mixed):
            return attend_back_call(
                pair, pairs, query, keys, value_rows, picks, hot_q, hot_k, hot_kt, log_total,
                mixed, grad_mixed,
            )

        return call

    def weights_some(start, more=()):
        def call(small, *grads):
            return weights_call(start, me_ref, normed, far_normed, grads, small, more, relative)

        return call

    back_through = (x, far_x, query_weight[0], far_weights)
    pairs = (4, width // 128 - 4)

    def table_row(grad_bias):
        return jnp.concatenate(
            [
                jnp.einsum("pabn,phba->hn", hot_x, grad_bias, precision=precise_variant),
                jnp.einsum("pabn,phba->hn", hot_y, grad_bias, precision=precise_variant),
            ],
            0,
        ).reshape(1, -1)

    if relative:
        z_low, z_high = (me >> 2) & 1, me >> 3

        def downs(pair):
            one, other = pair[:192], pair[192:]
            return jnp.where(z_low, other, one), jnp.where(z_low, one, other)

        (middle, normed_two, act, gh, small, ka, sa), _, _, _ = together(
            feed_first, (mixed, small)
        )
        (act, gh, small, kb, sb), (ca,), _, _ = together(
            feed_second, (normed_two, small, act, gh), [(sa, *CORE)]
        )
        up_go, down_go = added(ka[384:768], ca[384:768]), added(ka[1152:], ca[1152:])
        (output, grad_middle, grad_mixed, small, ko, so), (cb, x0, z0), _, _ = together(
            finish,
            (middle, small, act, gh),
            [(sb, *CORE), (down_go, *X), (up_go, *Z1)],
        )
        up_go = total(ka[192:384], ca[192:384], z0[192:]).astype(bf16)
        up_stay = total(ka[:192], ca[:192], z0[:192])
        go = added(kb[768:], cb[768:])
        (*grads, grad_bias), (co, z0), (x2,), _ = together(
            back_some(0, pairs[0]), (grad_mixed,), [(so, *CORE), (up_go, *Z2)], [(go, *X)]
        )
        one = total(ka[768:1152], ca[768:1152], x0).astype(bf16)
        one_keep, one_go = downs(one)
        up_low = total(up_stay, z0)
        go = jnp.concatenate([up_low[96:].astype(bf16), added(ko[192:], co[192:])], 0)
        (small, kq, sq), (z0,), (xo,), (x2,) = together(
            weights_some(0), (small, *grads), [(one_go, *Z1)], [(go, *X)], [x2]
        )
        down_one = added(one_keep, z0)
        two = total(kb[:768], cb[:768], x2).astype(bf16)
        two_keep, two_go = downs(two[384:])
        (*grads_two, grad_bias_two), (cq, z1), _, (xo,) = together(
            back_some(*pairs), (grad_mixed,), [(sq, *CORE), (two_go, *Z1)], [], [xo]
        )
        down_two = added(two_keep, z1)
        down_stay = jnp.where(z_high, down_two, down_one)
        down_go = jnp.where(z_high, down_one, down_two)
        go = added(kq[384:], cq[384:])
        rest = quads(two[:384], total(ko[:192], co[:192], xo[96:]).astype(bf16))
        (own_grad, far_grad, small, kr, sr), (xq, z1), (z3,), _ = together(
            weights_some(pairs[0] * 128, back_through),
            (small, *grads, *grads_two),
            [(go, *X), (rest[288:], *Z1)],
            [(down_go, *Z2)],
        )
        _, (cr,), (came_grad,), _ = together(None, (), [(sr, *CORE)], [(far_grad, *Y)])
        go, grad_bias, xq, z1 = lax.optimization_barrier(
            (added(kr[256:], cr[256:]), (grad_bias, grad_bias_two), xq, z1)
        )
        rest_go = added(rest[144:288], z1[144:])
        group_go = total(kq[192:384], cq[192:384], xq[192:]).astype(bf16)
        z4, z2 = swapped(group_go, *Z1), swapped(rest_go, *Z2)
        table = table_row(jnp.concatenate(grad_bias, 1))
        table = table + swapped(table, *CORE)
        _, (xr,), _, (z4, table) = together(None, (), [(go, *X)], [], [z4, table])
        r_go = total(kr[128:256], cr[128:256], xr[128:]).astype(bf16)
        group_go = total(kq[96:192], cq[96:192], xq[96:192], z4[96:]).astype(bf16)
        z5 = swapped(group_go, *Z2)
        _, (z1r, came), _, (z3,) = together(None, (), [(r_go, *Z1), (table, *X)], [], [z3])
        table = table + came
        r_go = total(kr[64:128], cr[64:128], xr[64:128], z1r[64:]).astype(bf16)
        _, (z2r, came), _, (z2, z5, came_grad) = together(
            None, (), [(r_go, *Z2), (table, *Z1)], [], [z2, z5, came_grad]
        )
        table = table + came
        up_low = total(up_low[:96], xo[:96])
        sum_down = total(down_stay, z3)
        rest = total(rest[:144], z1[:144], z2)
        first = total(kq[:96], cq[:96], xq[:96], z4[:96], z5)
        last = total(kr[:64], cr[:64], xr[:64], z1r[:64], z2r)
        sum_up = jnp.concatenate([up_low[:48], up_low[48:], rest[:48], rest[48:96]], 1)
        sum_out = rest[96:]

        def lanes_of(spread):
            pieces = [spread[:, 128 * i : 128 * i + chunk] for i in range(3)]
            pieces = jnp.concatenate(pieces, 0)
            return pieces[:SMALL] + pieces[SMALL:]

        def unit(values, place):
            block, lane = place // 3, place % 3
            return values[48 * block : 48 * block + 48, UNIT * lane : UNIT * (lane + 1)]

        def joined(first, last, i):
            return jnp.concatenate(
                [unit(first, 2 * i), unit(first, 2 * i + 1), unit(last, i)], 1
            )

        def ending(*given):
            lanes = lanes_of(last[48:])
            totals = lanes[20:24, 0]
            root_means = jnp.sqrt(totals[:3] / totals[3] + 1e-06).reshape(1, 3)
            up_part = lanes[16:20].reshape(1, hidden // shards)
            grad_tokens = tokens_call(*given)
            sum_query = joined(first, last, 0)
            return grad_tokens, lanes, root_means, up_part, sum_query, sum_up, sum_out, sum_down

        ended, (far_first, far_last, came), _, _ = together(
            ending,
            (x, first_gain, grad_middle, own_grad, came_grad),
            [(first.astype(bf16), *Y), (last, *Y), (table, *Z2)],
        )
        grad_tokens, lanes, root_means, up_part, sum_query, sum_up, sum_out, sum_down = ended
        table = table + came
        back = lanes_of(far_last[48:])[7:10]
        far_first = far_first.astype(f32)
        sum_keys, sum_values = joined(far_first, far_last, 1), joined(far_first, far_last, 2)
    else:
        middle, normed_two, act, gh, small, ka, _ = feed_first(mixed, small)
        act, gh, small, kb, _ = feed_second(normed_two, small, act, gh)
        output, grad_middle, grad_mixed, small, out_kept, _ = finish(middle, small, act, gh)
        *grads, grad_bias = back_some(0, pairs[0])(grad_mixed)
        small, kq, _ = weights_some(0)(small, *grads)
        *grads_two, grad_bias_two = back_some(*pairs)(grad_mixed)
        table = everywhere(table_row(jnp.concatenate([grad_bias, grad_bias_two], 1)))
        own_grad, far_grad, small, kr, _ = weights_some(pairs[0] * 128, back_through)(
            small, *grads, *grads_two
        )
        came_grad = swapped(far_grad, *Y)
        grad_tokens = tokens_call(x, first_gain, grad_middle, own_grad, came_grad)
        small = everywhere(small)

        def scattered(value):
            return lax.psum_scatter(value.astype(f32), "dp", scatter_dimension=0, tiled=True)

        def unit(values, place):
            block, lane = place // 3, place % 3
            return values[width * block : width * (block + 1), UNIT * lane : UNIT * (lane + 1)]

        ups = jnp.concatenate([ka, kb], 0).reshape(blocks, 2 * width, width)
        sum_up = scattered(jnp.concatenate([ups[j, :width] for j in range(blocks)], 1))
        sum_down = scattered(jnp.concatenate([ups[j, width:] for j in range(blocks)], 0))
        sum_out = scattered(out_kept)
        sum_query, sum_keys, sum_values = [
            scattered(
                jnp.concatenate([unit(kq, 2 * i), unit(kq, 2 * i + 1), unit(kr, i)], 1)
            )
            for i in range(3)
        ]
        sum_pair = jnp.concatenate([sum_keys, sum_values], 0).astype(bf16)
        lanes = lax.dynamic_slice_in_dim(small, me * chunk, chunk, 1)
        up_part = lax.dynamic_slice_in_dim(
            small[16 : 16 + blocks].reshape(1, hidden), me * (hidden // shards), hidden // shards, 1
        )
        totals = jnp.sum(small[20:24], 1)
        sum_pair, back = swapped((sum_pair, lanes[7:10]), *Y)
        root_means = jnp.sqrt(totals[:3] / totals[3] + 1e-06).reshape(1, 3)
        sum_keys, sum_values = sum_pair[:chunk].astype(f32), sum_pair[chunk:].astype(f32)

    return (
        output[None],
        grad_tokens[None],
        lanes[5:6] + back[1:2],
        lanes[6:7] + back[2:3],
        sum_query[None],
        lanes[4:5],
        sum_keys[None],
        sum_values[None],
        back[0:1],
        sum_out[None],
        lanes[0:1],
        lanes[1:2],
        lanes[2:3],
        sum_up[None],
        up_part,
        sum_down[None],
        lanes[3:4],
        lax.dynamic_slice_in_dim(table, me * chunk, chunk, 1),
        root_means,
    )


def solution(mesh):
    whole, split = P("stream", None), P("stream", "dp")
    cube, cut = P("stream", None, None), P("stream", "dp", None)
    pages = P(None, "dp", None)
    in_specs = (
        cut, whole, whole, cube, whole, cube, cube, whole, cube, whole, whole, whole,
        cube, whole, cube, whole, whole, pages, pages, P("dp", None, None), cut,
    )
    out_specs = (
        cut, cut, split, split, cut, split, cut, cut, split, cut, split, split, split,
        cut, split, cut, split, split, whole,
    )
    return jax.shard_map(body, mesh=mesh, in_specs=in_specs, out_specs=out_specs, check_vma=False)
```

```python
import functools

import jax
import jax.numpy as jnp
from jax import lax
from jax.experimental import pallas as pl
from jax.experimental.pallas import tpu as pltpu
from jax.sharding import PartitionSpec as P

HEADS = 12
BUCKETS = 32
SMALL = 24

score_scale = 0.125
norm_eps = 1e-05
mask_fill = -1000000000.0
box_step = 32
precise_variant = lax.Precision.HIGHEST
f32 = jnp.float32
bf16 = jnp.bfloat16


def nn(a, b):
    return lax.dot_general(a, b, (((1,), (0,)), ((), ())), preferred_element_type=f32)


def nt(a, b):
    return lax.dot_general(a, b, (((1,), (1,)), ((), ())), preferred_element_type=f32)


def tn(a, b):
    return lax.dot_general(a, b, (((0,), (0,)), ((), ())), preferred_element_type=f32)


def normal_rows(rows):
    centre = rows - jnp.mean(rows, -1, keepdims=True)
    spread = jnp.mean(centre * centre, -1, keepdims=True)
    scale = lax.rsqrt(spread + norm_eps)
    return centre * scale, scale


def params(mib=60):
    return pltpu.CompilerParams(vmem_limit_bytes=mib * 1024 * 1024)


def cost(flops, moved, trans=0, scale=1 / 64):
    return pl.CostEstimate(
        flops=int(flops * scale),
        bytes_accessed=int(moved * scale),
        transcendentals=int(trans * scale),
    )


def full(shape):
    zeros = (0,) * len(shape)
    return pl.BlockSpec(shape, lambda *_: zeros)


def query_kernel(x_ref, gain_ref, shift_ref, w_ref, b_ref, n_ref, q_ref):
    norm, _ = normal_rows(x_ref[...].astype(f32))
    low = (norm * gain_ref[...] + shift_ref[...]).astype(bf16)
    n_ref[...] = low
    query = (nn(low, w_ref[...]) + b_ref[...]).astype(bf16)
    q_ref[...] = (query.astype(f32) * score_scale).astype(bf16)


def query_call(x, gain, shift, weight, bias):
    length, width = x.shape
    tile = 256
    rows = pl.BlockSpec((tile, width), lambda i: (i, 0))
    return pl.pallas_call(
        query_kernel,
        grid=(length // tile,),
        in_specs=[rows, full((1, width)), full((1, width)), full(weight.shape), full((1, width))],
        out_specs=[rows, rows],
        out_shape=[jax.ShapeDtypeStruct(x.shape, bf16)] * 2,
        compiler_params=params(),
        cost_estimate=cost(2 * length * width * width, 6 * length * width + 2 * width * width),
        name="query",
    )(x, gain, shift, weight, bias)


def pair_kernel(me_ref, x_ref, rows_ref, *rest, count):
    pieces, (n_ref, k_ref, v_ref, copy_ref, w_ref) = rest[:count], rest[-5:]
    if count == 4:

        @pl.when(pl.program_id(0) == 0)
        def _():
            low = me_ref[0] & 3
            for place in range(4):
                w_ref[place ^ low] = pieces[place][...]

        weights = w_ref
    else:
        weights = pieces[0]
    half = weights.shape[1]
    copy_ref[...] = x_ref[...]
    norm, _ = normal_rows(x_ref[...].astype(f32))
    low = (norm * rows_ref[0:1, :] + rows_ref[1:2, :]).astype(bf16)
    n_ref[...] = low
    left, right = low[:, :half], low[:, half:]
    k_ref[...] = (nn(left, weights[0]) + nn(right, weights[1])).astype(bf16)
    v_ref[...] = (nn(left, weights[2]) + nn(right, weights[3]) + rows_ref[2:3, :]).astype(bf16)


def pair_call(page, length, me, x, rows, pieces, before):
    page_len, width = x.shape
    tile = 256
    first = page * page_len // tile
    placed = pl.BlockSpec((tile, width), lambda i, *_: (i + first, 0))
    left = pl.BlockSpec(memory_space=pl.ANY)
    weights = (4, width // 2, width)
    out_specs = [placed] * 4
    shapes = [jax.ShapeDtypeStruct((length, width), bf16)] * 4
    scratch = []
    if len(pieces) == 4:
        out_specs = out_specs + [full(weights)]
        shapes = shapes + [jax.ShapeDtypeStruct(weights, bf16)]
    else:
        scratch = [pltpu.VMEM((8, 128), f32)]
    grid_spec = pltpu.PrefetchScalarGridSpec(
        num_scalar_prefetch=1,
        grid=(page_len // tile,),
        in_specs=[
            pl.BlockSpec((tile, width), lambda i, *_: (i, 0)),
            full(rows.shape),
        ]
        + [full(piece.shape) for piece in pieces]
        + [left] * len(before),
        out_specs=out_specs,
        scratch_shapes=scratch,
    )
    return pl.pallas_call(
        functools.partial(pair_kernel, count=len(pieces)),
        grid_spec=grid_spec,
        out_shape=shapes,
        input_output_aliases={3 + len(pieces) + i: i for i in range(len(before))},
        compiler_params=params(),
        cost_estimate=cost(4 * page_len * width * width, 8 * page_len * width),
        name="pair",
    )(me, x, rows, *pieces, *before)


def head_lanes(value, head, head_dim):
    lane = lax.broadcasted_iota(jnp.int32, value.shape, 1)
    mine = (lane >= head * head_dim) & (lane < (head + 1) * head_dim)
    return jnp.where(mine, value, jnp.zeros_like(value))


def picks_kernel(hq_ref, bias_ref, out_ref):
    for pair in range(out_ref.shape[1] // 256):
        both = jnp.concatenate([bias_ref[0, 2 * pair], bias_ref[0, 2 * pair + 1]], 1)
        out_ref[:, 256 * pair : 256 * (pair + 1)] = nn(hq_ref[0], both).astype(bf16)


def picks_call(hot_q, bias):
    pages, page_len = hot_q.shape[0], hot_q.shape[1]
    return pl.pallas_call(
        picks_kernel,
        grid=(pages, 3),
        in_specs=[
            pl.BlockSpec((1, page_len, 64), lambda p, h: (p, 0, 0)),
            pl.BlockSpec((1, 4, 64, 128), lambda p, h: (p, h, 0, 0)),
        ],
        out_specs=pl.BlockSpec((page_len, 512), lambda p, h: (p, h)),
        out_shape=jax.ShapeDtypeStruct((pages * page_len, HEADS * 128), bf16),
        compiler_params=params(),
        cost_estimate=cost(2 * pages * page_len * HEADS * 128 * 64, pages * page_len * HEADS * 256),
        name="picks",
    )(hot_q, bias)


def pair_right(q, picks):
    heads = [head_lanes(q, head, 64) for head in range(2)]
    sides = [
        jnp.concatenate([heads[head], picks[:, 128 * head : 128 * (head + 1)]], 1)
        for head in range(2)
    ]
    return jnp.concatenate(heads, 0), jnp.concatenate(sides, 0)


def attend_kernel(q_ref, k_ref, v_ref, picks_ref, hk_ref, *rest):
    o_ref, lse_ref = rest[-2:]
    page_len = q_ref.shape[0]
    for pair in range(q_ref.shape[1] // 128):
        lanes = slice(128 * pair, 128 * (pair + 1))
        left = jnp.concatenate([k_ref[:, lanes], hk_ref[0]], 1)
        v_turned = v_ref[:, lanes].astype(f32).T.astype(bf16)
        _, right = pair_right(q_ref[:, lanes], picks_ref[:, 256 * pair : 256 * (pair + 1)])
        scores = nt(left, right)
        peak = jnp.max(scores, 0, keepdims=True)
        raised = jnp.exp(scores - peak)
        total = jnp.sum(raised, 0, keepdims=True)
        probs = (raised * (1.0 / total)).astype(bf16)
        lse = peak + jnp.log(total)
        parts = []
        for head in range(2):
            mine = slice(head * page_len, (head + 1) * page_len)
            parts.append(nn(v_turned[head * 64 : (head + 1) * 64], probs[:, mine]))
            lse_ref[0, pair, head : head + 1, :] = lse[:, mine]
        o_ref[:, lanes] = jnp.concatenate(parts, 0).T.astype(bf16)


PAIRS = 2


def attend_specs(page_len, page, first):
    rows = pl.BlockSpec((page_len, 128 * PAIRS), lambda p, h: (p + page, h + first))
    picks = pl.BlockSpec((page_len, 256 * PAIRS), lambda p, h: (p + page, h + first))
    lse = pl.BlockSpec((1, PAIRS, 2, page_len), lambda p, h: (p + page, h + first, 0, 0))

    def hot(*shape):
        return pl.BlockSpec((1,) + shape, lambda p, h: (p + page, 0, 0))

    return rows, picks, lse, hot


def attend_call(page, q, k, v, picks, hot_k, before):
    length, width = q.shape
    pages, page_len = hot_k.shape[0], hot_k.shape[1]
    rows, picks_spec, lse, hot = attend_specs(page_len, page, 0)
    left = pl.BlockSpec(memory_space=pl.ANY)
    return pl.pallas_call(
        attend_kernel,
        grid=(1, width // 128 // PAIRS),
        in_specs=[rows, rows, rows, picks_spec, hot(page_len, 128)] + [left] * len(before),
        out_specs=[rows, lse],
        out_shape=[
            jax.ShapeDtypeStruct((length, width), bf16),
            jax.ShapeDtypeStruct((pages, width // 128, 2, page_len), f32),
        ],
        input_output_aliases={5 + i: i for i in range(len(before))},
        compiler_params=params(),
        cost_estimate=cost(
            16 * page_len * page_len * width,
            8 * page_len * width,
            page_len * page_len * HEADS,
        ),
        name="attend",
    )(q, k, v, picks, hot_k, *before)


def attend_back_kernel(
    q_ref,
    k_ref,
    v_ref,
    picks_ref,
    hq_ref,
    hk_ref,
    hkt_ref,
    lse_ref,
    o_ref,
    do_ref,
    dq_ref,
    dk_ref,
    dv_ref,
    gb_ref,
):
    page_len = q_ref.shape[0]
    row = lax.broadcasted_iota(jnp.int32, (8, 128), 0)
    lane = lax.broadcasted_iota(jnp.int32, (8, 128), 1)
    chooser = (row == lane // 64).astype(bf16)
    for pair in range(q_ref.shape[1] // 128):
        lanes = slice(128 * pair, 128 * (pair + 1))
        k, v, do = k_ref[:, lanes], v_ref[:, lanes], do_ref[:, lanes]
        left = jnp.concatenate([k, hk_ref[0]], 1)
        k_turned = k.astype(f32).T.astype(bf16)
        overlap = do.astype(f32) * o_ref[:, lanes].astype(f32)
        high = overlap.astype(bf16)
        rest = (overlap - high.astype(f32)).astype(bf16)
        delta = nt(chooser, high) + nt(chooser, rest)
        delta = jnp.concatenate([delta[0:1], delta[1:2]], 1)
        lse = jnp.concatenate([lse_ref[0, pair, 0:1, :], lse_ref[0, pair, 1:2, :]], 1)
        queries, right = pair_right(q_ref[:, lanes], picks_ref[:, 256 * pair : 256 * (pair + 1)])
        do_heads = jnp.concatenate([head_lanes(do, head, 64) for head in range(2)], 0)
        probs = jnp.exp(nt(left, right) - lse)
        turn = (probs * (nt(v, do_heads) - delta)).astype(bf16)
        dv_ref[:, lanes] = nn(probs.astype(bf16), do_heads).astype(bf16)
        dk_ref[:, lanes] = nn(turn, queries).astype(bf16)
        parts, sums = [], []
        for head in range(2):
            both = nn(
                jnp.concatenate([k_turned[head * 64 : (head + 1) * 64], hkt_ref[0]], 0),
                turn[:, head * page_len : (head + 1) * page_len],
            )
            parts.append(both[:64])
            sums.append(both[64:])
        dq_ref[:, lanes] = (jnp.concatenate(parts, 0) * score_scale).T.astype(bf16)
        sums = jnp.concatenate(sums, 0)
        high = sums.astype(bf16)
        rest = (sums - high.astype(f32)).astype(bf16)
        grads = nn(jnp.concatenate([high, rest], 0), hq_ref[0])
        grads = grads[:128] + grads[128:]
        for head in range(2):
            gb_ref[0, 2 * pair + head] = grads[64 * head : 64 * (head + 1)]


def attend_back_call(pair, pairs, q, k, v, picks, hot_q, hot_k, hot_kt, lse_in, o, do):
    length, width = q.shape
    pages, page_len = hot_q.shape[0], hot_q.shape[1]
    rows, picks_spec, lse, hot = attend_specs(page_len, 0, pair // PAIRS)
    given = pl.BlockSpec((page_len, 128 * PAIRS), lambda p, h: (p, h))
    grad_bias = pl.BlockSpec((1, 2 * PAIRS, 64, 64), lambda p, h: (p, h, 0, 0))
    wide = jax.ShapeDtypeStruct((length, pairs * 128), bf16)
    return pl.pallas_call(
        attend_back_kernel,
        grid=(pages, pairs // PAIRS),
        in_specs=[
            rows,
            rows,
            rows,
            picks_spec,
            hot(page_len, 64),
            hot(page_len, 128),
            hot(64, page_len),
            lse,
            rows,
            rows,
        ],
        out_specs=[given, given, given, grad_bias],
        out_shape=[wide, wide, wide, jax.ShapeDtypeStruct((pages, 2 * pairs, 64, 64), f32)],
        compiler_params=params(),
        cost_estimate=cost(
            40 * length * page_len * pairs * 128,
            16 * length * pairs * 128,
            length * page_len * 2 * pairs,
            64,
        ),
        name="attend_back",
    )(q, k, v, picks, hot_q, hot_k, hot_kt, lse_in, o, do)


def put_rows(
    scratch, keep, send, me, relative, at, x_step, z_step, lanes=slice(None), source=slice(None)
):
    if not relative:
        keep[pl.ds(at, scratch.shape[0]), lanes] = scratch[:, source].astype(bf16)
        return
    step = scratch.shape[0] // 16
    for place in range(16):
        owner = place ^ me
        rows = scratch[pl.ds(pl.multiple_of(owner * step, step), step), source].astype(bf16)
        target = send if place & 1 else keep
        z = ((place >> 2) & 1) * 2 + (place >> 3)
        low = at + ((place >> 1) & 1) * x_step + z * z_step
        target[pl.ds(pl.multiple_of(low, 16), step), lanes] = rows


def put_quarter(scratch, keep, send, me, relative, at, x_step):
    if not relative:
        keep[pl.ds(at, scratch.shape[0]), :] = scratch[...].astype(bf16)
        return
    step = scratch.shape[0] // 4
    for place in range(4):
        owner = place ^ (me & 3)
        rows = scratch[pl.ds(pl.multiple_of(owner * step, step), step), :].astype(bf16)
        target = send if place & 1 else keep
        target[pl.ds(pl.multiple_of(at + (place >> 1) * x_step, 16), step), :] = rows


def block_shapes(rows, width, relative):
    if relative:
        return (rows // 2, width), (rows // 2, width)
    return (rows, width), (16, 128)


def feed_kernel(me_ref, *rest, first, blocks, relative, tile):
    ins, rest = rest[: 12 if first else 6], rest[12 if first else 8 :]
    if first:
        x_ref, mixed_ref, keep_ref, wo_ref, bo_ref, gain_ref, shift_ref = ins[:7]
        cot_ref, up_ref, upb_ref, down_ref, old_ref = ins[7:]
        middle_ref, n2_ref = rest[:2]
        rest = rest[2:]
    else:
        n2_ref, cot_ref, up_ref, upb_ref, down_ref, old_ref = ins
    act_ref, gh_ref, small_ref, kept_ref, sent_ref, dw_ref = rest[-6:]
    step = pl.program_id(0)
    length = cot_ref.shape[0]

    @pl.when(step == 0)
    def _():
        small_ref[...] = old_ref[...]
        if first:

            @pl.loop(0, length // 256)
            def _(i):
                at = pl.ds(pl.multiple_of(i * 256, 256), 256)
                branch = nn(mixed_ref[at, :], wo_ref[...]) + bo_ref[...]
                middle = x_ref[at, :].astype(f32) + branch
                middle_ref[at, :] = middle
                norm, _ = normal_rows(middle)
                n2_ref[at, :] = (norm * gain_ref[...] + shift_ref[...]).astype(bf16)
                small_ref[21:22, :] += jnp.sum(branch * branch * keep_ref[at, :], 0, keepdims=True)
                small_ref[23:24, :] += jnp.broadcast_to(
                    jnp.sum(keep_ref[at, :], 0, keepdims=True), (1, small_ref.shape[1])
                )

    row = (0 if first else blocks) + 16 + step

    @pl.loop(0, length // tile)
    def _(i):
        at = pl.ds(pl.multiple_of(i * tile, tile), tile)
        hidden = nn(n2_ref[at, :], up_ref[...]) + upb_ref[...]
        slope = nt(cot_ref[at, :], down_ref[...])
        gate = 0.5 * (1.0 + lax.erf(hidden * 0.7071067811865476))
        bell = jnp.exp(hidden * hidden * -0.5) * 0.3989422804014327
        act_ref[at, :] = (hidden * gate).astype(bf16)
        gh = (slope * (gate + hidden * bell)).astype(bf16)
        gh_ref[at, :] = gh
        small_ref[pl.ds(row, 1), :] += jnp.sum(gh.astype(f32), 0, keepdims=True)

    me = me_ref[0]
    width = dw_ref.shape[0]
    up_at, down_at = (step * 48, step * 192) if relative else (step * 2 * width, 0)
    dw_ref[...] = tn(n2_ref[...], gh_ref[...])
    up_steps = (96, 192) if first else (768, 96)
    put_rows(dw_ref, kept_ref, sent_ref, me, relative, up_at, *up_steps)
    dw_ref[...] = tn(act_ref[...], cot_ref[...])
    if relative:
        down_at = down_at + (768 if first else 384)
    else:
        down_at = up_at + width
    put_quarter(dw_ref, kept_ref, sent_ref, me, relative, down_at, 384 if first else 768)


def feed_call(part, parts, me, given, cot, up, upb, down, small, before, relative):
    length, width = cot.shape
    first = part == 0
    hidden = up.shape[1]
    blocks = hidden // width // parts
    start = part * blocks
    whole, row = full((length, width)), full((1, width))
    kept, sent = block_shapes(2 * width * blocks, width, relative)
    shape = jax.ShapeDtypeStruct
    if first:
        specs = [whole, whole, full((length, 1)), full((width, width)), row, row, row]
        outs = [whole, whole]
        shapes = [shape((length, width), f32), shape((length, width), bf16)]
    else:
        specs, outs, shapes = [whole], [], []
    columns = pl.BlockSpec((length, width), lambda j, *_: (0, j + start))
    left = pl.BlockSpec(memory_space=pl.ANY)
    grid_spec = pltpu.PrefetchScalarGridSpec(
        num_scalar_prefetch=1,
        grid=(blocks,),
        in_specs=specs
        + [
            whole,
            pl.BlockSpec((width, width), lambda j, *_: (0, j + start)),
            pl.BlockSpec((1, width), lambda j, *_: (0, j + start)),
            pl.BlockSpec((width, width), lambda j, *_: (j + start, 0)),
            full((SMALL, width)),
        ]
        + [left] * len(before),
        out_specs=outs + [columns, columns, full((SMALL, width)), full(kept), full(sent)],
        scratch_shapes=[pltpu.VMEM((width, width), f32)],
    )
    count = 1 + len(specs) + 5
    return pl.pallas_call(
        functools.partial(
            feed_kernel, first=first, blocks=blocks, relative=relative, tile=512
        ),
        grid_spec=grid_spec,
        out_shape=shapes
        + [
            shape((length, hidden), bf16),
            shape((length, hidden), bf16),
            shape((SMALL, width), f32),
            shape(kept, bf16),
            shape(sent, bf16),
        ],
        input_output_aliases={count + i: i for i in range(len(before))},
        compiler_params=params(),
        cost_estimate=cost(
            8 * length * width * width * blocks, 20 * length * width, 2 * length * width
        ),
        name="feed",
    )(me, *given, cot, up, upb, down, small, *before)


def finish_kernel(
    me_ref,
    act_ref,
    gh_ref,
    up_ref,
    down_ref,
    middle_ref,
    cot_ref,
    keep_ref,
    mixed_ref,
    wo_ref,
    gain_ref,
    downb_ref,
    old_ref,
    out_ref,
    gm_ref,
    gx_ref,
    small_ref,
    kept_ref,
    sent_ref,
    feed_ref,
    gn_ref,
    dw_ref,
    *,
    blocks,
    tile,
    relative,
):
    step = pl.program_id(0)

    @pl.when(step == 0)
    def _():
        small_ref[...] = old_ref[...]
        feed_ref[...] = jnp.zeros_like(feed_ref)
        gn_ref[...] = jnp.zeros_like(gn_ref)

    @pl.when(step < blocks - 1)
    def _():
        @pl.loop(0, feed_ref.shape[0] // 512)
        def _(i):
            at = pl.ds(pl.multiple_of(i * 512, 512), 512)
            feed_ref[at, :] += nn(act_ref[at, :], down_ref[...])
            gn_ref[at, :] += nt(gh_ref[at, :], up_ref[...])

    @pl.when(step >= blocks - 1)
    def _():
        lows = []
        for i in range(tile // 256):
            here = slice(i * 256, (i + 1) * 256)
            at = pl.ds(pl.multiple_of((step - blocks + 1) * tile + i * 256, 256), 256)
            feed = feed_ref[at, :] + nn(act_ref[at, :], down_ref[...]) + downb_ref[...]
            middle = middle_ref[here, :]
            output = middle + feed
            out_ref[here, :] = output.astype(bf16)
            weight = keep_ref[here, :]
            cot = cot_ref[here, :].astype(f32)
            norm, scale = normal_rows(middle)
            grad = gn_ref[at, :] + nt(gh_ref[at, :], up_ref[...])
            inner = grad * gain_ref[...]
            grad_middle = cot + scale * (
                inner
                - jnp.mean(inner, -1, keepdims=True)
                - norm * jnp.mean(inner * norm, -1, keepdims=True)
            )
            gm_ref[here, :] = grad_middle
            low = grad_middle.astype(bf16)
            gx_ref[here, :] = nt(low, wo_ref[...]).astype(bf16)
            lows.append(low)
            small_ref[0:1, :] += jnp.sum(low.astype(f32), 0, keepdims=True)
            small_ref[1:2, :] += jnp.sum(grad * norm, 0, keepdims=True)
            small_ref[2:3, :] += jnp.sum(grad, 0, keepdims=True)
            small_ref[3:4, :] += jnp.sum(cot, 0, keepdims=True)
            small_ref[20:21, :] += jnp.sum(output * output * weight, 0, keepdims=True)
            small_ref[22:23, :] += jnp.sum(feed * feed * weight, 0, keepdims=True)
        part = tn(mixed_ref[...], jnp.concatenate(lows, 0))

        @pl.when(step == blocks - 1)
        def _():
            dw_ref[...] = part

        @pl.when(step > blocks - 1)
        def _():
            dw_ref[...] += part

    @pl.when(step == pl.num_programs(0) - 1)
    def _():
        put_rows(dw_ref, kept_ref, sent_ref, me_ref[0], relative, 0, 192, 48)


def finish_call(me, acts, up, down, middle, cot, keep, mixed, wo, gain, downb, small, relative):
    length, width = mixed.shape
    blocks = up.shape[1] // width
    end = blocks - 1
    tile = 512
    whole, row = full((length, width)), full((1, width))
    kept, sent = block_shapes(width, width, relative)
    columns = pl.BlockSpec((length, width), lambda j, *_: (0, jnp.minimum(j, end)))

    def tiled(lanes):
        return pl.BlockSpec((tile, lanes), lambda j, *_: (jnp.maximum(j - end, 0), 0))

    rows = tiled(width)
    shape = jax.ShapeDtypeStruct
    grid_spec = pltpu.PrefetchScalarGridSpec(
        num_scalar_prefetch=1,
        grid=(end + length // tile,),
        in_specs=[
            columns,
            columns,
            pl.BlockSpec((width, width), lambda j, *_: (0, jnp.minimum(j, end))),
            pl.BlockSpec((width, width), lambda j, *_: (jnp.minimum(j, end), 0)),
            rows,
            rows,
            tiled(1),
            rows,
            full((width, width)),
            row,
            row,
            full((SMALL, width)),
        ],
        out_specs=[rows, rows, rows, full((SMALL, width)), full(kept), full(sent)],
        scratch_shapes=[
            pltpu.VMEM((length, width), f32),
            pltpu.VMEM((length, width), f32),
            pltpu.VMEM((width, width), f32),
        ],
    )
    return pl.pallas_call(
        functools.partial(finish_kernel, blocks=blocks, tile=tile, relative=relative),
        grid_spec=grid_spec,
        out_shape=[
            shape((length, width), bf16),
            shape((length, width), f32),
            shape((length, width), bf16),
            shape((SMALL, width), f32),
            shape(kept, bf16),
            shape(sent, bf16),
        ],
        compiler_params=params(),
        cost_estimate=cost(4 * length * width * width, 24 * length * width),
        name="finish",
    )(me, *acts, up, down, middle, cot, keep, mixed, wo, gain, downb, small)


UNIT = 256


def units_of(part):
    each = part // UNIT
    places = [(grad, unit) for grad in range(3) for unit in range(each)]
    return [(grad, unit, i // 3, i % 3) for i, (grad, unit) in enumerate(places)]


def spread_small(small, total, chunk):
    sums = jnp.broadcast_to(jnp.sum(small[20:24, :], 1, keepdims=True), (4, chunk))
    for owner in range(16):
        lanes = slice(owner * chunk, (owner + 1) * chunk)
        block, start = owner // 4, (owner % 4) * 4 * chunk
        ups = [
            small[16 + block : 17 + block, start + i * chunk : start + (i + 1) * chunk]
            for i in range(4)
        ]
        piece = jnp.concatenate([small[0:16, lanes], *ups, sums], 0)
        high = piece.astype(bf16).astype(f32)
        whole = jnp.concatenate([high, piece - high], 0)
        for i in range(3):
            total[owner * 16 : (owner + 1) * 16, i * 128 : i * 128 + chunk] = whole[
                i * 16 : (i + 1) * 16
            ]


def weights_kernel(me_ref, n_ref, np_ref, *rest, start, count, relative):
    refs, rest = rest[: 3 * count], rest[3 * count :]
    last = count > 1
    old_ref, rest = rest[0], rest[1:]
    if last:
        x_ref, xp_ref, wq_ref, wp_ref, gq_ref, gp_ref = rest[:6]
        rest = rest[6:]
    small_ref, kept_ref, sent_ref, *totals = rest
    step = pl.program_id(0)
    grads = [ref[...] for ref in refs[-3:]]
    part = grads[0].shape[1]
    lanes = slice(start, start + part)
    sources = [n_ref[...], np_ref[...], np_ref[...]]

    @pl.when(step == 0)
    def _():
        small_ref[...] = old_ref[...]
        for total in totals[:3]:
            total[...] = jnp.zeros_like(total)

    for total, source, grad in zip(totals, sources, grads):
        total[...] += tn(source, grad)
    small_ref[4:5, lanes] += jnp.sum(grads[0].astype(f32), 0, keepdims=True)
    small_ref[7:8, lanes] += jnp.sum(grads[2].astype(f32), 0, keepdims=True)
    if last:
        dq, dk, dv = [jnp.concatenate([ref[...] for ref in refs[i::3]], 1) for i in range(3)]
        width = wq_ref.shape[0]
        far = nt(dk, wp_ref[0:2].reshape(width, width))
        far = far + nt(dv, wp_ref[2:4].reshape(width, width))
        own = nt(dq, wq_ref[...])
        gq_ref[...] = own
        gp_ref[...] = far.astype(bf16)
        norm, _ = normal_rows(x_ref[...].astype(f32))
        far_norm, _ = normal_rows(xp_ref[...].astype(f32))
        small_ref[5:6, :] += jnp.sum(own * norm, 0, keepdims=True)
        small_ref[6:7, :] += jnp.sum(own, 0, keepdims=True)
        small_ref[8:9, :] += jnp.sum(far * far_norm, 0, keepdims=True)
        small_ref[9:10, :] += jnp.sum(far, 0, keepdims=True)

    @pl.when(step == pl.num_programs(0) - 1)
    def _():
        me = me_ref[0]
        z_step = 64 if last else 48 * part // UNIT
        for grad, unit, block, place in units_of(part):
            put_rows(
                totals[grad], kept_ref, sent_ref, me, relative,
                48 * block if relative else 768 * block, 4 * z_step, z_step,
                slice(place * UNIT, (place + 1) * UNIT), slice(unit * UNIT, (unit + 1) * UNIT),
            )
        if last and relative:
            spread = totals[3]
            spread[...] = jnp.zeros_like(spread)
            spread_small(small_ref[...], spread, small_ref.shape[1] // 16)
            put_rows(spread, kept_ref, sent_ref, me, relative, 48, 4 * z_step, z_step)


def weights_call(start, me, n, n_far, grads, small, more, relative):
    length, width = n.shape
    count = len(grads) // 3
    last = count > 1
    part = grads[-1].shape[1]
    tile = 256 if last else 512
    rows = pl.BlockSpec((tile, width), lambda i, *_: (i, 0))
    extra = last and relative
    kept, sent = block_shapes(width * part // UNIT + (256 if extra else 0), width, relative)
    shape = jax.ShapeDtypeStruct
    specs = [rows, rows]
    specs += [pl.BlockSpec((tile, grad.shape[1]), lambda i, *_: (i, 0)) for grad in grads]
    specs += [full((SMALL, width))]
    outs, shapes = [], []
    if last:
        specs += [rows, rows, full(more[2].shape), full(more[3].shape)]
        outs = [rows, rows]
        shapes = [shape((length, width), f32), shape((length, width), bf16)]
    grid_spec = pltpu.PrefetchScalarGridSpec(
        num_scalar_prefetch=1,
        grid=(length // tile,),
        in_specs=specs,
        out_specs=outs + [full((SMALL, width)), full(kept), full(sent)],
        scratch_shapes=[pltpu.VMEM((width, part), f32)] * 3
        + ([pltpu.VMEM((256, width), f32)] if extra else []),
    )
    return pl.pallas_call(
        functools.partial(weights_kernel, start=start, count=count, relative=relative),
        grid_spec=grid_spec,
        out_shape=shapes
        + [shape((SMALL, width), f32), shape(kept, bf16), shape(sent, bf16)],
        compiler_params=params(),
        cost_estimate=cost(6 * length * width * part, 24 * length * width),
        name="weights",
    )(me, n, n_far, *grads, small, *more)


def tokens_kernel(x_ref, gain_ref, gm_ref, gq_ref, gf_ref, out_ref):
    norm, scale = normal_rows(x_ref[...].astype(f32))
    inner = (gq_ref[...] + gf_ref[...].astype(f32)) * gain_ref[...]
    out_ref[...] = gm_ref[...] + scale * (
        inner
        - jnp.mean(inner, -1, keepdims=True)
        - norm * jnp.mean(inner * norm, -1, keepdims=True)
    )


def tokens_call(x, gain, gm, gq, gf):
    length, width = x.shape
    rows = pl.BlockSpec((256, width), lambda i: (i, 0))
    return pl.pallas_call(
        tokens_kernel,
        grid=(length // 256,),
        in_specs=[rows, full((1, width)), rows, rows, rows],
        out_specs=rows,
        out_shape=jax.ShapeDtypeStruct((length, width), f32),
        compiler_params=params(),
        cost_estimate=cost(20 * length * width, 16 * length * width),
        name="tokens",
    )(x, gain, gm, gq, gf)


def swapped(value, axis, mask):
    pairs = [(source, source ^ mask) for source in range(lax.axis_size(axis))]
    return lax.ppermute(value, axis, pairs)


def added(a, b, dtype=bf16):
    return (a.astype(f32) + b.astype(f32)).astype(dtype)


def together(kernel, inputs, moves=(), later=(), due=()):
    count = len(moves)
    moves = list(moves) + list(later)
    inputs, values = lax.optimization_barrier((inputs, [value for value, _, _ in moves]))
    came = [swapped(value, *way[1:]) for value, way in zip(values, moves)]
    results = kernel(*inputs) if kernel else []
    results, now, due = lax.optimization_barrier((results, came[:count], list(due)))
    return results, now, came[count:], due


def total(*values):
    return functools.reduce(jnp.add, [value.astype(f32) for value in values])


def quads(*values):
    values = [value.reshape(4, -1, value.shape[-1]) for value in values]
    return jnp.concatenate(values, 1).reshape(-1, values[0].shape[-1])


def everywhere(value):
    mask = 1
    while mask < lax.axis_size("dp"):
        value = value + swapped(value, "dp", mask)
        mask *= 2
    return value


def pick_stream(pair, stream):
    return jnp.where(stream == 0, pair[0], pair[1])


def box_onehots(seg_boxes, buckets):
    half = buckets // 2
    levels = jnp.arange(buckets, dtype=jnp.int32)
    centre_x = (seg_boxes[..., 0] + seg_boxes[..., 2]) // 2
    centre_y = (seg_boxes[..., 1] + seg_boxes[..., 3]) // 2
    step_x = (
        jnp.clip((centre_x[:, None, :] - centre_x[:, :, None]) // box_step, -half, half - 1) + half
    )
    step_y = (
        jnp.clip((centre_y[:, None, :] - centre_y[:, :, None]) // box_step, -half, half - 1) + half
    )
    return (
        (step_x[..., None] == levels).astype(jnp.float32),
        (step_y[..., None] == levels).astype(jnp.float32),
    )


def body(
    tokens,
    first_gain,
    first_shift,
    query_weight,
    query_bias,
    key_weight,
    value_weight,
    value_bias,
    out_weight,
    out_bias,
    second_gain,
    second_shift,
    up_weight,
    up_bias,
    down_weight,
    down_bias,
    box_table,
    segments,
    validity,
    seg_boxes,
    cotangent,
):
    stream = lax.axis_index("stream")
    me = lax.axis_index("dp")
    shards = lax.axis_size("dp")
    width = tokens.shape[2]
    hidden = up_weight.shape[2]
    pages, page_len = segments.shape[1], segments.shape[2]
    length = pages * page_len
    relative = shards == 16
    me_ref = me.reshape(1).astype(jnp.int32)
    x = tokens[0]

    own_seg = pick_stream(segments, stream)
    far_seg = pick_stream(segments, 1 - stream)
    own_keep = pick_stream(validity, stream)
    far_keep = pick_stream(validity, 1 - stream)
    levels = jnp.arange(64, dtype=jnp.int32)
    hot_q = (own_seg[:, :, None] == levels).astype(bf16)
    hot_kt = (far_seg[:, None, :] == levels[None, :, None]).astype(bf16)
    wide_levels = jnp.arange(128, dtype=jnp.int32)
    hot_k = jnp.where(
        wide_levels == 64,
        jnp.where(far_keep[:, :, None] > 0, 0.0, mask_fill),
        (far_seg[:, :, None] == wide_levels).astype(f32),
    ).astype(bf16)
    hot_x, hot_y = box_onehots(seg_boxes, BUCKETS)
    tables = box_table[0].reshape(2, HEADS, BUCKETS)
    seg_bias = (
        jnp.einsum("pabn,hn->phab", hot_x, tables[0], precision=precise_variant)
        + jnp.einsum("pabn,hn->phab", hot_y, tables[1], precision=precise_variant)
    ).astype(bf16)
    ones = (jnp.arange(64) == 0).astype(bf16)
    seg_bias = jnp.concatenate([seg_bias, jnp.broadcast_to(ones, seg_bias.shape)], -1)

    keep_column = own_keep.reshape(length, 1).astype(f32)
    blocks, chunk = hidden // width, width // shards
    cot = cotangent[0]
    Y, CORE, X, Z1, Z2 = ("stream", 1), ("dp", 1), ("dp", 2), ("dp", 4), ("dp", 8)

    low = me & 3
    half = width // 2

    def quarter(weight):
        return lax.dynamic_slice_in_dim(weight[0], (low & 1) * half, half, 0)

    piece = jnp.where(low < 2, quarter(key_weight), quarter(value_weight))
    vectors = jnp.concatenate([first_gain, first_shift, value_bias], 0)
    (normed, query), (piece,), _, (far_rows,) = together(
        query_call,
        (x, first_gain, first_shift, query_weight[0], query_bias),
        [(piece, *Y)],
        [],
        [swapped(vectors, *Y)],
    )
    page_x = [x[page * page_len : (page + 1) * page_len] for page in range(pages)]
    (picks, hot_q, hot_k), (x_piece, core_piece, came_x), _, _ = together(
        lambda bias, hot_q, hot_k: (picks_call(hot_q, bias), hot_q, hot_k),
        (seg_bias, hot_q, hot_k),
        [(piece, *X), (piece, *CORE), (page_x[0], *Y)],
    )
    far_pages = [came_x]
    pieces = [piece, core_piece, x_piece, swapped(x_piece, *CORE)]
    far, mixing = (), ()
    for page in range(pages):

        def page_step(came, pieces, far, mixing, page=page):
            far = pair_call(page, length, me_ref, came, far_rows, pieces, far)
            return far, attend_call(page, query, far[1], far[2], picks, hot_k, mixing)

        moves = [(page_x[page + 1], *Y)] if page + 1 < pages else []
        (result, mixing), came, _, _ = together(
            page_step, (far_pages[page], pieces, tuple(far), tuple(mixing)), moves
        )
        far = result[:4]
        if page == 0:
            pieces = [result[4]]
        far_pages += came
    far_normed, keys, value_rows, far_x = far
    far_weights = pieces[0]
    mixed, log_total = mixing

    small = jnp.zeros((SMALL, width), f32)

    def feed_first(mixed, small):
        return feed_call(
            0, 2, me_ref,
            (x, mixed, keep_column, out_weight[0], out_bias, second_gain, second_shift),
            cot, up_weight[0], up_bias, down_weight[0], small, (), relative,
        )

    def feed_second(n2, small, *acts):
        return feed_call(
            1, 2, me_ref, (n2,), cot, up_weight[0], up_bias, down_weight[0], small, acts, relative
        )

    def finish(middle, small, *acts):
        return finish_call(
            me_ref, acts, up_weight[0], down_weight[0], middle, cot, keep_column, mixed,
            out_weight[0], second_gain, down_bias, small, relative,
        )

    def back_some(pair, pairs):
        def call(grad_mixed):
            return attend_back_call(
                pair, pairs, query, keys, value_rows, picks, hot_q, hot_k, hot_kt, log_total,
                mixed, grad_mixed,
            )

        return call

    def weights_some(start, more=()):
        def call(small, *grads):
            return weights_call(start, me_ref, normed, far_normed, grads, small, more, relative)

        return call

    back_through = (x, far_x, query_weight[0], far_weights)
    pairs = (4, width // 128 - 4)

    def table_row(grad_bias):
        return jnp.concatenate(
            [
                jnp.einsum("pabn,phba->hn", hot_x, grad_bias, precision=precise_variant),
                jnp.einsum("pabn,phba->hn", hot_y, grad_bias, precision=precise_variant),
            ],
            0,
        ).reshape(1, -1)

    if relative:
        z_low, z_high = (me >> 2) & 1, me >> 3

        def downs(pair):
            one, other = pair[:192], pair[192:]
            return jnp.where(z_low, other, one), jnp.where(z_low, one, other)

        (middle, normed_two, act, gh, small, ka, sa), _, _, _ = together(
            feed_first, (mixed, small)
        )
        (act, gh, small, kb, sb), (ca,), _, _ = together(
            feed_second, (normed_two, small, act, gh), [(sa, *CORE)]
        )
        up_go, down_go = added(ka[384:768], ca[384:768]), added(ka[1152:], ca[1152:])
        (output, grad_middle, grad_mixed, small, ko, so), (cb, x0, z0), _, _ = together(
            finish,
            (middle, small, act, gh),
            [(sb, *CORE), (down_go, *X), (up_go, *Z1)],
        )
        up_go = total(ka[192:384], ca[192:384], z0[192:]).astype(bf16)
        up_stay = total(ka[:192], ca[:192], z0[:192])
        go = added(kb[768:], cb[768:])
        (*grads, grad_bias), (co, z0), (x2,), _ = together(
            back_some(0, pairs[0]), (grad_mixed,), [(so, *CORE), (up_go, *Z2)], [(go, *X)]
        )
        one = total(ka[768:1152], ca[768:1152], x0).astype(bf16)
        one_keep, one_go = downs(one)
        up_low = total(up_stay, z0)
        go = jnp.concatenate([up_low[96:].astype(bf16), added(ko[192:], co[192:])], 0)
        (small, kq, sq), (z0,), (xo,), (x2,) = together(
            weights_some(0), (small, *grads), [(one_go, *Z1)], [(go, *X)], [x2]
        )
        down_one = added(one_keep, z0)
        two = total(kb[:768], cb[:768], x2).astype(bf16)
        two_keep, two_go = downs(two[384:])
        (*grads_two, grad_bias_two), (cq, z1), _, (xo,) = together(
            back_some(*pairs), (grad_mixed,), [(sq, *CORE), (two_go, *Z1)], [], [xo]
        )
        down_two = added(two_keep, z1)
        down_stay = jnp.where(z_high, down_two, down_one)
        down_go = jnp.where(z_high, down_one, down_two)
        go = added(kq[384:], cq[384:])
        rest = quads(two[:384], total(ko[:192], co[:192], xo[96:]).astype(bf16))
        (own_grad, far_grad, small, kr, sr), (xq, z1), (z3,), _ = together(
            weights_some(pairs[0] * 128, back_through),
            (small, *grads, *grads_two),
            [(go, *X), (rest[288:], *Z1)],
            [(down_go, *Z2)],
        )
        _, (cr,), (came_grad,), _ = together(None, (), [(sr, *CORE)], [(far_grad, *Y)])
        go, grad_bias, xq, z1 = lax.optimization_barrier(
            (added(kr[256:], cr[256:]), (grad_bias, grad_bias_two), xq, z1)
        )
        rest_go = added(rest[144:288], z1[144:])
        group_go = total(kq[192:384], cq[192:384], xq[192:]).astype(bf16)
        z4, z2 = swapped(group_go, *Z1), swapped(rest_go, *Z2)
        table = table_row(jnp.concatenate(grad_bias, 1))
        table = table + swapped(table, *CORE)
        _, (xr,), _, (z4, table) = together(None, (), [(go, *X)], [], [z4, table])
        r_go = total(kr[128:256], cr[128:256], xr[128:]).astype(bf16)
        group_go = total(kq[96:192], cq[96:192], xq[96:192], z4[96:]).astype(bf16)
        z5 = swapped(group_go, *Z2)
        _, (z1r, came), _, (z3,) = together(None, (), [(r_go, *Z1), (table, *X)], [], [z3])
        table = table + came
        r_go = total(kr[64:128], cr[64:128], xr[64:128], z1r[64:]).astype(bf16)
        _, (z2r, came), _, (z2, z5, came_grad) = together(
            None, (), [(r_go, *Z2), (table, *Z1)], [], [z2, z5, came_grad]
        )
        table = table + came
        up_low = total(up_low[:96], xo[:96])
        sum_down = total(down_stay, z3)
        rest = total(rest[:144], z1[:144], z2)
        first = total(kq[:96], cq[:96], xq[:96], z4[:96], z5)
        last = total(kr[:64], cr[:64], xr[:64], z1r[:64], z2r)
        sum_up = jnp.concatenate([up_low[:48], up_low[48:], rest[:48], rest[48:96]], 1)
        sum_out = rest[96:]

        def lanes_of(spread):
            pieces = [spread[:, 128 * i : 128 * i + chunk] for i in range(3)]
            pieces = jnp.concatenate(pieces, 0)
            return pieces[:SMALL] + pieces[SMALL:]

        def unit(values, place):
            block, lane = place // 3, place % 3
            return values[48 * block : 48 * block + 48, UNIT * lane : UNIT * (lane + 1)]

        def joined(first, last, i):
            return jnp.concatenate(
                [unit(first, 2 * i), unit(first, 2 * i + 1), unit(last, i)], 1
            )

        def ending(*given):
            lanes = lanes_of(last[48:])
            totals = lanes[20:24, 0]
            root_means = jnp.sqrt(totals[:3] / totals[3] + 1e-06).reshape(1, 3)
            up_part = lanes[16:20].reshape(1, hidden // shards)
            grad_tokens = tokens_call(*given)
            sum_query = joined(first, last, 0)
            return grad_tokens, lanes, root_means, up_part, sum_query, sum_up, sum_out, sum_down

        ended, (far_first, far_last, came), _, _ = together(
            ending,
            (x, first_gain, grad_middle, own_grad, came_grad),
            [(first.astype(bf16), *Y), (last, *Y), (table, *Z2)],
        )
        grad_tokens, lanes, root_means, up_part, sum_query, sum_up, sum_out, sum_down = ended
        table = table + came
        back = lanes_of(far_last[48:])[7:10]
        far_first = far_first.astype(f32)
        sum_keys, sum_values = joined(far_first, far_last, 1), joined(far_first, far_last, 2)
    else:
        middle, normed_two, act, gh, small, ka, _ = feed_first(mixed, small)
        act, gh, small, kb, _ = feed_second(normed_two, small, act, gh)
        output, grad_middle, grad_mixed, small, out_kept, _ = finish(middle, small, act, gh)
        *grads, grad_bias = back_some(0, pairs[0])(grad_mixed)
        small, kq, _ = weights_some(0)(small, *grads)
        *grads_two, grad_bias_two = back_some(*pairs)(grad_mixed)
        table = everywhere(table_row(jnp.concatenate([grad_bias, grad_bias_two], 1)))
        own_grad, far_grad, small, kr, _ = weights_some(pairs[0] * 128, back_through)(
            small, *grads, *grads_two
        )
        came_grad = swapped(far_grad, *Y)
        grad_tokens = tokens_call(x, first_gain, grad_middle, own_grad, came_grad)
        small = everywhere(small)

        def scattered(value):
            return lax.psum_scatter(value.astype(f32), "dp", scatter_dimension=0, tiled=True)

        def unit(values, place):
            block, lane = place // 3, place % 3
            return values[width * block : width * (block + 1), UNIT * lane : UNIT * (lane + 1)]

        ups = jnp.concatenate([ka, kb], 0).reshape(blocks, 2 * width, width)
        sum_up = scattered(jnp.concatenate([ups[j, :width] for j in range(blocks)], 1))
        sum_down = scattered(jnp.concatenate([ups[j, width:] for j in range(blocks)], 0))
        sum_out = scattered(out_kept)
        sum_query, sum_keys, sum_values = [
            scattered(
                jnp.concatenate([unit(kq, 2 * i), unit(kq, 2 * i + 1), unit(kr, i)], 1)
            )
            for i in range(3)
        ]
        sum_pair = jnp.concatenate([sum_keys, sum_values], 0).astype(bf16)
        lanes = lax.dynamic_slice_in_dim(small, me * chunk, chunk, 1)
        up_part = lax.dynamic_slice_in_dim(
            small[16 : 16 + blocks].reshape(1, hidden), me * (hidden // shards), hidden // shards, 1
        )
        totals = jnp.sum(small[20:24], 1)
        sum_pair, back = swapped((sum_pair, lanes[7:10]), *Y)
        root_means = jnp.sqrt(totals[:3] / totals[3] + 1e-06).reshape(1, 3)
        sum_keys, sum_values = sum_pair[:chunk].astype(f32), sum_pair[chunk:].astype(f32)

    return (
        output[None],
        grad_tokens[None],
        lanes[5:6] + back[1:2],
        lanes[6:7] + back[2:3],
        sum_query[None],
        lanes[4:5],
        sum_keys[None],
        sum_values[None],
        back[0:1],
        sum_out[None],
        lanes[0:1],
        lanes[1:2],
        lanes[2:3],
        sum_up[None],
        up_part,
        sum_down[None],
        lanes[3:4],
        lax.dynamic_slice_in_dim(table, me * chunk, chunk, 1),
        root_means,
    )


def solution(mesh):
    whole, split = P("stream", None), P("stream", "dp")
    cube, cut = P("stream", None, None), P("stream", "dp", None)
    pages = P(None, "dp", None)
    in_specs = (
        cut, whole, whole, cube, whole, cube, cube, whole, cube, whole, whole, whole,
        cube, whole, cube, whole, whole, pages, pages, P("dp", None, None), cut,
    )
    out_specs = (
        cut, cut, split, split, cut, split, cut, cut, split, cut, split, split, split,
        cut, split, cut, split, split, whole,
    )
    return jax.shard_map(body, mesh=mesh, in_specs=in_specs, out_specs=out_specs, check_vma=False)
```

```python
import functools

import jax
import jax.numpy as jnp
from jax import lax
from jax.experimental import pallas as pl
from jax.experimental.pallas import tpu as pltpu
from jax.sharding import PartitionSpec as P

HEADS = 12
BUCKETS = 32
SMALL = 24

score_scale = 0.125
norm_eps = 1e-05
mask_fill = -1000000000.0
box_step = 32
precise_variant = lax.Precision.HIGHEST
f32 = jnp.float32
bf16 = jnp.bfloat16


def nn(a, b):
    return lax.dot_general(a, b, (((1,), (0,)), ((), ())), preferred_element_type=f32)


def nt(a, b):
    return lax.dot_general(a, b, (((1,), (1,)), ((), ())), preferred_element_type=f32)


def tn(a, b):
    return lax.dot_general(a, b, (((0,), (0,)), ((), ())), preferred_element_type=f32)


def normal_rows(rows):
    centre = rows - jnp.mean(rows, -1, keepdims=True)
    spread = jnp.mean(centre * centre, -1, keepdims=True)
    scale = lax.rsqrt(spread + norm_eps)
    return centre * scale, scale


def params(mib=60):
    return pltpu.CompilerParams(vmem_limit_bytes=mib * 1024 * 1024)


def cost(flops, moved, trans=0, scale=1 / 64):
    return pl.CostEstimate(
        flops=int(flops * scale),
        bytes_accessed=int(moved * scale),
        transcendentals=int(trans * scale),
    )


def full(shape):
    zeros = (0,) * len(shape)
    return pl.BlockSpec(shape, lambda *_: zeros)


def query_kernel(x_ref, gain_ref, shift_ref, w_ref, b_ref, n_ref, q_ref):
    norm, _ = normal_rows(x_ref[...].astype(f32))
    low = (norm * gain_ref[...] + shift_ref[...]).astype(bf16)
    n_ref[...] = low
    query = (nn(low, w_ref[...]) + b_ref[...]).astype(bf16)
    q_ref[...] = (query.astype(f32) * score_scale).astype(bf16)


def query_call(x, gain, shift, weight, bias):
    length, width = x.shape
    tile = 256
    rows = pl.BlockSpec((tile, width), lambda i: (i, 0))
    return pl.pallas_call(
        query_kernel,
        grid=(length // tile,),
        in_specs=[rows, full((1, width)), full((1, width)), full(weight.shape), full((1, width))],
        out_specs=[rows, rows],
        out_shape=[jax.ShapeDtypeStruct(x.shape, bf16)] * 2,
        compiler_params=params(),
        cost_estimate=cost(2 * length * width * width, 6 * length * width + 2 * width * width),
        name="query",
    )(x, gain, shift, weight, bias)


def pair_kernel(me_ref, x_ref, rows_ref, *rest, count):
    pieces, (n_ref, k_ref, v_ref, copy_ref, w_ref) = rest[:count], rest[-5:]
    if count == 4:

        @pl.when(pl.program_id(0) == 0)
        def _():
            low = me_ref[0] & 3
            for place in range(4):
                w_ref[place ^ low] = pieces[place][...]

        weights = w_ref
    else:
        weights = pieces[0]
    half = weights.shape[1]
    copy_ref[...] = x_ref[...]
    norm, _ = normal_rows(x_ref[...].astype(f32))
    low = (norm * rows_ref[0:1, :] + rows_ref[1:2, :]).astype(bf16)
    n_ref[...] = low
    left, right = low[:, :half], low[:, half:]
    k_ref[...] = (nn(left, weights[0]) + nn(right, weights[1])).astype(bf16)
    v_ref[...] = (nn(left, weights[2]) + nn(right, weights[3]) + rows_ref[2:3, :]).astype(bf16)


def pair_call(page, length, me, x, rows, pieces, before):
    page_len, width = x.shape
    tile = 256
    first = page * page_len // tile
    placed = pl.BlockSpec((tile, width), lambda i, *_: (i + first, 0))
    left = pl.BlockSpec(memory_space=pl.ANY)
    weights = (4, width // 2, width)
    out_specs = [placed] * 4
    shapes = [jax.ShapeDtypeStruct((length, width), bf16)] * 4
    scratch = []
    if len(pieces) == 4:
        out_specs = out_specs + [full(weights)]
        shapes = shapes + [jax.ShapeDtypeStruct(weights, bf16)]
    else:
        scratch = [pltpu.VMEM((8, 128), f32)]
    grid_spec = pltpu.PrefetchScalarGridSpec(
        num_scalar_prefetch=1,
        grid=(page_len // tile,),
        in_specs=[
            pl.BlockSpec((tile, width), lambda i, *_: (i, 0)),
            full(rows.shape),
        ]
        + [full(piece.shape) for piece in pieces]
        + [left] * len(before),
        out_specs=out_specs,
        scratch_shapes=scratch,
    )
    return pl.pallas_call(
        functools.partial(pair_kernel, count=len(pieces)),
        grid_spec=grid_spec,
        out_shape=shapes,
        input_output_aliases={3 + len(pieces) + i: i for i in range(len(before))},
        compiler_params=params(),
        cost_estimate=cost(4 * page_len * width * width, 8 * page_len * width),
        name="pair",
    )(me, x, rows, *pieces, *before)


def head_lanes(value, head, head_dim):
    lane = lax.broadcasted_iota(jnp.int32, value.shape, 1)
    mine = (lane >= head * head_dim) & (lane < (head + 1) * head_dim)
    return jnp.where(mine, value, jnp.zeros_like(value))


def picks_kernel(hq_ref, bias_ref, out_ref):
    for pair in range(out_ref.shape[1] // 256):
        both = jnp.concatenate([bias_ref[0, 2 * pair], bias_ref[0, 2 * pair + 1]], 1)
        out_ref[:, 256 * pair : 256 * (pair + 1)] = nn(hq_ref[0], both).astype(bf16)


def picks_call(hot_q, bias):
    pages, page_len = hot_q.shape[0], hot_q.shape[1]
    return pl.pallas_call(
        picks_kernel,
        grid=(pages, 3),
        in_specs=[
            pl.BlockSpec((1, page_len, 64), lambda p, h: (p, 0, 0)),
            pl.BlockSpec((1, 4, 64, 128), lambda p, h: (p, h, 0, 0)),
        ],
        out_specs=pl.BlockSpec((page_len, 512), lambda p, h: (p, h)),
        out_shape=jax.ShapeDtypeStruct((pages * page_len, HEADS * 128), bf16),
        compiler_params=params(),
        cost_estimate=cost(2 * pages * page_len * HEADS * 128 * 64, pages * page_len * HEADS * 256),
        name="picks",
    )(hot_q, bias)


def pair_right(q, picks):
    heads = [head_lanes(q, head, 64) for head in range(2)]
    sides = [
        jnp.concatenate([heads[head], picks[:, 128 * head : 128 * (head + 1)]], 1)
        for head in range(2)
    ]
    return jnp.concatenate(heads, 0), jnp.concatenate(sides, 0)


def attend_kernel(q_ref, k_ref, v_ref, picks_ref, hk_ref, *rest):
    o_ref, lse_ref = rest[-2:]
    page_len = q_ref.shape[0]
    for pair in range(q_ref.shape[1] // 128):
        lanes = slice(128 * pair, 128 * (pair + 1))
        left = jnp.concatenate([k_ref[:, lanes], hk_ref[0]], 1)
        v_turned = v_ref[:, lanes].astype(f32).T.astype(bf16)
        _, right = pair_right(q_ref[:, lanes], picks_ref[:, 256 * pair : 256 * (pair + 1)])
        scores = nt(left, right)
        peak = jnp.max(scores, 0, keepdims=True)
        raised = jnp.exp(scores - peak)
        total = jnp.sum(raised, 0, keepdims=True)
        probs = (raised * (1.0 / total)).astype(bf16)
        lse = peak + jnp.log(total)
        parts = []
        for head in range(2):
            mine = slice(head * page_len, (head + 1) * page_len)
            parts.append(nn(v_turned[head * 64 : (head + 1) * 64], probs[:, mine]))
            lse_ref[0, pair, head : head + 1, :] = lse[:, mine]
        o_ref[:, lanes] = jnp.concatenate(parts, 0).T.astype(bf16)


PAIRS = 2


def attend_specs(page_len, page, first):
    rows = pl.BlockSpec((page_len, 128 * PAIRS), lambda p, h: (p + page, h + first))
    picks = pl.BlockSpec((page_len, 256 * PAIRS), lambda p, h: (p + page, h + first))
    lse = pl.BlockSpec((1, PAIRS, 2, page_len), lambda p, h: (p + page, h + first, 0, 0))

    def hot(*shape):
        return pl.BlockSpec((1,) + shape, lambda p, h: (p + page, 0, 0))

    return rows, picks, lse, hot


def attend_call(page, q, k, v, picks, hot_k, before):
    length, width = q.shape
    pages, page_len = hot_k.shape[0], hot_k.shape[1]
    rows, picks_spec, lse, hot = attend_specs(page_len, page, 0)
    left = pl.BlockSpec(memory_space=pl.ANY)
    return pl.pallas_call(
        attend_kernel,
        grid=(1, width // 128 // PAIRS),
        in_specs=[rows, rows, rows, picks_spec, hot(page_len, 128)] + [left] * len(before),
        out_specs=[rows, lse],
        out_shape=[
            jax.ShapeDtypeStruct((length, width), bf16),
            jax.ShapeDtypeStruct((pages, width // 128, 2, page_len), f32),
        ],
        input_output_aliases={5 + i: i for i in range(len(before))},
        compiler_params=params(),
        cost_estimate=cost(
            16 * page_len * page_len * width,
            8 * page_len * width,
            page_len * page_len * HEADS,
        ),
        name="attend",
    )(q, k, v, picks, hot_k, *before)


def attend_back_kernel(
    q_ref,
    k_ref,
    v_ref,
    picks_ref,
    hq_ref,
    hk_ref,
    hkt_ref,
    lse_ref,
    o_ref,
    do_ref,
    dq_ref,
    dk_ref,
    dv_ref,
    gb_ref,
):
    page_len = q_ref.shape[0]
    row = lax.broadcasted_iota(jnp.int32, (8, 128), 0)
    lane = lax.broadcasted_iota(jnp.int32, (8, 128), 1)
    chooser = (row == lane // 64).astype(bf16)
    for pair in range(q_ref.shape[1] // 128):
        lanes = slice(128 * pair, 128 * (pair + 1))
        k, v, do = k_ref[:, lanes], v_ref[:, lanes], do_ref[:, lanes]
        left = jnp.concatenate([k, hk_ref[0]], 1)
        k_turned = k.astype(f32).T.astype(bf16)
        overlap = do.astype(f32) * o_ref[:, lanes].astype(f32)
        high = overlap.astype(bf16)
        rest = (overlap - high.astype(f32)).astype(bf16)
        delta = nt(chooser, high) + nt(chooser, rest)
        delta = jnp.concatenate([delta[0:1], delta[1:2]], 1)
        lse = jnp.concatenate([lse_ref[0, pair, 0:1, :], lse_ref[0, pair, 1:2, :]], 1)
        queries, right = pair_right(q_ref[:, lanes], picks_ref[:, 256 * pair : 256 * (pair + 1)])
        do_heads = jnp.concatenate([head_lanes(do, head, 64) for head in range(2)], 0)
        probs = jnp.exp(nt(left, right) - lse)
        turn = (probs * (nt(v, do_heads) - delta)).astype(bf16)
        dv_ref[:, lanes] = nn(probs.astype(bf16), do_heads).astype(bf16)
        dk_ref[:, lanes] = nn(turn, queries).astype(bf16)
        parts, sums = [], []
        for head in range(2):
            both = nn(
                jnp.concatenate([k_turned[head * 64 : (head + 1) * 64], hkt_ref[0]], 0),
                turn[:, head * page_len : (head + 1) * page_len],
            )
            parts.append(both[:64])
            sums.append(both[64:])
        dq_ref[:, lanes] = (jnp.concatenate(parts, 0) * score_scale).T.astype(bf16)
        sums = jnp.concatenate(sums, 0)
        high = sums.astype(bf16)
        rest = (sums - high.astype(f32)).astype(bf16)
        grads = nn(jnp.concatenate([high, rest], 0), hq_ref[0])
        grads = grads[:128] + grads[128:]
        for head in range(2):
            gb_ref[0, 2 * pair + head] = grads[64 * head : 64 * (head + 1)]


def attend_back_call(pair, pairs, q, k, v, picks, hot_q, hot_k, hot_kt, lse_in, o, do):
    length, width = q.shape
    pages, page_len = hot_q.shape[0], hot_q.shape[1]
    rows, picks_spec, lse, hot = attend_specs(page_len, 0, pair // PAIRS)
    given = pl.BlockSpec((page_len, 128 * PAIRS), lambda p, h: (p, h))
    grad_bias = pl.BlockSpec((1, 2 * PAIRS, 64, 64), lambda p, h: (p, h, 0, 0))
    wide = jax.ShapeDtypeStruct((length, pairs * 128), bf16)
    return pl.pallas_call(
        attend_back_kernel,
        grid=(pages, pairs // PAIRS),
        in_specs=[
            rows,
            rows,
            rows,
            picks_spec,
            hot(page_len, 64),
            hot(page_len, 128),
            hot(64, page_len),
            lse,
            rows,
            rows,
        ],
        out_specs=[given, given, given, grad_bias],
        out_shape=[wide, wide, wide, jax.ShapeDtypeStruct((pages, 2 * pairs, 64, 64), f32)],
        compiler_params=params(),
        cost_estimate=cost(
            40 * length * page_len * pairs * 128,
            16 * length * pairs * 128,
            length * page_len * 2 * pairs,
            64,
        ),
        name="attend_back",
    )(q, k, v, picks, hot_q, hot_k, hot_kt, lse_in, o, do)


def put_rows(
    scratch, keep, send, me, relative, at, x_step, z_step, lanes=slice(None), source=slice(None)
):
    if not relative:
        keep[pl.ds(at, scratch.shape[0]), lanes] = scratch[:, source].astype(bf16)
        return
    step = scratch.shape[0] // 16
    for place in range(16):
        owner = place ^ me
        rows = scratch[pl.ds(pl.multiple_of(owner * step, step), step), source].astype(bf16)
        target = send if place & 1 else keep
        z = ((place >> 2) & 1) * 2 + (place >> 3)
        low = at + ((place >> 1) & 1) * x_step + z * z_step
        target[pl.ds(pl.multiple_of(low, 16), step), lanes] = rows


def put_quarter(scratch, keep, send, me, relative, at, x_step):
    if not relative:
        keep[pl.ds(at, scratch.shape[0]), :] = scratch[...].astype(bf16)
        return
    step = scratch.shape[0] // 4
    for place in range(4):
        owner = place ^ (me & 3)
        rows = scratch[pl.ds(pl.multiple_of(owner * step, step), step), :].astype(bf16)
        target = send if place & 1 else keep
        target[pl.ds(pl.multiple_of(at + (place >> 1) * x_step, 16), step), :] = rows


def block_shapes(rows, width, relative):
    if relative:
        return (rows // 2, width), (rows // 2, width)
    return (rows, width), (16, 128)


def feed_kernel(me_ref, *rest, first, blocks, relative, tile):
    ins, rest = rest[: 12 if first else 6], rest[12 if first else 8 :]
    if first:
        x_ref, mixed_ref, keep_ref, wo_ref, bo_ref, gain_ref, shift_ref = ins[:7]
        cot_ref, up_ref, upb_ref, down_ref, old_ref = ins[7:]
        middle_ref, n2_ref = rest[:2]
        rest = rest[2:]
    else:
        n2_ref, cot_ref, up_ref, upb_ref, down_ref, old_ref = ins
    act_ref, gh_ref, small_ref, kept_ref, sent_ref, dw_ref = rest[-6:]
    step = pl.program_id(0)
    length = cot_ref.shape[0]

    @pl.when(step == 0)
    def _():
        small_ref[...] = old_ref[...]
        if first:

            @pl.loop(0, length // 256)
            def _(i):
                at = pl.ds(pl.multiple_of(i * 256, 256), 256)
                branch = nn(mixed_ref[at, :], wo_ref[...]) + bo_ref[...]
                middle = x_ref[at, :].astype(f32) + branch
                middle_ref[at, :] = middle
                norm, _ = normal_rows(middle)
                n2_ref[at, :] = (norm * gain_ref[...] + shift_ref[...]).astype(bf16)
                small_ref[21:22, :] += jnp.sum(branch * branch * keep_ref[at, :], 0, keepdims=True)
                small_ref[23:24, :] += jnp.broadcast_to(
                    jnp.sum(keep_ref[at, :], 0, keepdims=True), (1, small_ref.shape[1])
                )

    row = (0 if first else blocks) + 16 + step

    @pl.loop(0, length // tile)
    def _(i):
        at = pl.ds(pl.multiple_of(i * tile, tile), tile)
        hidden = nn(n2_ref[at, :], up_ref[...]) + upb_ref[...]
        slope = nt(cot_ref[at, :], down_ref[...])
        gate = 0.5 * (1.0 + lax.erf(hidden * 0.7071067811865476))
        bell = jnp.exp(hidden * hidden * -0.5) * 0.3989422804014327
        act_ref[at, :] = (hidden * gate).astype(bf16)
        gh = (slope * (gate + hidden * bell)).astype(bf16)
        gh_ref[at, :] = gh
        small_ref[pl.ds(row, 1), :] += jnp.sum(gh.astype(f32), 0, keepdims=True)

    me = me_ref[0]
    width = dw_ref.shape[0]
    up_at, down_at = (step * 48, step * 192) if relative else (step * 2 * width, 0)
    dw_ref[...] = tn(n2_ref[...], gh_ref[...])
    up_steps = (96, 192) if first else (768, 96)
    put_rows(dw_ref, kept_ref, sent_ref, me, relative, up_at, *up_steps)
    dw_ref[...] = tn(act_ref[...], cot_ref[...])
    if relative:
        down_at = down_at + (768 if first else 384)
    else:
        down_at = up_at + width
    put_quarter(dw_ref, kept_ref, sent_ref, me, relative, down_at, 384 if first else 768)


def feed_call(part, parts, me, given, cot, up, upb, down, small, before, relative):
    length, width = cot.shape
    first = part == 0
    hidden = up.shape[1]
    blocks = hidden // width // parts
    start = part * blocks
    whole, row = full((length, width)), full((1, width))
    kept, sent = block_shapes(2 * width * blocks, width, relative)
    shape = jax.ShapeDtypeStruct
    if first:
        specs = [whole, whole, full((length, 1)), full((width, width)), row, row, row]
        outs = [whole, whole]
        shapes = [shape((length, width), f32), shape((length, width), bf16)]
    else:
        specs, outs, shapes = [whole], [], []
    columns = pl.BlockSpec((length, width), lambda j, *_: (0, j + start))
    left = pl.BlockSpec(memory_space=pl.ANY)
    grid_spec = pltpu.PrefetchScalarGridSpec(
        num_scalar_prefetch=1,
        grid=(blocks,),
        in_specs=specs
        + [
            whole,
            pl.BlockSpec((width, width), lambda j, *_: (0, j + start)),
            pl.BlockSpec((1, width), lambda j, *_: (0, j + start)),
            pl.BlockSpec((width, width), lambda j, *_: (j + start, 0)),
            full((SMALL, width)),
        ]
        + [left] * len(before),
        out_specs=outs + [columns, columns, full((SMALL, width)), full(kept), full(sent)],
        scratch_shapes=[pltpu.VMEM((width, width), f32)],
    )
    count = 1 + len(specs) + 5
    return pl.pallas_call(
        functools.partial(
            feed_kernel, first=first, blocks=blocks, relative=relative, tile=512
        ),
        grid_spec=grid_spec,
        out_shape=shapes
        + [
            shape((length, hidden), bf16),
            shape((length, hidden), bf16),
            shape((SMALL, width), f32),
            shape(kept, bf16),
            shape(sent, bf16),
        ],
        input_output_aliases={count + i: i for i in range(len(before))},
        compiler_params=params(),
        cost_estimate=cost(
            8 * length * width * width * blocks, 20 * length * width, 2 * length * width
        ),
        name="feed",
    )(me, *given, cot, up, upb, down, small, *before)


def finish_kernel(
    me_ref,
    act_ref,
    gh_ref,
    up_ref,
    down_ref,
    middle_ref,
    cot_ref,
    keep_ref,
    mixed_ref,
    wo_ref,
    gain_ref,
    downb_ref,
    old_ref,
    out_ref,
    gm_ref,
    gx_ref,
    small_ref,
    kept_ref,
    sent_ref,
    feed_ref,
    gn_ref,
    dw_ref,
    *,
    blocks,
    tile,
    relative,
):
    step = pl.program_id(0)

    @pl.when(step == 0)
    def _():
        small_ref[...] = old_ref[...]
        feed_ref[...] = jnp.zeros_like(feed_ref)
        gn_ref[...] = jnp.zeros_like(gn_ref)

    @pl.when(step < blocks - 1)
    def _():
        @pl.loop(0, feed_ref.shape[0] // 512)
        def _(i):
            at = pl.ds(pl.multiple_of(i * 512, 512), 512)
            feed_ref[at, :] += nn(act_ref[at, :], down_ref[...])
            gn_ref[at, :] += nt(gh_ref[at, :], up_ref[...])

    @pl.when(step >= blocks - 1)
    def _():
        lows = []
        for i in range(tile // 256):
            here = slice(i * 256, (i + 1) * 256)
            at = pl.ds(pl.multiple_of((step - blocks + 1) * tile + i * 256, 256), 256)
            feed = feed_ref[at, :] + nn(act_ref[at, :], down_ref[...]) + downb_ref[...]
            middle = middle_ref[here, :]
            output = middle + feed
            out_ref[here, :] = output.astype(bf16)
            weight = keep_ref[here, :]
            cot = cot_ref[here, :].astype(f32)
            norm, scale = normal_rows(middle)
            grad = gn_ref[at, :] + nt(gh_ref[at, :], up_ref[...])
            inner = grad * gain_ref[...]
            grad_middle = cot + scale * (
                inner
                - jnp.mean(inner, -1, keepdims=True)
                - norm * jnp.mean(inner * norm, -1, keepdims=True)
            )
            gm_ref[here, :] = grad_middle
            low = grad_middle.astype(bf16)
            gx_ref[here, :] = nt(low, wo_ref[...]).astype(bf16)
            lows.append(low)
            small_ref[0:1, :] += jnp.sum(low.astype(f32), 0, keepdims=True)
            small_ref[1:2, :] += jnp.sum(grad * norm, 0, keepdims=True)
            small_ref[2:3, :] += jnp.sum(grad, 0, keepdims=True)
            small_ref[3:4, :] += jnp.sum(cot, 0, keepdims=True)
            small_ref[20:21, :] += jnp.sum(output * output * weight, 0, keepdims=True)
            small_ref[22:23, :] += jnp.sum(feed * feed * weight, 0, keepdims=True)
        part = tn(mixed_ref[...], jnp.concatenate(lows, 0))

        @pl.when(step == blocks - 1)
        def _():
            dw_ref[...] = part

        @pl.when(step > blocks - 1)
        def _():
            dw_ref[...] += part

    @pl.when(step == pl.num_programs(0) - 1)
    def _():
        put_rows(dw_ref, kept_ref, sent_ref, me_ref[0], relative, 0, 192, 48)


def finish_call(me, acts, up, down, middle, cot, keep, mixed, wo, gain, downb, small, relative):
    length, width = mixed.shape
    blocks = up.shape[1] // width
    end = blocks - 1
    tile = 512
    whole, row = full((length, width)), full((1, width))
    kept, sent = block_shapes(width, width, relative)
    columns = pl.BlockSpec((length, width), lambda j, *_: (0, jnp.minimum(j, end)))

    def tiled(lanes):
        return pl.BlockSpec((tile, lanes), lambda j, *_: (jnp.maximum(j - end, 0), 0))

    rows = tiled(width)
    shape = jax.ShapeDtypeStruct
    grid_spec = pltpu.PrefetchScalarGridSpec(
        num_scalar_prefetch=1,
        grid=(end + length // tile,),
        in_specs=[
            columns,
            columns,
            pl.BlockSpec((width, width), lambda j, *_: (0, jnp.minimum(j, end))),
            pl.BlockSpec((width, width), lambda j, *_: (jnp.minimum(j, end), 0)),
            rows,
            rows,
            tiled(1),
            rows,
            full((width, width)),
            row,
            row,
            full((SMALL, width)),
        ],
        out_specs=[rows, rows, rows, full((SMALL, width)), full(kept), full(sent)],
        scratch_shapes=[
            pltpu.VMEM((length, width), f32),
            pltpu.VMEM((length, width), f32),
            pltpu.VMEM((width, width), f32),
        ],
    )
    return pl.pallas_call(
        functools.partial(finish_kernel, blocks=blocks, tile=tile, relative=relative),
        grid_spec=grid_spec,
        out_shape=[
            shape((length, width), bf16),
            shape((length, width), f32),
            shape((length, width), bf16),
            shape((SMALL, width), f32),
            shape(kept, bf16),
            shape(sent, bf16),
        ],
        compiler_params=params(),
        cost_estimate=cost(4 * length * width * width, 24 * length * width),
        name="finish",
    )(me, *acts, up, down, middle, cot, keep, mixed, wo, gain, downb, small)


UNIT = 256


def units_of(part):
    each = part // UNIT
    places = [(grad, unit) for grad in range(3) for unit in range(each)]
    return [(grad, unit, i // 3, i % 3) for i, (grad, unit) in enumerate(places)]


def spread_small(small, total, chunk):
    sums = jnp.broadcast_to(jnp.sum(small[20:24, :], 1, keepdims=True), (4, chunk))
    for owner in range(16):
        lanes = slice(owner * chunk, (owner + 1) * chunk)
        block, start = owner // 4, (owner % 4) * 4 * chunk
        ups = [
            small[16 + block : 17 + block, start + i * chunk : start + (i + 1) * chunk]
            for i in range(4)
        ]
        piece = jnp.concatenate([small[0:16, lanes], *ups, sums], 0)
        high = piece.astype(bf16).astype(f32)
        whole = jnp.concatenate([high, piece - high], 0)
        for i in range(3):
            total[owner * 16 : (owner + 1) * 16, i * 128 : i * 128 + chunk] = whole[
                i * 16 : (i + 1) * 16
            ]


def weights_kernel(me_ref, n_ref, np_ref, *rest, start, count, relative):
    refs, rest = rest[: 3 * count], rest[3 * count :]
    last = count > 1
    old_ref, rest = rest[0], rest[1:]
    if last:
        x_ref, xp_ref, wq_ref, wp_ref, gq_ref, gp_ref = rest[:6]
        rest = rest[6:]
    small_ref, kept_ref, sent_ref, *totals = rest
    step = pl.program_id(0)
    grads = [ref[...] for ref in refs[-3:]]
    part = grads[0].shape[1]
    lanes = slice(start, start + part)
    sources = [n_ref[...], np_ref[...], np_ref[...]]

    @pl.when(step == 0)
    def _():
        small_ref[...] = old_ref[...]
        for total in totals[:3]:
            total[...] = jnp.zeros_like(total)

    for total, source, grad in zip(totals, sources, grads):
        total[...] += tn(source, grad)
    small_ref[4:5, lanes] += jnp.sum(grads[0].astype(f32), 0, keepdims=True)
    small_ref[7:8, lanes] += jnp.sum(grads[2].astype(f32), 0, keepdims=True)
    if last:
        dq, dk, dv = [jnp.concatenate([ref[...] for ref in refs[i::3]], 1) for i in range(3)]
        width = wq_ref.shape[0]
        far = nt(dk, wp_ref[0:2].reshape(width, width))
        far = far + nt(dv, wp_ref[2:4].reshape(width, width))
        own = nt(dq, wq_ref[...])
        gq_ref[...] = own
        gp_ref[...] = far.astype(bf16)
        norm, _ = normal_rows(x_ref[...].astype(f32))
        far_norm, _ = normal_rows(xp_ref[...].astype(f32))
        small_ref[5:6, :] += jnp.sum(own * norm, 0, keepdims=True)
        small_ref[6:7, :] += jnp.sum(own, 0, keepdims=True)
        small_ref[8:9, :] += jnp.sum(far * far_norm, 0, keepdims=True)
        small_ref[9:10, :] += jnp.sum(far, 0, keepdims=True)

    @pl.when(step == pl.num_programs(0) - 1)
    def _():
        me = me_ref[0]
        z_step = 64 if last else 48 * part // UNIT
        for grad, unit, block, place in units_of(part):
            put_rows(
                totals[grad], kept_ref, sent_ref, me, relative,
                48 * block if relative else 768 * block, 4 * z_step, z_step,
                slice(place * UNIT, (place + 1) * UNIT), slice(unit * UNIT, (unit + 1) * UNIT),
            )
        if last and relative:
            spread = totals[3]
            spread[...] = jnp.zeros_like(spread)
            spread_small(small_ref[...], spread, small_ref.shape[1] // 16)
            put_rows(spread, kept_ref, sent_ref, me, relative, 48, 4 * z_step, z_step)


def weights_call(start, me, n, n_far, grads, small, more, relative):
    length, width = n.shape
    count = len(grads) // 3
    last = count > 1
    part = grads[-1].shape[1]
    tile = 256
    rows = pl.BlockSpec((tile, width), lambda i, *_: (i, 0))
    extra = last and relative
    kept, sent = block_shapes(width * part // UNIT + (256 if extra else 0), width, relative)
    shape = jax.ShapeDtypeStruct
    specs = [rows, rows]
    specs += [pl.BlockSpec((tile, grad.shape[1]), lambda i, *_: (i, 0)) for grad in grads]
    specs += [full((SMALL, width))]
    outs, shapes = [], []
    if last:
        specs += [rows, rows, full(more[2].shape), full(more[3].shape)]
        outs = [rows, rows]
        shapes = [shape((length, width), f32), shape((length, width), bf16)]
    grid_spec = pltpu.PrefetchScalarGridSpec(
        num_scalar_prefetch=1,
        grid=(length // tile,),
        in_specs=specs,
        out_specs=outs + [full((SMALL, width)), full(kept), full(sent)],
        scratch_shapes=[pltpu.VMEM((width, part), f32)] * 3
        + ([pltpu.VMEM((256, width), f32)] if extra else []),
    )
    return pl.pallas_call(
        functools.partial(weights_kernel, start=start, count=count, relative=relative),
        grid_spec=grid_spec,
        out_shape=shapes
        + [shape((SMALL, width), f32), shape(kept, bf16), shape(sent, bf16)],
        compiler_params=params(),
        cost_estimate=cost(6 * length * width * part, 24 * length * width),
        name="weights",
    )(me, n, n_far, *grads, small, *more)


def tokens_kernel(x_ref, gain_ref, gm_ref, gq_ref, gf_ref, out_ref):
    norm, scale = normal_rows(x_ref[...].astype(f32))
    inner = (gq_ref[...] + gf_ref[...].astype(f32)) * gain_ref[...]
    out_ref[...] = gm_ref[...] + scale * (
        inner
        - jnp.mean(inner, -1, keepdims=True)
        - norm * jnp.mean(inner * norm, -1, keepdims=True)
    )


def tokens_call(x, gain, gm, gq, gf):
    length, width = x.shape
    rows = pl.BlockSpec((256, width), lambda i: (i, 0))
    return pl.pallas_call(
        tokens_kernel,
        grid=(length // 256,),
        in_specs=[rows, full((1, width)), rows, rows, rows],
        out_specs=rows,
        out_shape=jax.ShapeDtypeStruct((length, width), f32),
        compiler_params=params(),
        cost_estimate=cost(20 * length * width, 16 * length * width),
        name="tokens",
    )(x, gain, gm, gq, gf)


def swapped(value, axis, mask):
    pairs = [(source, source ^ mask) for source in range(lax.axis_size(axis))]
    return lax.ppermute(value, axis, pairs)


def added(a, b, dtype=bf16):
    return (a.astype(f32) + b.astype(f32)).astype(dtype)


def together(kernel, inputs, moves=(), later=(), due=()):
    count = len(moves)
    moves = list(moves) + list(later)
    inputs, values = lax.optimization_barrier((inputs, [value for value, _, _ in moves]))
    came = [swapped(value, *way[1:]) for value, way in zip(values, moves)]
    results = kernel(*inputs) if kernel else []
    results, now, due = lax.optimization_barrier((results, came[:count], list(due)))
    return results, now, came[count:], due


def total(*values):
    return functools.reduce(jnp.add, [value.astype(f32) for value in values])


def quads(*values):
    values = [value.reshape(4, -1, value.shape[-1]) for value in values]
    return jnp.concatenate(values, 1).reshape(-1, values[0].shape[-1])


def everywhere(value):
    mask = 1
    while mask < lax.axis_size("dp"):
        value = value + swapped(value, "dp", mask)
        mask *= 2
    return value


def pick_stream(pair, stream):
    return jnp.where(stream == 0, pair[0], pair[1])


def box_onehots(seg_boxes, buckets):
    half = buckets // 2
    levels = jnp.arange(buckets, dtype=jnp.int32)
    centre_x = (seg_boxes[..., 0] + seg_boxes[..., 2]) // 2
    centre_y = (seg_boxes[..., 1] + seg_boxes[..., 3]) // 2
    step_x = (
        jnp.clip((centre_x[:, None, :] - centre_x[:, :, None]) // box_step, -half, half - 1) + half
    )
    step_y = (
        jnp.clip((centre_y[:, None, :] - centre_y[:, :, None]) // box_step, -half, half - 1) + half
    )
    return (
        (step_x[..., None] == levels).astype(jnp.float32),
        (step_y[..., None] == levels).astype(jnp.float32),
    )


def body(
    tokens,
    first_gain,
    first_shift,
    query_weight,
    query_bias,
    key_weight,
    value_weight,
    value_bias,
    out_weight,
    out_bias,
    second_gain,
    second_shift,
    up_weight,
    up_bias,
    down_weight,
    down_bias,
    box_table,
    segments,
    validity,
    seg_boxes,
    cotangent,
):
    stream = lax.axis_index("stream")
    me = lax.axis_index("dp")
    shards = lax.axis_size("dp")
    width = tokens.shape[2]
    hidden = up_weight.shape[2]
    pages, page_len = segments.shape[1], segments.shape[2]
    length = pages * page_len
    relative = shards == 16
    me_ref = me.reshape(1).astype(jnp.int32)
    x = tokens[0]

    own_seg = pick_stream(segments, stream)
    far_seg = pick_stream(segments, 1 - stream)
    own_keep = pick_stream(validity, stream)
    far_keep = pick_stream(validity, 1 - stream)
    levels = jnp.arange(64, dtype=jnp.int32)
    hot_q = (own_seg[:, :, None] == levels).astype(bf16)
    hot_kt = (far_seg[:, None, :] == levels[None, :, None]).astype(bf16)
    wide_levels = jnp.arange(128, dtype=jnp.int32)
    hot_k = jnp.where(
        wide_levels == 64,
        jnp.where(far_keep[:, :, None] > 0, 0.0, mask_fill),
        (far_seg[:, :, None] == wide_levels).astype(f32),
    ).astype(bf16)
    hot_x, hot_y = box_onehots(seg_boxes, BUCKETS)
    tables = box_table[0].reshape(2, HEADS, BUCKETS)
    seg_bias = (
        jnp.einsum("pabn,hn->phab", hot_x, tables[0], precision=precise_variant)
        + jnp.einsum("pabn,hn->phab", hot_y, tables[1], precision=precise_variant)
    ).astype(bf16)
    ones = (jnp.arange(64) == 0).astype(bf16)
    seg_bias = jnp.concatenate([seg_bias, jnp.broadcast_to(ones, seg_bias.shape)], -1)

    keep_column = own_keep.reshape(length, 1).astype(f32)
    blocks, chunk = hidden // width, width // shards
    cot = cotangent[0]
    Y, CORE, X, Z1, Z2 = ("stream", 1), ("dp", 1), ("dp", 2), ("dp", 4), ("dp", 8)

    low = me & 3
    half = width // 2

    def quarter(weight):
        return lax.dynamic_slice_in_dim(weight[0], (low & 1) * half, half, 0)

    piece = jnp.where(low < 2, quarter(key_weight), quarter(value_weight))
    vectors = jnp.concatenate([first_gain, first_shift, value_bias], 0)
    (normed, query), (piece,), _, (far_rows,) = together(
        query_call,
        (x, first_gain, first_shift, query_weight[0], query_bias),
        [(piece, *Y)],
        [],
        [swapped(vectors, *Y)],
    )
    page_x = [x[page * page_len : (page + 1) * page_len] for page in range(pages)]
    (picks, hot_q, hot_k), (x_piece, core_piece, came_x), _, _ = together(
        lambda bias, hot_q, hot_k: (picks_call(hot_q, bias), hot_q, hot_k),
        (seg_bias, hot_q, hot_k),
        [(piece, *X), (piece, *CORE), (page_x[0], *Y)],
    )
    far_pages = [came_x]
    pieces = [piece, core_piece, x_piece, swapped(x_piece, *CORE)]
    far, mixing = (), ()
    for page in range(pages):

        def page_step(came, pieces, far, mixing, page=page):
            far = pair_call(page, length, me_ref, came, far_rows, pieces, far)
            return far, attend_call(page, query, far[1], far[2], picks, hot_k, mixing)

        moves = [(page_x[page + 1], *Y)] if page + 1 < pages else []
        (result, mixing), came, _, _ = together(
            page_step, (far_pages[page], pieces, tuple(far), tuple(mixing)), moves
        )
        far = result[:4]
        if page == 0:
            pieces = [result[4]]
        far_pages += came
    far_normed, keys, value_rows, far_x = far
    far_weights = pieces[0]
    mixed, log_total = mixing

    small = jnp.zeros((SMALL, width), f32)

    def feed_first(mixed, small):
        return feed_call(
            0, 2, me_ref,
            (x, mixed, keep_column, out_weight[0], out_bias, second_gain, second_shift),
            cot, up_weight[0], up_bias, down_weight[0], small, (), relative,
        )

    def feed_second(n2, small, *acts):
        return feed_call(
            1, 2, me_ref, (n2,), cot, up_weight[0], up_bias, down_weight[0], small, acts, relative
        )

    def finish(middle, small, *acts):
        return finish_call(
            me_ref, acts, up_weight[0], down_weight[0], middle, cot, keep_column, mixed,
            out_weight[0], second_gain, down_bias, small, relative,
        )

    def back_some(pair, pairs):
        def call(grad_mixed):
            return attend_back_call(
                pair, pairs, query, keys, value_rows, picks, hot_q, hot_k, hot_kt, log_total,
                mixed, grad_mixed,
            )

        return call

    def weights_some(start, more=()):
        def call(small, *grads):
            return weights_call(start, me_ref, normed, far_normed, grads, small, more, relative)

        return call

    back_through = (x, far_x, query_weight[0], far_weights)
    pairs = (4, width // 128 - 4)

    def table_row(grad_bias):
        return jnp.concatenate(
            [
                jnp.einsum("pabn,phba->hn", hot_x, grad_bias, precision=precise_variant),
                jnp.einsum("pabn,phba->hn", hot_y, grad_bias, precision=precise_variant),
            ],
            0,
        ).reshape(1, -1)

    if relative:
        z_low, z_high = (me >> 2) & 1, me >> 3

        def downs(pair):
            one, other = pair[:192], pair[192:]
            return jnp.where(z_low, other, one), jnp.where(z_low, one, other)

        (middle, normed_two, act, gh, small, ka, sa), _, _, _ = together(
            feed_first, (mixed, small)
        )
        (act, gh, small, kb, sb), (ca,), _, _ = together(
            feed_second, (normed_two, small, act, gh), [(sa, *CORE)]
        )
        up_go, down_go = added(ka[384:768], ca[384:768]), added(ka[1152:], ca[1152:])
        (output, grad_middle, grad_mixed, small, ko, so), (cb, x0, z0), _, _ = together(
            finish,
            (middle, small, act, gh),
            [(sb, *CORE), (down_go, *X), (up_go, *Z1)],
        )
        up_go = total(ka[192:384], ca[192:384], z0[192:]).astype(bf16)
        up_stay = total(ka[:192], ca[:192], z0[:192])
        go = added(kb[768:], cb[768:])
        (*grads, grad_bias), (co, z0), (x2,), _ = together(
            back_some(0, pairs[0]), (grad_mixed,), [(so, *CORE), (up_go, *Z2)], [(go, *X)]
        )
        one = total(ka[768:1152], ca[768:1152], x0).astype(bf16)
        one_keep, one_go = downs(one)
        up_low = total(up_stay, z0)
        go = jnp.concatenate([up_low[96:].astype(bf16), added(ko[192:], co[192:])], 0)
        (small, kq, sq), (z0,), (xo,), (x2,) = together(
            weights_some(0), (small, *grads), [(one_go, *Z1)], [(go, *X)], [x2]
        )
        down_one = added(one_keep, z0)
        two = total(kb[:768], cb[:768], x2).astype(bf16)
        two_keep, two_go = downs(two[384:])
        (*grads_two, grad_bias_two), (cq, z1), _, (xo,) = together(
            back_some(*pairs), (grad_mixed,), [(sq, *CORE), (two_go, *Z1)], [], [xo]
        )
        down_two = added(two_keep, z1)
        down_stay = jnp.where(z_high, down_two, down_one)
        down_go = jnp.where(z_high, down_one, down_two)
        go = added(kq[384:], cq[384:])
        rest = quads(two[:384], total(ko[:192], co[:192], xo[96:]).astype(bf16))
        (own_grad, far_grad, small, kr, sr), (xq, z1), (z3,), _ = together(
            weights_some(pairs[0] * 128, back_through),
            (small, *grads, *grads_two),
            [(go, *X), (rest[288:], *Z1)],
            [(down_go, *Z2)],
        )
        _, (cr,), (came_grad,), _ = together(None, (), [(sr, *CORE)], [(far_grad, *Y)])
        go, grad_bias, xq, z1 = lax.optimization_barrier(
            (added(kr[256:], cr[256:]), (grad_bias, grad_bias_two), xq, z1)
        )
        rest_go = added(rest[144:288], z1[144:])
        group_go = total(kq[192:384], cq[192:384], xq[192:]).astype(bf16)
        z4, z2 = swapped(group_go, *Z1), swapped(rest_go, *Z2)
        table = table_row(jnp.concatenate(grad_bias, 1))
        table = table + swapped(table, *CORE)
        _, (xr,), _, (z4, table) = together(None, (), [(go, *X)], [], [z4, table])
        r_go = total(kr[128:256], cr[128:256], xr[128:]).astype(bf16)
        group_go = total(kq[96:192], cq[96:192], xq[96:192], z4[96:]).astype(bf16)
        z5 = swapped(group_go, *Z2)
        _, (z1r, came), _, (z3,) = together(None, (), [(r_go, *Z1), (table, *X)], [], [z3])
        table = table + came
        r_go = total(kr[64:128], cr[64:128], xr[64:128], z1r[64:]).astype(bf16)
        _, (z2r, came), _, (z2, z5, came_grad) = together(
            None, (), [(r_go, *Z2), (table, *Z1)], [], [z2, z5, came_grad]
        )
        table = table + came
        up_low = total(up_low[:96], xo[:96])
        sum_down = total(down_stay, z3)
        rest = total(rest[:144], z1[:144], z2)
        first = total(kq[:96], cq[:96], xq[:96], z4[:96], z5)
        last = total(kr[:64], cr[:64], xr[:64], z1r[:64], z2r)
        sum_up = jnp.concatenate([up_low[:48], up_low[48:], rest[:48], rest[48:96]], 1)
        sum_out = rest[96:]

        def lanes_of(spread):
            pieces = [spread[:, 128 * i : 128 * i + chunk] for i in range(3)]
            pieces = jnp.concatenate(pieces, 0)
            return pieces[:SMALL] + pieces[SMALL:]

        def unit(values, place):
            block, lane = place // 3, place % 3
            return values[48 * block : 48 * block + 48, UNIT * lane : UNIT * (lane + 1)]

        def joined(first, last, i):
            return jnp.concatenate(
                [unit(first, 2 * i), unit(first, 2 * i + 1), unit(last, i)], 1
            )

        def ending(*given):
            lanes = lanes_of(last[48:])
            totals = lanes[20:24, 0]
            root_means = jnp.sqrt(totals[:3] / totals[3] + 1e-06).reshape(1, 3)
            up_part = lanes[16:20].reshape(1, hidden // shards)
            grad_tokens = tokens_call(*given)
            sum_query = joined(first, last, 0)
            return grad_tokens, lanes, root_means, up_part, sum_query, sum_up, sum_out, sum_down

        ended, (far_first, far_last, came), _, _ = together(
            ending,
            (x, first_gain, grad_middle, own_grad, came_grad),
            [(first.astype(bf16), *Y), (last, *Y), (table, *Z2)],
        )
        grad_tokens, lanes, root_means, up_part, sum_query, sum_up, sum_out, sum_down = ended
        table = table + came
        back = lanes_of(far_last[48:])[7:10]
        far_first = far_first.astype(f32)
        sum_keys, sum_values = joined(far_first, far_last, 1), joined(far_first, far_last, 2)
    else:
        middle, normed_two, act, gh, small, ka, _ = feed_first(mixed, small)
        act, gh, small, kb, _ = feed_second(normed_two, small, act, gh)
        output, grad_middle, grad_mixed, small, out_kept, _ = finish(middle, small, act, gh)
        *grads, grad_bias = back_some(0, pairs[0])(grad_mixed)
        small, kq, _ = weights_some(0)(small, *grads)
        *grads_two, grad_bias_two = back_some(*pairs)(grad_mixed)
        table = everywhere(table_row(jnp.concatenate([grad_bias, grad_bias_two], 1)))
        own_grad, far_grad, small, kr, _ = weights_some(pairs[0] * 128, back_through)(
            small, *grads, *grads_two
        )
        came_grad = swapped(far_grad, *Y)
        grad_tokens = tokens_call(x, first_gain, grad_middle, own_grad, came_grad)
        small = everywhere(small)

        def scattered(value):
            return lax.psum_scatter(value.astype(f32), "dp", scatter_dimension=0, tiled=True)

        def unit(values, place):
            block, lane = place // 3, place % 3
            return values[width * block : width * (block + 1), UNIT * lane : UNIT * (lane + 1)]

        ups = jnp.concatenate([ka, kb], 0).reshape(blocks, 2 * width, width)
        sum_up = scattered(jnp.concatenate([ups[j, :width] for j in range(blocks)], 1))
        sum_down = scattered(jnp.concatenate([ups[j, width:] for j in range(blocks)], 0))
        sum_out = scattered(out_kept)
        sum_query, sum_keys, sum_values = [
            scattered(
                jnp.concatenate([unit(kq, 2 * i), unit(kq, 2 * i + 1), unit(kr, i)], 1)
            )
            for i in range(3)
        ]
        sum_pair = jnp.concatenate([sum_keys, sum_values], 0).astype(bf16)
        lanes = lax.dynamic_slice_in_dim(small, me * chunk, chunk, 1)
        up_part = lax.dynamic_slice_in_dim(
            small[16 : 16 + blocks].reshape(1, hidden), me * (hidden // shards), hidden // shards, 1
        )
        totals = jnp.sum(small[20:24], 1)
        sum_pair, back = swapped((sum_pair, lanes[7:10]), *Y)
        root_means = jnp.sqrt(totals[:3] / totals[3] + 1e-06).reshape(1, 3)
        sum_keys, sum_values = sum_pair[:chunk].astype(f32), sum_pair[chunk:].astype(f32)

    return (
        output[None],
        grad_tokens[None],
        lanes[5:6] + back[1:2],
        lanes[6:7] + back[2:3],
        sum_query[None],
        lanes[4:5],
        sum_keys[None],
        sum_values[None],
        back[0:1],
        sum_out[None],
        lanes[0:1],
        lanes[1:2],
        lanes[2:3],
        sum_up[None],
        up_part,
        sum_down[None],
        lanes[3:4],
        lax.dynamic_slice_in_dim(table, me * chunk, chunk, 1),
        root_means,
    )


def solution(mesh):
    whole, split = P("stream", None), P("stream", "dp")
    cube, cut = P("stream", None, None), P("stream", "dp", None)
    pages = P(None, "dp", None)
    in_specs = (
        cut, whole, whole, cube, whole, cube, cube, whole, cube, whole, whole, whole,
        cube, whole, cube, whole, whole, pages, pages, P("dp", None, None), cut,
    )
    out_specs = (
        cut, cut, split, split, cut, split, cut, cut, split, cut, split, split, split,
        cut, split, cut, split, split, whole,
    )
    return jax.shard_map(body, mesh=mesh, in_specs=in_specs, out_specs=out_specs, check_vma=False)
```
